32 devices in a mesh: pipe: 4 (over y, x), ctx: 8 (over z, core).
Axes of the slice: x: 2, y: 2, z: 4, core: 2. Of those that a mesh axis runs over, the one named last changes fastest.
Arguments:
- inner_x: bfloat16 [4, 1024, 8192], P('pipe', 'ctx'), may hold values from -6 to 6
- dt_raw: bfloat16 [4, 1024, 8192], P('pipe', 'ctx'), may hold values from -8 to -0.4
- grad_out: bfloat16 [4, 1024, 8192], P('pipe', 'ctx'), may hold values from -6 to 6
- state_maps: float32 [4, 2, 16, 1024], P('pipe', None, None, 'ctx'), may hold values from -6 to 6
- saved_states: float32 [4, 8, 16, 8192], P('pipe', 'ctx'), may hold values from -0.3 to 0.3
- a_log: float32 [4, 16, 8192], P('pipe'), may hold values from -0.5 to 0.5
- conv_weight: float32 [4, 4, 8192], P('pipe'), may hold values from -3 to 3
- conv_bias: float32 [4, 8192], P('pipe'), may hold values from -3 to 3
- skip_gain: float32 [4, 8192], P('pipe'), may hold values from 0.5 to 1.5
- doc_lengths: int32 [4, 8], P('pipe'), may hold values from 1 to 385, 1024 in all within a row
Outputs:
- upstream: bfloat16 [4, 1024, 8192], P('pipe', 'ctx')
- grad_dt: bfloat16 [4, 1024, 8192], P('pipe', 'ctx')
- grad_maps: float32 [4, 2, 16, 1024], P('pipe', None, None, 'ctx')
- grad_params: float32 [4, 22, 8192], P('pipe', None, 'ctx')
The draws below stay inside these ranges and needn't reach their ends.
Inputs may be any that keep to these rules, and one draw needn't show every extreme that they name: `doc_lengths`: each section's lengths sum to 1024; the longest is exactly 385, so that no document touches more than 4 context shards and some document touches exactly 4.
All inputs are finite; a program needn't handle non-finite values.
Results may differ from the reference program's by a relative error of at most 0.001.
Values may be sent and summed in bfloat16 or wider, within the bound.
No kernel may reach another device: no remote copies, remote signals or barrier semaphores. Data moves between devices by JAX's collectives and lax.ppermute only.
A program may use at most 256 MiB of HBM per device.

```python
import math
import jax
import jax.numpy as jnp
import numpy as np
from jax import lax

CHANNELS = 8192
STATE = 16
CONV = 4
TOK_DEV = 128
SECTIONS = 4
SHARDS = 8
JOINED_ITEMS = 1024
DOCS = 8
MOSTLEN = 385


def draw_dt_raw(key, part):
    keys = jax.random.split(key, 4)
    share = 0.5
    pick = jax.random.uniform(keys[0], (SECTIONS, 1, CHANNELS), jnp.float32)
    starting_shift = jnp.where(pick < share, math.log(0.03), math.log(0.001))
    interval_extent = jax.random.uniform(keys[1], (SECTIONS, SHARDS, 1, CHANNELS), jnp.float32, -0.35, 0.35)
    interval_extent = jnp.broadcast_to(interval_extent, (SECTIONS, SHARDS, TOK_DEV, CHANNELS)).reshape(SECTIONS, JOINED_ITEMS, CHANNELS)
    approximate_guess = jax.random.uniform(keys[2], (SECTIONS, JOINED_ITEMS, CHANNELS), jnp.float32, -0.35, 0.35)
    marked_locations = jax.random.randint(keys[3], (SECTIONS, 1, 6), 0, JOINED_ITEMS)
    contiguous_count = jnp.any(jnp.arange(JOINED_ITEMS)[None, :, None] == marked_locations, axis=2)[:, :, None]
    scalar_element = jnp.where(contiguous_count, -0.5, starting_shift + interval_extent + approximate_guess)
    return scalar_element.astype(jnp.bfloat16)


def strengthened(entries, stream_key, source, target, shards_of, factor):
    owner, partner = [(jnp.arange(entries.shape[dim]) // (entries.shape[dim] // shards_of)).reshape([-1 if axis == dim else 1 for axis in range(entries.ndim)]) for dim in (source, target)]
    chosen = jax.random.permutation(stream_key, shards_of)[partner]
    strong = (owner == chosen) | (owner == (partner + shards_of // 2) % shards_of)
    return jnp.where(strong, factor * entries, entries)


def shard_levels(stream_key, extent, cuts, smallest, largest):
    level = 1.0
    for dim, parts in cuts:
        steps = jax.random.uniform(jax.random.fold_in(jax.random.fold_in(stream_key, 6), dim), (parts,), jnp.float32, smallest / len(cuts), largest / len(cuts))
        level = level * jnp.repeat(jnp.exp(steps), extent[dim] // parts).reshape((-1,) + (1,) * (len(extent) - 1 - dim))
    return level


def profile(count, total, bound, skew):
    weights = [(1 << 20) // math.isqrt(standing ** skew) + 1 for standing in range(2, count + 1)]
    surplus, given = total - bound - (count - 1), [1] * (count - 1)
    while surplus > 0:
        free = [i for i in range(count - 1) if given[i] < bound]
        mass, left = sum([weights[i] for i in free]), surplus
        for i in free:
            addition = min(bound - given[i], max(1, left * weights[i] // mass), surplus)
            given[i] = given[i] + addition
            surplus = surplus - addition
    return np.array([bound] + given)


def uneven_parts(key, number_of, total, most, slope):
    if number_of == 2:
        one = jax.random.randint(key, (), max(1, total - most), min(most, total - 1) + 1)
        return jnp.stack([one, total - one])
    tallies = jnp.asarray(profile(number_of, total, most, slope), jnp.int32)
    twos = (number_of - 1) // 2
    giver, sink = tallies[1:1 + 2 * twos:2], tallies[2:2 + 2 * twos:2]
    margin = jnp.minimum(giver - 1, most - sink)
    moved = jax.random.randint(jax.random.fold_in(key, 1), (twos,), 0, 1 << 20) % (margin + 1)
    tallies = tallies.at[1:1 + 2 * twos:2].set(giver - moved).at[2:2 + 2 * twos:2].set(sink + moved)
    return tallies[jax.random.permutation(jax.random.fold_in(key, 2), number_of)]


def normal_values(own_key, extent, width, bound, cuts=(), kind=jnp.bfloat16):
    loudness = shard_levels(own_key, extent, cuts, -0.22, 0.18) if cuts else 1.0
    entries = jax.random.normal(own_key, extent, jnp.float32) * width * loudness
    return jnp.minimum(jnp.maximum(entries, -bound), bound).astype(kind)


def noise_with(key, extent, width, most, shards, heavy, kind=jnp.bfloat16):
    values = width * jax.random.normal(key, extent, jnp.float32)
    if shards:
        values = values * shard_levels(key, extent, shards, -0.22, 0.18)
    return jnp.clip(strengthened(values, jax.random.fold_in(key, 3), *heavy), -most, most).astype(kind)


def setup_inputs(seed: int = 0) -> dict:
    key_of = jax.random.split(jax.random.key(seed), 11)
    return {
        "inner_x": normal_values(key_of[0], (SECTIONS, JOINED_ITEMS, CHANNELS), 1.0, 6.0, ((0, 4), (1, 8))),
        "dt_raw": draw_dt_raw(jax.random.fold_in(key_of[10], 71), 0),
        "grad_out": noise_with(key_of[2], (SECTIONS, JOINED_ITEMS, CHANNELS), 1.0, 6.0, ((0, 4), (1, 8)), (1, 2, 8, 2.0)),
        "state_maps": normal_values(key_of[3], (SECTIONS, 2, STATE, JOINED_ITEMS), 1.0, 6.0, ((0, 4), (3, 8)), jnp.float32),
        "saved_states": normal_values(key_of[4], (SECTIONS, SHARDS, STATE, CHANNELS), 0.05, 0.3, ((0, 4), (1, 8)), jnp.float32),
        "a_log": jnp.clip(jax.random.uniform(key_of[5], (SECTIONS, STATE, CHANNELS), jnp.float32, -0.5, 0.5) * shard_levels(key_of[5], (SECTIONS, STATE, CHANNELS), ((0, 4),), -0.4, 0.0), -0.5, 0.5),
        "conv_weight": normal_values(key_of[6], (SECTIONS, CONV, CHANNELS), CONV ** -0.5, 3.0, ((0, 4),), jnp.float32),
        "conv_bias": normal_values(key_of[7], (SECTIONS, CHANNELS), 0.5, 3.0, ((0, 4),), jnp.float32),
        "skip_gain": jnp.clip(0.5 + 1.0 * jax.random.uniform(key_of[8], (SECTIONS, CHANNELS), jnp.float32) ** shard_levels(key_of[8], (SECTIONS, CHANNELS), ((0, 4),), -0.2, 0.2), 0.5, 1.5),
        "doc_lengths": jax.vmap(lambda own: uneven_parts(own, DOCS, JOINED_ITEMS, MOSTLEN, 2))(jax.random.split(key_of[9], SECTIONS)).reshape((SECTIONS, DOCS)).astype(jnp.int32),
    }


def silu_slope(scalar_element):
    sigm = jax.nn.sigmoid(scalar_element)
    return sigm * (1.0 + scalar_element * (1.0 - sigm))


def section(inner_x, dt_raw, grad_out, state_maps, saved_states, a_log, conv_weight, conv_bias, skip_gain, doc_lengths):
    starts = jnp.cumsum(doc_lengths) - doc_lengths
    position = jnp.arange(JOINED_ITEMS, dtype=jnp.int32)
    doc_start = jnp.max(jnp.where(position[:, None] >= starts[None, :], starts[None, :], 0), axis=1)
    resets = jnp.any(position[:, None] == starts[None, :], axis=1)
    keeping = 1.0 - resets.astype(jnp.float32)
    padded = jnp.concatenate([jnp.zeros((CONV - 1, CHANNELS), jnp.float32), inner_x.astype(jnp.float32)], 0)
    valid_masks = [(position - (CONV - 1 - j) >= doc_start).astype(jnp.float32)[:, None] for j in range(CONV)]
    conv_out = jnp.broadcast_to(conv_bias[None, :], (JOINED_ITEMS, CHANNELS))
    for j in range(CONV):
        conv_out = conv_out + conv_weight[j][None, :] * padded[j:j + JOINED_ITEMS] * valid_masks[j]
    activated = jax.nn.silu(conv_out)
    step_size = jax.nn.softplus(dt_raw.astype(jnp.float32))
    decay_rate = -jnp.exp(a_log)
    grad_y = grad_out.astype(jnp.float32)
    b_rows = state_maps[0].T
    c_rows = state_maps[1].T

    def by_shard(array):
        return array.reshape((SHARDS, TOK_DEV) + array.shape[1:])

    def shard_step(carried, inputs):
        incoming, rate_grad = carried
        act_s, step_s, keep_s, b_s, c_s, y_s, start_state = inputs

        def forward(state, token):
            act_t, step_t, keep_t, b_t = token
            decay = keep_t * jnp.exp(step_t[None, :] * decay_rate)
            new_state = decay * state + (step_t * act_t)[None, :] * b_t[:, None]
            return new_state, (state, decay, new_state)

        _, (befores, decays, afters) = lax.scan(forward, start_state, (act_s, step_s, keep_s, b_s))

        def backward(carry_pair, token):
            adjoint, grad_acc = carry_pair
            act_t, step_t, b_t, c_t, y_t, before, decay, after = token
            adjoint_now = c_t[:, None] * y_t[None, :] + adjoint
            scaled = adjoint_now * step_t[None, :]
            prior = decay * before
            grad_u = skip_gain * y_t + jnp.sum(scaled * b_t[:, None], axis=0)
            grad_step = jnp.sum(adjoint_now * (b_t[:, None] * act_t[None, :] + decay_rate * prior), axis=0)
            grad_acc = grad_acc + scaled * prior
            grad_b = jnp.sum(scaled * act_t[None, :], axis=1)
            grad_c = jnp.sum(after * y_t[None, :], axis=1)
            return (decay * adjoint_now, grad_acc), (grad_u, grad_step, grad_b, grad_c)

        (outgoing, rate_grad), results = lax.scan(backward, (incoming, rate_grad), (act_s, step_s, b_s, c_s, y_s, befores, decays, afters), reverse=True)
        return (outgoing, rate_grad), results

    zeros_state = jnp.zeros((STATE, CHANNELS), jnp.float32)
    (_, rate_grad), (grad_u, grad_step, grad_b, grad_c) = lax.scan(shard_step, (zeros_state, zeros_state), (by_shard(activated), by_shard(step_size), by_shard(keeping), by_shard(b_rows), by_shard(c_rows), by_shard(grad_y), saved_states), reverse=True)
    grad_u = grad_u.reshape(JOINED_ITEMS, CHANNELS)
    grad_step = grad_step.reshape(JOINED_ITEMS, CHANNELS)
    grad_b = grad_b.reshape(JOINED_ITEMS, STATE)
    grad_c = grad_c.reshape(JOINED_ITEMS, STATE)
    grad_dt = (grad_step * jax.nn.sigmoid(dt_raw.astype(jnp.float32))).astype(jnp.bfloat16)
    grad_conv = grad_u * silu_slope(conv_out)
    grad_padded = jnp.zeros((JOINED_ITEMS + CONV - 1, CHANNELS), jnp.float32)
    tap_grads = []
    for j in range(CONV):
        masked = grad_conv * valid_masks[j]
        grad_padded = grad_padded + jnp.pad(masked * conv_weight[j][None, :], ((j, CONV - 1 - j), (0, 0)))
        tap_grads.append(jnp.sum(masked * padded[j:j + JOINED_ITEMS], axis=0))
    grad_x = grad_padded[CONV - 1:].astype(jnp.bfloat16)
    grad_maps = jnp.stack([grad_b.T, grad_c.T], 0)
    grad_params = jnp.concatenate([rate_grad * decay_rate, jnp.stack(tap_grads, 0), jnp.sum(grad_y * activated, axis=0)[None, :], jnp.sum(grad_conv, axis=0)[None, :]], 0)
    return grad_x, grad_dt, grad_maps, grad_params


def reference(inner_x, dt_raw, grad_out, state_maps, saved_states, a_log, conv_weight, conv_bias, skip_gain, doc_lengths):
    results = lax.map(lambda inputs: section(*inputs), (inner_x, dt_raw, grad_out, state_maps, saved_states, a_log, conv_weight, conv_bias, skip_gain, doc_lengths))
    grad_x, grad_dt, grad_maps, grad_params = results
    upstream = jnp.concatenate([grad_x[1:], jnp.zeros_like(grad_x[:1])], 0)
    return upstream, grad_dt, grad_maps, grad_params
```

```python
import functools

import jax
import jax.numpy as jnp
from jax import lax
from jax.experimental import pallas as pl
from jax.experimental.pallas import tpu as pltpu
from jax.sharding import PartitionSpec as P

LANES = 128
LOG2E = 1.4426950408889634
LN2 = 0.6931471805599453
RESET_STEP = 1e4
PAST = 8


def shift_to(x, axis, by):
    length = lax.axis_size(axis)
    pairs = [(i, i + by) for i in range(length) if 0 <= i + by < length]
    return lax.ppermute(x, axis, pairs)


def fill_keep(off_ref, len_ref, keep_ref, rows):
    def clear(i, _):
        keep_ref[i] = jnp.float32(1.0)
        return 0

    lax.fori_loop(0, rows + PAST, clear, 0)

    def mark(d, start):
        at = start - off_ref[0] + PAST

        @pl.when(jnp.logical_and(at >= 0, at < rows + PAST))
        def _():
            keep_ref[at] = jnp.float32(0.0)

        return start + len_ref[0, d]

    lax.fori_loop(0, len_ref.shape[1], mark, jnp.int32(0))


def softplus_of(dt):
    return jnp.log1p(jnp.exp(dt))


def head_kernel(group, unroll, off_ref, len_ref, maps_ref, dt_ref, gy_ref, alog_ref, head_ref,
                thr_ref, keep_ref, dt_s, gy_s, al_s, a2_s, tot_s):
    rows = dt_ref.shape[0]
    states = alog_ref.shape[0]

    @pl.when(pl.program_id(0) == 0)
    def _():
        fill_keep(off_ref, len_ref, keep_ref, rows)

    for j in range(group):
        cols = slice(j * LANES, (j + 1) * LANES)
        dt_s[j * rows:(j + 1) * rows, :] = dt_ref[:, cols].astype(jnp.float32)
        gy_s[j * rows:(j + 1) * rows, :] = gy_ref[:, cols].astype(jnp.float32)
        al_s[j * states:(j + 1) * states, :] = -LOG2E * jnp.exp(alog_ref[:, cols])
    for n in range(states):
        a2_s[n] = al_s[pl.ds(n, group, stride=states), :]

    def token(i, carry):
        cars, total = carry
        t = rows - 1 - i
        gy = gy_s[pl.ds(t, group, stride=rows), :]
        step = softplus_of(dt_s[pl.ds(t, group, stride=rows), :])
        step = step + (1.0 - keep_ref[PAST + t]) * RESET_STEP
        out = []
        for n in range(states):
            decay = jnp.exp2(step * a2_s[n])
            out.append(decay * (maps_ref[states + n, t] * gy + cars[n]))
        return tuple(out), total + step

    zero = jnp.zeros((group, LANES), jnp.float32)
    cars, total = lax.fori_loop(0, rows, token, ((zero,) * states, zero), unroll=unroll)
    for n in range(states):
        head_ref[0, n] = cars[n]
        thr_ref[0, n] = jnp.exp2(total * a2_s[n])


def head_call(group, off, lengths, maps, dt, gy, alog, base, blocks):
    rows = dt.shape[0]
    states = alog.shape[0]
    width = group * LANES
    smem = pl.BlockSpec(memory_space=pltpu.SMEM)
    col = lambda i: (0, base + i)
    carry = jax.ShapeDtypeStruct((blocks, states, group, LANES), jnp.float32)
    return pl.pallas_call(
        functools.partial(head_kernel, group, 4),
        grid=(blocks,),
        out_shape=(carry, carry),
        in_specs=[smem, smem, smem, pl.BlockSpec((rows, width), col),
                  pl.BlockSpec((rows, width), col), pl.BlockSpec((states, width), col)],
        out_specs=(pl.BlockSpec((1, states, group, LANES), lambda i: (i, 0, 0, 0)),) * 2,
        scratch_shapes=[
            pltpu.SMEM((rows + PAST,), jnp.float32),
            pltpu.VMEM((group * rows, LANES), jnp.float32),
            pltpu.VMEM((group * rows, LANES), jnp.float32),
            pltpu.VMEM((group * states, LANES), jnp.float32),
            pltpu.VMEM((states, group, LANES), jnp.float32),
            pltpu.VMEM((group, LANES), jnp.float32),
        ],
        compiler_params=pltpu.CompilerParams(
            dimension_semantics=("arbitrary",), vmem_limit_bytes=16 << 20),
        cost_estimate=pl.CostEstimate(
            flops=blocks * rows * states * width * 6, transcendentals=0,
            bytes_accessed=blocks * width * (rows * 4 + states * 12)),
        name="head",
    )(off, lengths, maps, dt, gy, alog)


def main_kernel(group, part, off_ref, len_ref, maps_ref, x_ref, hist_ref, dt_ref, gy_ref,
                start_ref, alog_ref, cw_ref, cb_ref, sk_ref, gin_ref,
                gx_ref, gdt_ref, edge_ref, gp_ref, gm_ref,
                keep_ref, x_s, dt_s, gy_s, al_s, st_s, row_s, a2_s, hist_s, wt_s,
                step_t, du_t, gy_t, u_t, sig_t, slope_t, w_t, v_t, dec_s, h_s, acc_s, out_s, gp_s):
    rows = x_ref.shape[0]
    states = alog_ref.shape[0]
    first = pl.program_id(0) == 0
    f32 = jnp.float32

    @pl.when(first)
    def _():
        fill_keep(off_ref, len_ref, keep_ref, rows)

    for j in range(group):
        cols = slice(j * LANES, (j + 1) * LANES)
        tall = slice(j * rows, (j + 1) * rows)
        x_s[tall, :] = x_ref[:, cols].astype(f32)
        dt_s[tall, :] = dt_ref[:, cols].astype(f32)
        gy_s[tall, :] = gy_ref[:, cols].astype(f32)
        al_s[j * states:(j + 1) * states, :] = -LOG2E * jnp.exp(alog_ref[:, cols])
        st_s[j * states:(j + 1) * states, :] = start_ref[:, cols]
        hist_s[j:j + 1, :] = hist_ref[0:1, cols].astype(f32)
        hist_s[group + j:group + j + 1, :] = hist_ref[1:2, cols].astype(f32)
        hist_s[2 * group + j:2 * group + j + 1, :] = hist_ref[2:3, cols].astype(f32)
        for k in range(4):
            wt_s[k * group + j:k * group + j + 1, :] = cw_ref[k:k + 1, cols]
        wt_s[4 * group + j:4 * group + j + 1, :] = cb_ref[:, cols]
        wt_s[5 * group + j:5 * group + j + 1, :] = sk_ref[:, cols]
    for n in range(states):
        a2_s[n] = al_s[pl.ds(n, group, stride=states), :]
        h_s[0, n] = st_s[pl.ds(n, group, stride=states), :]

    def weight(k):
        return wt_s[k * group:(k + 1) * group, :]

    def past(k):
        return hist_s[k * group:(k + 1) * group, :]

    def rows_of(t, carry):
        before, x1, x2 = carry
        keep = keep_ref[PAST + t]
        own = pl.ds(t, group, stride=rows)
        x = x_s[own, :]
        y = gy_s[own, :]
        dt = dt_s[own, :]
        k1 = keep * before
        k2 = keep * x1
        k3 = keep * x2
        conv = weight(4) + weight(0) * k3 + weight(1) * k2 + weight(2) * k1 + weight(3) * x
        sig = 1.0 / (1.0 + jnp.exp(-conv))
        u = conv * sig
        e = jnp.exp(dt)
        step = jnp.log1p(e)
        step_t[t] = step + (1.0 - keep) * RESET_STEP
        du_t[t] = step * u
        gy_t[t] = y
        u_t[t] = u
        sig_t[t] = e / (1.0 + e)
        slope_t[t] = sig * (1.0 + conv * (1.0 - sig))
        return x, k1, k2

    k_1 = keep_ref[PAST - 1]
    k_2 = keep_ref[PAST - 2]
    lax.fori_loop(0, rows, rows_of, (past(2), k_1 * past(1), k_1 * k_2 * past(0)), unroll=2)

    @pl.when(first)
    def _():
        def wipe(t, _):
            for n in range(2 * states):
                acc_s[n, t] = jnp.zeros((8, LANES), f32)
            return 0
        lax.fori_loop(0, rows, wipe, 0)

    def fold(p):
        out = p[0:8]
        for k in range(1, group // 8):
            out = out + p[k * 8:(k + 1) * 8]
        return out

    for lo in range(0, states, part):
        hi = lo + part

        def forward(t, hs):
            step = step_t[t]
            du = du_t[t]
            out = []
            for n in range(lo, hi):
                decay = jnp.exp2(step * a2_s[n])
                h = decay * hs[n - lo] + maps_ref[n, t] * du
                dec_s[t, n - lo] = decay
                h_s[t + 1, n] = h
                out.append(h)
            return tuple(out)

        lax.fori_loop(0, rows, forward, tuple(h_s[0, n] for n in range(lo, hi)), unroll=2)

        def backward(i, carry):
            cars, rates = carry
            t = rows - 1 - i
            step = step_t[t]
            du = du_t[t]
            y = gy_t[t]
            new_cars, new_rates = [], []
            w = jnp.zeros_like(y) if lo == 0 else w_t[t]
            v = jnp.zeros_like(y) if lo == 0 else v_t[t]
            for n in range(lo, hi):
                m = n - lo
                g = maps_ref[states + n, t] * y + cars[m]
                acc_s[n, t] += fold(g * du)
                acc_s[states + n, t] += fold(h_s[t + 1, n] * y)
                w = w + maps_ref[n, t] * g
                car = dec_s[t, m] * g
                aq = a2_s[n] * (car * h_s[t, n])
                v = v + aq
                new_cars.append(car)
                new_rates.append(rates[m] + step * aq)
            w_t[t] = w
            v_t[t] = v
            return tuple(new_cars), tuple(new_rates)

        zero = jnp.zeros((group, LANES), f32)
        _, rates = lax.fori_loop(
            0, rows, backward,
            (tuple(gin_ref[0, n] for n in range(lo, hi)), (zero,) * part), unroll=2)
        for n in range(lo, hi):
            gp_s[pl.ds(n, group, stride=24), :] = rates[n - lo] * LN2

    def finish(i, carry):
        d1, d2, d3, taps, bias, skip = carry
        t = rows - 1 - i
        own = pl.ds(t, group, stride=rows)
        x = x_s[own, :]
        y = gy_t[t]
        u = u_t[t]
        w = w_t[t]
        du = du_t[t]
        sig = sig_t[t]
        step = step_t[t] - (1.0 - keep_ref[PAST + t]) * RESET_STEP
        step = jnp.where(step_t[t] > 0.5 * RESET_STEP, softplus_of(dt_s[own, :]), step)
        grad_u = weight(5) * y + step * w
        grad_step = u * w + LN2 * v_t[t]
        dt_s[own, :] = grad_step * sig
        gc = grad_u * slope_t[t]
        x_s[own, :] = weight(3) * gc + weight(2) * d1 + weight(1) * d2 + weight(0) * d3
        taps = (taps[0] + x * d3, taps[1] + x * d2, taps[2] + x * d1, taps[3] + x * gc)
        keep = keep_ref[PAST + t]
        return keep * gc, keep * d1, keep * d2, taps, bias + gc, skip + y * u

    zero = past(0) * 0.0
    d1, d2, d3, taps, bias, skip = lax.fori_loop(
        0, rows, finish, (zero, zero, zero, (zero,) * 4, zero, zero), unroll=2)
    taps = list(taps)
    for k in range(3):
        out = weight(0) * d3
        taps[0] = taps[0] + past(2 - k) * d3
        if k < 2:
            out = out + weight(1) * d2
            taps[1] = taps[1] + past(2 - k) * d2
        if k < 1:
            out = out + weight(2) * d1
            taps[2] = taps[2] + past(2 - k) * d1
        row_s[pl.ds(2 - k, group, stride=8), :] = out
        keep = keep_ref[PAST - 1 - k]
        d1, d2, d3 = d1, keep * d1, keep * d2
    for k in range(4):
        gp_s[pl.ds(states + k, group, stride=24), :] = taps[k]
    gp_s[pl.ds(states + 4, group, stride=24), :] = skip
    gp_s[pl.ds(states + 5, group, stride=24), :] = bias
    for k in range(3):
        row_s[pl.ds(3 + k, group, stride=8), :] = x_s[pl.ds(rows - 3 + k, group, stride=rows), :]

    for j in range(group):
        cols = slice(j * LANES, (j + 1) * LANES)
        tall = slice(j * rows, (j + 1) * rows)
        gx_ref[:, cols] = x_s[tall, :].astype(jnp.bfloat16)
        gdt_ref[:, cols] = dt_s[tall, :].astype(jnp.bfloat16)
        edge_ref[:, cols] = row_s[j * 8:j * 8 + 6, :]
        gp_ref[:, cols] = gp_s[j * 24:j * 24 + states + 6, :]

    @pl.when(pl.program_id(0) == pl.num_programs(0) - 1)
    def _():
        def reduce_state(n, _):
            for tb in range(rows // 8):
                total = acc_s[n, tb * 8:tb * 8 + 8]
                out_s[tb * 8:tb * 8 + 8, :] = jnp.sum(total, axis=1)
            flat = out_s[...].T
            gm_ref[pl.ds(n, 1), :] = jnp.sum(flat, axis=0, keepdims=True)
            return 0
        lax.fori_loop(0, 2 * states, reduce_state, 0)


def main_call(group, part, off, lengths, maps, x, hist, dt, gy, start, alog, cw, cb, sk, gin,
              base, blocks):
    rows = x.shape[0]
    states = alog.shape[0]
    width = group * LANES
    smem = pl.BlockSpec(memory_space=pltpu.SMEM)
    col = lambda i: (0, base + i)
    out_col = lambda i: (0, i)
    f32 = jnp.float32
    table = pltpu.VMEM((rows, group, LANES), f32)
    return pl.pallas_call(
        functools.partial(main_kernel, group, part),
        grid=(blocks,),
        out_shape=(
            jax.ShapeDtypeStruct((rows, blocks * width), jnp.bfloat16),
            jax.ShapeDtypeStruct((rows, blocks * width), jnp.bfloat16),
            jax.ShapeDtypeStruct((6, blocks * width), f32),
            jax.ShapeDtypeStruct((states + 6, blocks * width), f32),
            jax.ShapeDtypeStruct((2 * states, rows), f32),
        ),
        in_specs=[smem, smem, smem,
                  pl.BlockSpec((rows, width), col),
                  pl.BlockSpec((3, width), col),
                  pl.BlockSpec((rows, width), col),
                  pl.BlockSpec((rows, width), col),
                  pl.BlockSpec((states, width), col),
                  pl.BlockSpec((states, width), col),
                  pl.BlockSpec((4, width), col),
                  pl.BlockSpec((1, width), col),
                  pl.BlockSpec((1, width), col),
                  pl.BlockSpec((1, states, group, LANES), lambda i: (i, 0, 0, 0))],
        out_specs=(pl.BlockSpec((rows, width), out_col),
                   pl.BlockSpec((rows, width), out_col),
                   pl.BlockSpec((6, width), out_col),
                   pl.BlockSpec((states + 6, width), out_col),
                   pl.BlockSpec((2 * states, rows), lambda i: (0, 0))),
        scratch_shapes=[
            pltpu.SMEM((rows + PAST,), f32),
            pltpu.VMEM((group * rows, LANES), f32),
            pltpu.VMEM((group * rows, LANES), f32),
            pltpu.VMEM((group * rows, LANES), f32),
            pltpu.VMEM((group * states, LANES), f32),
            pltpu.VMEM((group * states, LANES), f32),
            pltpu.VMEM((group * 8, LANES), f32),
            pltpu.VMEM((states, group, LANES), f32),
            pltpu.VMEM((3 * group, LANES), f32),
            pltpu.VMEM((6 * group, LANES), f32),
            table, table, table, table, table, table, table, table,
            pltpu.VMEM((rows, part, group, LANES), f32),
            pltpu.VMEM((rows + 1, states, group, LANES), f32),
            pltpu.VMEM((2 * states, rows, 8, LANES), f32),
            pltpu.VMEM((rows, LANES), f32),
            pltpu.VMEM((group * 24, LANES), f32),
        ],
        compiler_params=pltpu.CompilerParams(
            dimension_semantics=("arbitrary",), vmem_limit_bytes=60 << 20),
        cost_estimate=pl.CostEstimate(
            flops=blocks * rows * states * width * 24, transcendentals=0,
            bytes_accessed=blocks * width * (rows * 10 + states * 16)),
        name="main",
    )(off, lengths, maps, x, hist, dt, gy, start, alog, cw, cb, sk, gin)


def on_device(inner_x, dt_raw, grad_out, state_maps, saved_states, a_log, conv_weight, conv_bias,
              skip_gain, doc_lengths):
    rows = inner_x.shape[1]
    channels = inner_x.shape[2]
    states = a_log.shape[1]
    group = 8
    blocks = channels // (group * LANES)
    off = (lax.axis_index("ctx") * rows).astype(jnp.int32).reshape(1)
    maps = state_maps[0].reshape(2 * states, rows)
    x, dt, gy = inner_x[0], dt_raw[0], grad_out[0]
    hist = shift_to(x[rows - 3:], "ctx", 1)

    head, through = head_call(group, off, doc_lengths, maps, dt, gy, a_log[0], 0, blocks)
    arrived = shift_to(head, "ctx", -1)
    for _ in range(2):
        arrived = shift_to(head + through * arrived, "ctx", -1)

    gx, gdt, edge, gp, gm = main_call(
        group, states, off, doc_lengths, maps, x, hist, dt, gy, saved_states[0, 0], a_log[0],
        conv_weight[0], conv_bias, skip_gain, arrived, 0, blocks)

    spilled = shift_to(edge[:3], "ctx", -1)
    tail = (edge[3:] + spilled).astype(jnp.bfloat16)
    upstream = shift_to(gx, "pipe", -1)
    tail = shift_to(tail, "pipe", -1)
    upstream = lax.dynamic_update_slice(upstream, tail, (rows - 3, 0))
    shares = lax.psum_scatter(gp, "ctx", scatter_dimension=1, tiled=True)
    return upstream[None], gdt[None], gm.reshape(1, 2, states, rows), shares[None]


def solution(mesh):
    in_specs = (
        P("pipe", "ctx", None),
        P("pipe", "ctx", None),
        P("pipe", "ctx", None),
        P("pipe", None, None, "ctx"),
        P("pipe", "ctx", None, None),
        P("pipe", None, None),
        P("pipe", None, None),
        P("pipe", None),
        P("pipe", None),
        P("pipe", None),
    )
    out_specs = (
        P("pipe", "ctx", None),
        P("pipe", "ctx", None),
        P("pipe", None, None, "ctx"),
        P("pipe", None, "ctx"),
    )
    return jax.shard_map(
        on_device, mesh=mesh, in_specs=in_specs, out_specs=out_specs, check_vma=False
    )
```

```python
import functools

import jax
import jax.numpy as jnp
from jax import lax
from jax.experimental import pallas as pl
from jax.experimental.pallas import tpu as pltpu
from jax.sharding import PartitionSpec as P

LANES = 128
LOG2E = 1.4426950408889634
LN2 = 0.6931471805599453
RESET_STEP = 1e4
PAST = 8
CHUNK = 8
WIDE = 16
MIB = 1 << 20
HEAD_VMEM = 60 * MIB
MAIN_VMEM = 60 * MIB
REACH = 3


def shift_to(x, axis, by):
    length = lax.axis_size(axis)
    pairs = [(i, i + by) for i in range(length) if 0 <= i + by < length]
    return lax.ppermute(x, axis, pairs)


def at_chunk(i, size):
    return pl.multiple_of(i * size, size)


def fill_keep(offset, len_ref, keep_t):
    rows, lanes = keep_t.shape
    place = lax.broadcasted_iota(jnp.int32, (rows, lanes), 0) + (offset - PAST)

    def mark(d, carry):
        start, keep = carry
        return start + len_ref[0, d], jnp.where(place == start, 0.0, keep)

    _, keep = lax.fori_loop(
        0, len_ref.shape[1], mark, (jnp.int32(0), jnp.ones((rows, lanes), jnp.float32)))
    keep_t[...] = keep


def fill_maps(maps_ref, maps_t):
    count, rows = maps_ref.shape
    turned = maps_ref[...].T
    for n in range(count):
        maps_t[n * rows:(n + 1) * rows, :] = jnp.broadcast_to(turned[:, n:n + 1], (rows, LANES))


def spread(ref, row, group):
    return ref[pl.ds(row, group, stride=0), :]


def gather_positions(src_ref, dst, group, first=0):
    rows = src_ref.shape[0]

    def move(i, _):
        t = at_chunk(i, WIDE)
        wide = src_ref[pl.ds(t, WIDE), :].astype(jnp.float32)
        dst[pl.ds(first + t, WIDE)] = wide.reshape(WIDE, group, LANES)
        return 0

    lax.fori_loop(0, rows // WIDE, move, 0)


def scatter_positions(src, dst_ref, group):
    rows = dst_ref.shape[0]

    def move(i, _):
        t = at_chunk(i, WIDE)
        wide = src[pl.ds(t, WIDE)].reshape(WIDE, group * LANES)
        dst_ref[pl.ds(t, WIDE), :] = wide.astype(dst_ref.dtype)
        return 0

    lax.fori_loop(0, rows // WIDE, move, 0)


def head_kernel(group, unroll, place_ref, len_ref, maps_ref, dt_ref, gy_ref, alog_ref, head_ref,
                keep_t, maps_t, step_t, gy_t, a2_s):
    rows = dt_ref.shape[0]
    states = alog_ref.shape[0]

    fill_keep(place_ref[0] * rows, len_ref, keep_t)
    fill_maps(maps_ref, maps_t)
    gather_positions(gy_ref, gy_t, group)
    gather_positions(dt_ref, step_t, group)
    a2_s[...] = (-LOG2E * jnp.exp(alog_ref[...])).reshape(states, group, LANES)

    def steps(i, total):
        t = at_chunk(i, CHUNK)
        step = jnp.log1p(jnp.exp(step_t[pl.ds(t, CHUNK)]))
        for k in range(CHUNK):
            one = step[k] + (1.0 - spread(keep_t, PAST + t + k, group)) * RESET_STEP
            step_t[t + k] = one
            total = total + one
        return total

    zero = jnp.zeros((group, LANES), jnp.float32)
    total = lax.fori_loop(0, rows // CHUNK, steps, zero)

    def token(i, cars):
        t = rows - 1 - i
        gy = gy_t[t]
        step = step_t[t]
        out = []
        for n in range(states):
            decay = jnp.exp2(step * a2_s[n])
            out.append(decay * (spread(maps_t, n * rows + t, group) * gy + cars[n]))
        return tuple(out)

    cars = lax.fori_loop(0, rows, token, (zero,) * states, unroll=unroll)
    for n in range(states):
        head_ref[n] = cars[n]
    head_ref[states] = total


def head_call(group, block, place, lengths, maps, dt, gy, alog):
    rows = dt.shape[0]
    states = alog.shape[0]
    width = group * LANES
    smem = pl.BlockSpec(memory_space=pltpu.SMEM)
    col = lambda i: (0, block)
    f32 = jnp.float32
    return pl.pallas_call(
        functools.partial(head_kernel, group, 8),
        grid=(1,),
        out_shape=jax.ShapeDtypeStruct((states + 1, group, LANES), f32),
        in_specs=[smem, smem, pl.BlockSpec((states, rows), lambda i: (1, 0)),
                  pl.BlockSpec((rows, width), col),
                  pl.BlockSpec((rows, width), col), pl.BlockSpec((states, width), col)],
        out_specs=pl.BlockSpec((states + 1, group, LANES), lambda i: (0, 0, 0)),
        scratch_shapes=[
            pltpu.VMEM((rows + 3 * PAST, LANES), f32),
            pltpu.VMEM((states * rows + 8, LANES), f32),
            pltpu.VMEM((rows, group, LANES), f32),
            pltpu.VMEM((rows, group, LANES), f32),
            pltpu.VMEM((states, group, LANES), f32),
        ],
        compiler_params=pltpu.CompilerParams(
            dimension_semantics=("arbitrary",), vmem_limit_bytes=HEAD_VMEM),
        cost_estimate=pl.CostEstimate(
            flops=rows * states * width * 1000, transcendentals=0,
            bytes_accessed=width * rows * states * 4),
        name="head",
    )(place, lengths, maps, dt, gy, alog)


def main_kernel(group, part, shards, place_ref, len_ref, maps_ref, x_ref, hist_ref, dt_ref, gy_ref,
                start_ref, alog_ref, cw_ref, cb_ref, sk_ref, next_ref, next2_ref, next3_ref, *rest):
    rest = rest[-24:]
    (gx_ref, gdt_ref, edge_ref, gp_ref, gm_ref,
     keep_t, maps_t, x_t, sig_t, gy_t, a2_s, small_s, start_s, gin_s,
     step_t, du_t, u_t, slope_t, w_t, v_t, gc_t, h_s, acc_s, gp_s) = rest
    rows = x_ref.shape[0]
    states = alog_ref.shape[0]
    f32 = jnp.float32
    zero = jnp.zeros((group, LANES), f32)

    fill_keep(place_ref[0] * rows, len_ref, keep_t)
    fill_maps(maps_ref, maps_t)
    gather_positions(x_ref, x_t, group, 3)
    gather_positions(gy_ref, gy_t, group)
    gather_positions(dt_ref, step_t, group)
    a2_s[...] = (-LOG2E * jnp.exp(alog_ref[...])).reshape(states, group, LANES)
    start_s[...] = start_ref[...].reshape(states, group, LANES)
    x_t[0:3] = hist_ref[...].astype(f32).reshape(3, group, LANES)
    small_s[0:4] = cw_ref[...].reshape(4, group, LANES)
    small_s[4:5] = cb_ref[...].reshape(1, group, LANES)
    small_s[5:6] = sk_ref[...].reshape(1, group, LANES)
    gc_t[0:3] = jnp.zeros((3, group, LANES), f32)
    gc_t[rows + 3:rows + 6] = jnp.zeros((3, group, LANES), f32)

    def keep_at(t):
        return spread(keep_t, PAST + t, group)

    def rows_of(i, _):
        t = at_chunk(i, CHUNK)
        for k in range(CHUNK):
            keep = keep_at(t + k)
            conv = keep_at(t + k - 2) * (small_s[0] * x_t[t + k])
            conv = keep_at(t + k - 1) * (small_s[1] * x_t[t + k + 1] + conv)
            conv = keep * (small_s[2] * x_t[t + k + 2] + conv)
            conv = small_s[4] + small_s[3] * x_t[t + k + 3] + conv
            sig = 1.0 / (1.0 + jnp.exp(-conv))
            u = conv * sig
            e = jnp.exp(step_t[t + k])
            step = jnp.log1p(e)
            step_t[t + k] = step + (1.0 - keep) * RESET_STEP
            du_t[t + k] = step * u
            u_t[t + k] = u
            sig_t[t + k] = e / (1.0 + e)
            slope_t[t + k] = sig * (1.0 + conv * (1.0 - sig))
            w_t[t + k] = step
        return 0

    lax.fori_loop(0, rows // CHUNK, rows_of, 0)

    last = shards - 1 - place_ref[0]
    for n in range(states):
        arrived = jnp.where(last >= 3, next3_ref[0, n], 0.0)
        for d, ref in ((2, next2_ref), (1, next_ref)):
            arrived = ref[0, n] + jnp.exp2(ref[0, states] * a2_s[n]) * arrived
            arrived = jnp.where(last >= d, arrived, 0.0)
        gin_s[n] = arrived

    def fold(p):
        out = p[0:8]
        for k in range(1, group // 8):
            out = out + p[k * 8:(k + 1) * 8]
        return out

    for lo in range(0, states, part):
        hi = lo + part

        for n in range(lo, hi):
            h_s[0, n - lo] = start_s[n]

        def forward(t, hs):
            step = step_t[t]
            du = du_t[t]
            out = []
            for n in range(lo, hi):
                decay = jnp.exp2(step * a2_s[n])
                h = decay * hs[n - lo] + spread(maps_t, n * rows + t, group) * du
                h_s[t + 1, n - lo] = h
                out.append(h)
            return tuple(out)

        lax.fori_loop(0, rows, forward, tuple(start_s[n] for n in range(lo, hi)), unroll=8)

        def backward(i, carry):
            cars, rates = carry
            t = rows - 1 - i
            step = step_t[t]
            du = du_t[t]
            y = gy_t[t]
            new_cars, new_rates = [], []
            w = None if lo == 0 else gc_t[t + 3]
            v = None if lo == 0 else v_t[t]
            for n in range(lo, hi):
                m = n - lo
                g = spread(maps_t, (states + n) * rows + t, group) * y + cars[m]
                acc_s[n, t] = fold(g * du)
                acc_s[states + n, t] = fold(h_s[t + 1, m] * y)
                bg = spread(maps_t, n * rows + t, group) * g
                w = bg if w is None else w + bg
                car = jnp.exp2(step * a2_s[n]) * g
                aq = a2_s[n] * (car * h_s[t, m])
                v = aq if v is None else v + aq
                new_cars.append(car)
                new_rates.append(rates[m] + step * aq)
            gc_t[t + 3] = w
            v_t[t] = v
            return tuple(new_cars), tuple(new_rates)

        _, rates = lax.fori_loop(
            0, rows, backward,
            (tuple(gin_s[n] for n in range(lo, hi)), (zero,) * part), unroll=4)
        for n in range(lo, hi):
            gp_s[n] = rates[n - lo] * LN2

    def finish(i, carry):
        taps = list(carry)
        t = at_chunk(rows // CHUNK - 1 - i, CHUNK)
        for k in range(CHUNK - 1, -1, -1):
            y = gy_t[t + k]
            u = u_t[t + k]
            w = gc_t[t + k + 3]
            grad_u = small_s[5] * y + w_t[t + k] * w
            v_t[t + k] = (u * w + LN2 * v_t[t + k]) * sig_t[t + k]
            gc = grad_u * slope_t[t + k]
            gc_t[t + k + 3] = gc
            x = small_s[0] * gc_t[t + k + 6] * keep_at(t + k + 3)
            x = (small_s[1] * gc_t[t + k + 5] + x) * keep_at(t + k + 2)
            x = (small_s[2] * gc_t[t + k + 4] + x) * keep_at(t + k + 1)
            w_t[t + k] = small_s[3] * gc + x
            e1 = keep_at(t + k) * gc
            e2 = keep_at(t + k - 1) * e1
            e3 = keep_at(t + k - 2) * e2
            taps[0] += e3 * x_t[t + k]
            taps[1] += e2 * x_t[t + k + 1]
            taps[2] += e1 * x_t[t + k + 2]
            taps[3] += gc * x_t[t + k + 3]
            taps[4] += y * u
            taps[5] += gc
        return tuple(taps)

    taps = lax.fori_loop(0, rows // CHUNK, finish, (zero,) * 6)
    for k in range(6):
        gp_s[states + k] = taps[k]
    for k in range(3):
        x = small_s[0] * gc_t[k + 3] * keep_at(k)
        x = (small_s[1] * gc_t[k + 2] + x) * keep_at(k - 1)
        x = (small_s[2] * gc_t[k + 1] + x) * keep_at(k - 2)
        small_s[6 + k] = x
    scatter_positions(w_t, gx_ref, group)
    scatter_positions(v_t, gdt_ref, group)
    edge_ref[0:3, :] = small_s[6:9].reshape(3, group * LANES)
    edge_ref[3:6, :] = w_t[rows - 3:rows].reshape(3, group * LANES)
    gp_ref[...] = gp_s[...].reshape(states + 6, group * LANES)

    def reduce_state(n, _):
        for tb in range(rows // 8):
            total = acc_s[n, tb * 8:tb * 8 + 8]
            maps_t[tb * 8:tb * 8 + 8, :] = jnp.sum(total, axis=1)
        flat = maps_t[0:rows, :].T
        gm_ref[pl.ds(n, 1), :] = jnp.sum(flat, axis=0, keepdims=True)
        return 0

    lax.fori_loop(0, 2 * states, reduce_state, 0)


def main_call(group, part, shards, block, place, lengths, maps, x, hist, dt, gy, start, alog, cw,
              cb, sk, heads, gdt):
    rows, channels = x.shape
    states = alog.shape[0]
    width = group * LANES
    smem = pl.BlockSpec(memory_space=pltpu.SMEM)
    col = lambda i, p: (0, block)
    f32 = jnp.float32
    table = pltpu.VMEM((rows, group, LANES), f32)
    vectors = pltpu.VMEM((states, group, LANES), f32)

    def later(d):
        return pl.BlockSpec((1, states + 1, group, LANES),
                            lambda i, p: (jnp.minimum(p[0] + d, shards - 1), 0, 0, 0))

    operands = [place, lengths, maps, x, hist, dt, gy, start, alog, cw, cb, sk, heads, heads, heads]
    in_specs = [smem, pl.BlockSpec((2 * states, rows), lambda i, p: (0, 0)),
                pl.BlockSpec((rows, width), col),
                pl.BlockSpec((3, width), col),
                pl.BlockSpec((rows, width), col),
                pl.BlockSpec((rows, width), col),
                pl.BlockSpec((states, width), col),
                pl.BlockSpec((states, width), col),
                pl.BlockSpec((4, width), col),
                pl.BlockSpec((1, width), col),
                pl.BlockSpec((1, width), col),
                later(1), later(2), later(3)]
    aliases = {}
    if gdt is not None:
        aliases = {len(operands): 1}
        operands.append(gdt)
        in_specs.append(pl.BlockSpec(memory_space=pl.ANY))
    return pl.pallas_call(
        functools.partial(main_kernel, group, part, shards),
        out_shape=(
            jax.ShapeDtypeStruct((rows, width), jnp.bfloat16),
            jax.ShapeDtypeStruct((rows, channels), jnp.bfloat16),
            jax.ShapeDtypeStruct((6, width), f32),
            jax.ShapeDtypeStruct((states + 6, width), f32),
            jax.ShapeDtypeStruct((2 * states, rows), f32),
        ),
        grid_spec=pltpu.PrefetchScalarGridSpec(
            num_scalar_prefetch=1,
            grid=(1,),
            in_specs=in_specs,
            out_specs=(pl.BlockSpec((rows, width), lambda i, p: (0, 0)),
                       pl.BlockSpec((rows, width), col),
                       pl.BlockSpec((6, width), lambda i, p: (0, 0)),
                       pl.BlockSpec((states + 6, width), lambda i, p: (0, 0)),
                       pl.BlockSpec((2 * states, rows), lambda i, p: (0, 0))),
            scratch_shapes=[
                pltpu.VMEM((rows + 3 * PAST, LANES), f32),
                pltpu.VMEM((2 * states * rows + 8, LANES), f32),
                pltpu.VMEM((rows + 3, group, LANES), f32),
                table, table,
                vectors,
                pltpu.VMEM((9, group, LANES), f32),
                vectors, vectors,
                table, table, table, table, table, table,
                pltpu.VMEM((rows + 6, group, LANES), f32),
                pltpu.VMEM((rows + 1, part, group, LANES), f32),
                pltpu.VMEM((2 * states, rows, 8, LANES), f32),
                pltpu.VMEM((states + 6, group, LANES), f32),
            ]),
        input_output_aliases=aliases,
        compiler_params=pltpu.CompilerParams(
            dimension_semantics=("arbitrary",), vmem_limit_bytes=MAIN_VMEM),
        cost_estimate=pl.CostEstimate(
            flops=rows * states * width * 5000, transcendentals=0,
            bytes_accessed=width * rows * states * 18),
        name="main",
    )(*operands)


def on_device(inner_x, dt_raw, grad_out, state_maps, saved_states, a_log, conv_weight, conv_bias,
              skip_gain, doc_lengths):
    rows = inner_x.shape[1]
    channels = inner_x.shape[2]
    states = a_log.shape[1]
    shards = lax.axis_size("ctx")
    sections = lax.axis_size("pipe")
    group = 16
    width = group * LANES
    blocks = channels // width
    me = lax.axis_index("ctx").astype(jnp.int32)
    place = me.reshape(1)
    maps = state_maps[0].reshape(2 * states, rows)
    x, dt, gy = inner_x[0], dt_raw[0], grad_out[0]
    hist = shift_to(x[rows - 3:], "ctx", 1)

    def after(value, *earlier):
        return lax.optimization_barrier((value,) + earlier)[0]

    own, heads = [], []
    for b in range(blocks):
        here = after(place, hist) if b == min(2, blocks - 1) else place
        own.append(head_call(group, b, here, doc_lengths, maps, dt, gy, a_log[0]))
        heads.append(lax.all_gather(own[-1], "ctx"))
    ready = after(place, *own)

    gdt = None
    maps_sum = 0.0
    arrived, edges, shares = [], [], []
    for b in range(blocks):
        here = after(ready, *arrived[:-1], *shares[:-1]) if b == blocks - 1 else ready
        gx, gdt, edge, gp, gm = main_call(
            group, 8, shards, b, here, doc_lengths, maps, x, hist, dt, gy, saved_states[0, 0],
            a_log[0], conv_weight[0], conv_bias, skip_gain, heads[b], gdt)
        arrived.append(shift_to(gx, "pipe", -1))
        if b > 0:
            gp = after(gp, shares[b - 1])
        shares.append(lax.psum(gp, "ctx"))
        edges.append(edge)
        maps_sum = maps_sum + gm
    if blocks > 1:
        edges[-1] = after(edges[-1], arrived[-2])

    edge = jnp.concatenate(edges, 1)
    mine = shift_to(edge[3:], "pipe", -1)
    pairs = [(s * shards + k, (s - 1) * shards + k - 1)
             for s in range(1, sections) for k in range(1, shards)]
    spilled = lax.ppermute(edge[:3], ("pipe", "ctx"), pairs)
    tail = (mine + spilled).astype(jnp.bfloat16)
    upstream = jnp.concatenate(arrived, 1)
    upstream = lax.dynamic_update_slice(upstream, tail, (rows - 3, 0))
    share = channels // shards
    params = lax.dynamic_slice_in_dim(jnp.concatenate(shares, 1), me * share, share, 1)
    return upstream[None], gdt[None], maps_sum.reshape(1, 2, states, rows), params[None]


def solution(mesh):
    in_specs = (
        P("pipe", "ctx", None),
        P("pipe", "ctx", None),
        P("pipe", "ctx", None),
        P("pipe", None, None, "ctx"),
        P("pipe", "ctx", None, None),
        P("pipe", None, None),
        P("pipe", None, None),
        P("pipe", None),
        P("pipe", None),
        P("pipe", None),
    )
    out_specs = (
        P("pipe", "ctx", None),
        P("pipe", "ctx", None),
        P("pipe", None, None, "ctx"),
        P("pipe", None, "ctx"),
    )
    return jax.shard_map(
        on_device, mesh=mesh, in_specs=in_specs, out_specs=out_specs, check_vma=False
    )
```

```python
import functools

import jax
import jax.numpy as jnp
from jax import lax
from jax.experimental import pallas as pl
from jax.experimental.pallas import tpu as pltpu
from jax.sharding import PartitionSpec as P

LANES = 128
LOG2E = 1.4426950408889634
LN2 = 0.6931471805599453
RESET_STEP = 1e4
PAST = 8
CHUNK = 8
WIDE = 16
MIB = 1 << 20
HEAD_VMEM = 60 * MIB
MAIN_VMEM = 60 * MIB
REACH = 3


def shift_to(x, axis, by):
    length = lax.axis_size(axis)
    pairs = [(i, i + by) for i in range(length) if 0 <= i + by < length]
    return lax.ppermute(x, axis, pairs)


def after(value, *earlier):
    return lax.optimization_barrier((value,) + earlier)[0]


def at_chunk(i, size):
    return pl.multiple_of(i * size, size)


def fill_keep(offset, len_ref, keep_t):
    rows, lanes = keep_t.shape
    place = lax.broadcasted_iota(jnp.int32, (rows, lanes), 0) + (offset - PAST)

    def mark(d, carry):
        start, keep = carry
        return start + len_ref[0, d], jnp.where(place == start, 0.0, keep)

    _, keep = lax.fori_loop(
        0, len_ref.shape[1], mark, (jnp.int32(0), jnp.ones((rows, lanes), jnp.float32)))
    keep_t[...] = keep


def fill_maps(maps_ref, maps_t):
    count, rows = maps_ref.shape
    turned = maps_ref[...].T
    for n in range(count):
        maps_t[n * rows:(n + 1) * rows, :] = jnp.broadcast_to(turned[:, n:n + 1], (rows, LANES))


def spread(ref, row, group):
    return ref[pl.ds(row, group, stride=0), :]


def gather_positions(src_ref, dst, group, first=0):
    rows = src_ref.shape[0]

    def move(i, _):
        t = at_chunk(i, WIDE)
        wide = src_ref[pl.ds(t, WIDE), :].astype(jnp.float32)
        dst[pl.ds(first + t, WIDE)] = wide.reshape(WIDE, group, LANES)
        return 0

    lax.fori_loop(0, rows // WIDE, move, 0)


def scatter_positions(src, dst_ref, group):
    rows = dst_ref.shape[0]

    def move(i, _):
        t = at_chunk(i, WIDE)
        wide = src[pl.ds(t, WIDE)].reshape(WIDE, group * LANES)
        dst_ref[pl.ds(t, WIDE), :] = wide.astype(dst_ref.dtype)
        return 0

    lax.fori_loop(0, rows // WIDE, move, 0)


def head_kernel(group, unroll, place_ref, len_ref, maps_ref, dt_ref, gy_ref, alog_ref, head_ref,
                keep_t, maps_t, step_t, gy_t, a2_s):
    rows = dt_ref.shape[0]
    states = alog_ref.shape[0]

    @pl.when(pl.program_id(0) == 0)
    def _():
        fill_keep(place_ref[0] * rows, len_ref, keep_t)
        fill_maps(maps_ref, maps_t)

    gather_positions(gy_ref, gy_t, group)
    gather_positions(dt_ref, step_t, group)
    a2_s[...] = (-LOG2E * jnp.exp(alog_ref[...])).reshape(states, group, LANES)

    def steps(i, total):
        t = at_chunk(i, CHUNK)
        step = jnp.log1p(jnp.exp(step_t[pl.ds(t, CHUNK)]))
        for k in range(CHUNK):
            one = step[k] + (1.0 - spread(keep_t, PAST + t + k, group)) * RESET_STEP
            step_t[t + k] = one
            total = total + one
        return total

    zero = jnp.zeros((group, LANES), jnp.float32)
    total = lax.fori_loop(0, rows // CHUNK, steps, zero)

    def token(i, cars):
        t = rows - 1 - i
        gy = gy_t[t]
        step = step_t[t]
        out = []
        for n in range(states):
            decay = jnp.exp2(step * a2_s[n])
            out.append(decay * (spread(maps_t, n * rows + t, group) * gy + cars[n]))
        return tuple(out)

    cars = lax.fori_loop(0, rows, token, (zero,) * states, unroll=unroll)
    for n in range(states):
        head_ref[0, n] = cars[n]
    head_ref[0, states] = total


def head_call(group, block, blocks, place, lengths, maps, dt, gy, alog):
    rows = dt.shape[0]
    states = alog.shape[0]
    width = group * LANES
    smem = pl.BlockSpec(memory_space=pltpu.SMEM)
    col = lambda i: (0, block + i)
    f32 = jnp.float32
    return pl.pallas_call(
        functools.partial(head_kernel, group, 8),
        grid=(blocks,),
        out_shape=jax.ShapeDtypeStruct((blocks, states + 1, group, LANES), f32),
        in_specs=[smem, smem, pl.BlockSpec((states, rows), lambda i: (1, 0)),
                  pl.BlockSpec((rows, width), col),
                  pl.BlockSpec((rows, width), col), pl.BlockSpec((states, width), col)],
        out_specs=pl.BlockSpec((1, states + 1, group, LANES), lambda i: (i, 0, 0, 0)),
        scratch_shapes=[
            pltpu.VMEM((rows + 3 * PAST, LANES), f32),
            pltpu.VMEM((states * rows + 8, LANES), f32),
            pltpu.VMEM((rows, group, LANES), f32),
            pltpu.VMEM((rows, group, LANES), f32),
            pltpu.VMEM((states, group, LANES), f32),
        ],
        compiler_params=pltpu.CompilerParams(
            dimension_semantics=("arbitrary",), vmem_limit_bytes=HEAD_VMEM),
        cost_estimate=pl.CostEstimate(
            flops=blocks * rows * states * width * 1000, transcendentals=0,
            bytes_accessed=blocks * width * rows * states * 4),
        name="head",
    )(place, lengths, maps, dt, gy, alog)


def main_kernel(group, part, shards, place_ref, len_ref, maps_ref, x_ref, hist_ref, dt_ref, gy_ref,
                start_ref, alog_ref, cw_ref, cb_ref, sk_ref, next_ref, next2_ref, next3_ref, *rest):
    maps_before = rest[-26] if len(rest) > 25 else None
    rest = rest[-25:]
    (gx_ref, gdt_ref, mine_ref, spill_ref, gp_ref, gm_ref,
     keep_t, maps_t, x_t, sig_t, gy_t, a2_s, small_s, start_s, gin_s,
     step_t, du_t, u_t, slope_t, w_t, v_t, gc_t, h_s, acc_s, gp_s) = rest
    rows = x_ref.shape[0]
    states = alog_ref.shape[0]
    f32 = jnp.float32
    zero = jnp.zeros((group, LANES), f32)

    fill_keep(place_ref[0] * rows, len_ref, keep_t)
    fill_maps(maps_ref, maps_t)
    gather_positions(x_ref, x_t, group, 3)
    gather_positions(gy_ref, gy_t, group)
    gather_positions(dt_ref, step_t, group)
    a2_s[...] = (-LOG2E * jnp.exp(alog_ref[...])).reshape(states, group, LANES)
    start_s[...] = start_ref[...].reshape(states, group, LANES)
    x_t[0:3] = hist_ref[...].astype(f32).reshape(3, group, LANES)
    small_s[0:4] = cw_ref[...].reshape(4, group, LANES)
    small_s[4:5] = cb_ref[...].reshape(1, group, LANES)
    small_s[5:6] = sk_ref[...].reshape(1, group, LANES)
    gc_t[0:3] = jnp.zeros((3, group, LANES), f32)
    gc_t[rows + 3:rows + 6] = jnp.zeros((3, group, LANES), f32)

    def keep_at(t):
        return spread(keep_t, PAST + t, group)

    def rows_of(i, _):
        t = at_chunk(i, CHUNK)
        for k in range(CHUNK):
            keep = keep_at(t + k)
            conv = keep_at(t + k - 2) * (small_s[0] * x_t[t + k])
            conv = keep_at(t + k - 1) * (small_s[1] * x_t[t + k + 1] + conv)
            conv = keep * (small_s[2] * x_t[t + k + 2] + conv)
            conv = small_s[4] + small_s[3] * x_t[t + k + 3] + conv
            sig = 1.0 / (1.0 + jnp.exp(-conv))
            u = conv * sig
            e = jnp.exp(step_t[t + k])
            step = jnp.log1p(e)
            step_t[t + k] = step + (1.0 - keep) * RESET_STEP
            du_t[t + k] = step * u
            u_t[t + k] = u
            sig_t[t + k] = e / (1.0 + e)
            slope_t[t + k] = sig * (1.0 + conv * (1.0 - sig))
            w_t[t + k] = step
        return 0

    lax.fori_loop(0, rows // CHUNK, rows_of, 0)

    last = shards - 1 - place_ref[0]
    for n in range(states):
        arrived = jnp.where(last >= 3, next3_ref[0, n], 0.0)
        for d, ref in ((2, next2_ref), (1, next_ref)):
            arrived = ref[0, n] + jnp.exp2(ref[0, states] * a2_s[n]) * arrived
            arrived = jnp.where(last >= d, arrived, 0.0)
        gin_s[n] = arrived

    def fold(p):
        out = p[0:8]
        for k in range(1, group // 8):
            out = out + p[k * 8:(k + 1) * 8]
        return out

    for lo in range(0, states, part):
        hi = lo + part

        for n in range(lo, hi):
            h_s[0, n - lo] = start_s[n]

        def forward(t, hs):
            step = step_t[t]
            du = du_t[t]
            out = []
            for n in range(lo, hi):
                decay = jnp.exp2(step * a2_s[n])
                h = decay * hs[n - lo] + spread(maps_t, n * rows + t, group) * du
                h_s[t + 1, n - lo] = h
                out.append(h)
            return tuple(out)

        lax.fori_loop(0, rows, forward, tuple(start_s[n] for n in range(lo, hi)), unroll=8)

        def backward(i, carry):
            cars, rates = carry
            t = rows - 1 - i
            step = step_t[t]
            du = du_t[t]
            y = gy_t[t]
            new_cars, new_rates = [], []
            w = None if lo == 0 else gc_t[t + 3]
            v = None if lo == 0 else v_t[t]
            for n in range(lo, hi):
                m = n - lo
                g = spread(maps_t, (states + n) * rows + t, group) * y + cars[m]
                acc_s[n, t] = fold(g * du)
                acc_s[states + n, t] = fold(h_s[t + 1, m] * y)
                bg = spread(maps_t, n * rows + t, group) * g
                w = bg if w is None else w + bg
                car = jnp.exp2(step * a2_s[n]) * g
                aq = a2_s[n] * (car * h_s[t, m])
                v = aq if v is None else v + aq
                new_cars.append(car)
                new_rates.append(rates[m] + step * aq)
            gc_t[t + 3] = w
            v_t[t] = v
            return tuple(new_cars), tuple(new_rates)

        _, rates = lax.fori_loop(
            0, rows, backward,
            (tuple(gin_s[n] for n in range(lo, hi)), (zero,) * part), unroll=4)
        for n in range(lo, hi):
            gp_s[n] = rates[n - lo] * LN2

    def finish(i, carry):
        taps = list(carry)
        t = at_chunk(rows // CHUNK - 1 - i, CHUNK)
        for k in range(CHUNK - 1, -1, -1):
            y = gy_t[t + k]
            u = u_t[t + k]
            w = gc_t[t + k + 3]
            grad_u = small_s[5] * y + w_t[t + k] * w
            v_t[t + k] = (u * w + LN2 * v_t[t + k]) * sig_t[t + k]
            gc = grad_u * slope_t[t + k]
            gc_t[t + k + 3] = gc
            x = small_s[0] * gc_t[t + k + 6] * keep_at(t + k + 3)
            x = (small_s[1] * gc_t[t + k + 5] + x) * keep_at(t + k + 2)
            x = (small_s[2] * gc_t[t + k + 4] + x) * keep_at(t + k + 1)
            w_t[t + k] = small_s[3] * gc + x
            e1 = keep_at(t + k) * gc
            e2 = keep_at(t + k - 1) * e1
            e3 = keep_at(t + k - 2) * e2
            taps[0] += e3 * x_t[t + k]
            taps[1] += e2 * x_t[t + k + 1]
            taps[2] += e1 * x_t[t + k + 2]
            taps[3] += gc * x_t[t + k + 3]
            taps[4] += y * u
            taps[5] += gc
        return tuple(taps)

    taps = lax.fori_loop(0, rows // CHUNK, finish, (zero,) * 6)
    for k in range(6):
        gp_s[states + k] = taps[k]
    for k in range(3):
        x = small_s[0] * gc_t[k + 3] * keep_at(k)
        x = (small_s[1] * gc_t[k + 2] + x) * keep_at(k - 1)
        x = (small_s[2] * gc_t[k + 1] + x) * keep_at(k - 2)
        small_s[6 + k] = x
    scatter_positions(w_t, gx_ref, group)
    scatter_positions(v_t, gdt_ref, group)
    mine_ref[...] = w_t[rows - 3:rows].reshape(3, group * LANES)
    spill_ref[...] = small_s[6:9].reshape(3, group * LANES)
    gp_ref[...] = gp_s[...].reshape(states + 6, group * LANES)

    sub = lax.broadcasted_iota(jnp.int32, (8, LANES), 0)

    def pair_up(parts, shift):
        low = (sub & shift) == 0
        return [jnp.where(low, a, b) + pltpu.roll(jnp.where(low, b, a), shift, 0)
                for a, b in zip(parts[::2], parts[1::2])]

    def add_sublanes(n, _):
        for tb in range(rows // 8):
            parts = [acc_s[n, tb * 8 + k] for k in range(8)]
            for shift in (1, 2, 4):
                parts = pair_up(parts, shift)
            maps_t[pl.ds(n * rows + tb * 8, 8), :] = parts[0]
        return 0

    def add_lanes(n, _):
        flat = maps_t[pl.ds(at_chunk(n, rows), rows), :].T
        total = jnp.sum(flat, axis=0, keepdims=True)
        if maps_before is not None:
            total = total + maps_before[pl.ds(n, 1), :]
        gm_ref[pl.ds(n, 1), :] = total
        return 0

    lax.fori_loop(0, 2 * states, add_sublanes, 0)
    lax.fori_loop(0, 2 * states, add_lanes, 0, unroll=4)


def main_call(group, part, shards, block, place, lengths, maps, x, hist, dt, gy, start, alog, cw,
              cb, sk, heads, carried):
    rows, channels = x.shape
    states = alog.shape[0]
    width = group * LANES
    smem = pl.BlockSpec(memory_space=pltpu.SMEM)
    col = lambda i, p: (0, block)
    f32 = jnp.float32
    table = pltpu.VMEM((rows, group, LANES), f32)
    vectors = pltpu.VMEM((states, group, LANES), f32)

    def later(d):
        return pl.BlockSpec((1, states + 1, group, LANES),
                            lambda i, p: (jnp.minimum(p[0] + d, shards - 1), 0, 0, 0))

    operands = [place, lengths, maps, x, hist, dt, gy, start, alog, cw, cb, sk, heads, heads, heads]
    in_specs = [smem, pl.BlockSpec((2 * states, rows), lambda i, p: (0, 0)),
                pl.BlockSpec((rows, width), col),
                pl.BlockSpec((3, width), col),
                pl.BlockSpec((rows, width), col),
                pl.BlockSpec((rows, width), col),
                pl.BlockSpec((states, width), col),
                pl.BlockSpec((states, width), col),
                pl.BlockSpec((4, width), col),
                pl.BlockSpec((1, width), col),
                pl.BlockSpec((1, width), col),
                later(1), later(2), later(3)]
    aliases = {}
    if carried is not None:
        aliases = {len(operands) + k: k + 1 for k in range(len(carried))}
        operands += carried
        in_specs += [pl.BlockSpec(memory_space=pl.ANY)] * (len(carried) - 1)
        in_specs.append(pl.BlockSpec((2 * states, rows), lambda i, p: (0, 0)))
    return pl.pallas_call(
        functools.partial(main_kernel, group, part, shards),
        out_shape=(
            jax.ShapeDtypeStruct((rows, width), jnp.bfloat16),
            jax.ShapeDtypeStruct((rows, channels), jnp.bfloat16),
            jax.ShapeDtypeStruct((3, channels), f32),
            jax.ShapeDtypeStruct((3, channels), f32),
            jax.ShapeDtypeStruct((states + 6, channels), f32),
            jax.ShapeDtypeStruct((2 * states, rows), f32),
        ),
        grid_spec=pltpu.PrefetchScalarGridSpec(
            num_scalar_prefetch=1,
            grid=(1,),
            in_specs=in_specs,
            out_specs=(pl.BlockSpec((rows, width), lambda i, p: (0, 0)),
                       pl.BlockSpec((rows, width), col),
                       pl.BlockSpec((3, width), col),
                       pl.BlockSpec((3, width), col),
                       pl.BlockSpec((states + 6, width), col),
                       pl.BlockSpec((2 * states, rows), lambda i, p: (0, 0))),
            scratch_shapes=[
                pltpu.VMEM((rows + 3 * PAST, LANES), f32),
                pltpu.VMEM((2 * states * rows + 8, LANES), f32),
                pltpu.VMEM((rows + 3, group, LANES), f32),
                table, table,
                vectors,
                pltpu.VMEM((9, group, LANES), f32),
                vectors, vectors,
                table, table, table, table, table, table,
                pltpu.VMEM((rows + 6, group, LANES), f32),
                pltpu.VMEM((rows + 1, part, group, LANES), f32),
                pltpu.VMEM((2 * states, rows, 8, LANES), f32),
                pltpu.VMEM((states + 6, group, LANES), f32),
            ]),
        input_output_aliases=aliases,
        compiler_params=pltpu.CompilerParams(
            dimension_semantics=("arbitrary",), vmem_limit_bytes=MAIN_VMEM),
        cost_estimate=pl.CostEstimate(
            flops=rows * states * width * 5000, transcendentals=0,
            bytes_accessed=width * rows * states * 18),
        name="main",
    )(*operands)


def join_kernel(count, *refs):
    out_ref = refs[-1]
    width = refs[0].shape[1]
    for b in range(count):
        out_ref[:, b * width:(b + 1) * width] = refs[b][...]


def join_edge_kernel(count, *refs):
    join_kernel(count, *refs[:count], refs[-1])
    rows = refs[0].shape[0]
    tail = refs[count][...] + refs[count + 1][...]
    refs[-1][rows - 3:rows, :] = tail.astype(jnp.bfloat16)


def join_call(blocks, mine=None, spilled=None):
    count = len(blocks)
    rows, width = blocks[0].shape
    edges = [] if mine is None else [mine, spilled]
    body = join_kernel if mine is None else join_edge_kernel
    return pl.pallas_call(
        functools.partial(body, count),
        out_shape=jax.ShapeDtypeStruct((rows, count * width), blocks[0].dtype),
        compiler_params=pltpu.CompilerParams(vmem_limit_bytes=16 * MIB),
        name="join",
    )(*blocks, *edges)


def on_device(inner_x, dt_raw, grad_out, state_maps, saved_states, a_log, conv_weight, conv_bias,
              skip_gain, doc_lengths):
    rows = inner_x.shape[1]
    channels = inner_x.shape[2]
    states = a_log.shape[1]
    shards = lax.axis_size("ctx")
    sections = lax.axis_size("pipe")
    group = 16
    width = group * LANES
    blocks = channels // width
    me = lax.axis_index("ctx").astype(jnp.int32)
    place = me.reshape(1)
    maps = state_maps[0].reshape(2 * states, rows)
    x, dt, gy = inner_x[0], dt_raw[0], grad_out[0]
    hist = shift_to(x[rows - 3:], "ctx", 1)

    def after(value, *earlier):
        return lax.optimization_barrier((value,) + earlier)[0]

    first = head_call(group, 0, 1, place, doc_lengths, maps, dt, gy, a_log[0])
    heads = [lax.all_gather(first[0], "ctx")]
    ready = place
    if blocks > 1:
        others = head_call(group, 1, blocks - 1, after(place, first), doc_lengths, maps, dt, gy,
                           a_log[0])
        heads += [lax.all_gather(others[b], "ctx") for b in range(blocks - 1)]
        ready = after(place, others)

    carried = None
    arrived = []
    for b in range(blocks):
        here = after(ready, *arrived[:-1]) if b == blocks - 1 else ready
        gx, *carried = main_call(
            group, 8, shards, b, here, doc_lengths, maps, x, hist, dt, gy, saved_states[0, 0],
            a_log[0], conv_weight[0], conv_bias, skip_gain, heads[b], carried)
        arrived.append(shift_to(gx, "pipe", -1))
    gdt, mine, spill, params, grad_maps = carried
    if blocks > 1:
        mine, spill, params, _ = lax.optimization_barrier((mine, spill, params, arrived[-2]))

    shares = lax.psum_scatter(params, "ctx", scatter_dimension=1, tiled=True)
    mine = shift_to(mine, "pipe", -1)
    pairs = [(s * shards + k, (s - 1) * shards + k - 1)
             for s in range(1, sections) for k in range(1, shards)]
    spilled = lax.ppermute(spill, ("pipe", "ctx"), pairs)
    upstream = join_call(arrived, mine, spilled)
    return upstream[None], gdt[None], grad_maps.reshape(1, 2, states, rows), shares[None]


def solution(mesh):
    in_specs = (
        P("pipe", "ctx", None),
        P("pipe", "ctx", None),
        P("pipe", "ctx", None),
        P("pipe", None, None, "ctx"),
        P("pipe", "ctx", None, None),
        P("pipe", None, None),
        P("pipe", None, None),
        P("pipe", None),
        P("pipe", None),
        P("pipe", None),
    )
    out_specs = (
        P("pipe", "ctx", None),
        P("pipe", "ctx", None),
        P("pipe", None, None, "ctx"),
        P("pipe", None, "ctx"),
    )
    return jax.shard_map(
        on_device, mesh=mesh, in_specs=in_specs, out_specs=out_specs, check_vma=False
    )
```

```python
import functools

import jax
import jax.numpy as jnp
from jax import lax
from jax.experimental import pallas as pl
from jax.experimental.pallas import tpu as pltpu
from jax.sharding import PartitionSpec as P

LANES = 128
LOG2E = 1.4426950408889634
LN2 = 0.6931471805599453
RESET_STEP = 1e4
PAST = 8
CHUNK = 8
WIDE = 16
MIB = 1 << 20
HEAD_VMEM = 60 * MIB
MAIN_VMEM = 60 * MIB
REACH = 3


def shift_to(x, axis, by):
    length = lax.axis_size(axis)
    pairs = [(i, i + by) for i in range(length) if 0 <= i + by < length]
    return lax.ppermute(x, axis, pairs)


def after(value, *earlier):
    return lax.optimization_barrier((value,) + earlier)[0]


def at_chunk(i, size):
    return pl.multiple_of(i * size, size)


def fill_keep(offset, len_ref, keep_t):
    rows, lanes = keep_t.shape
    place = lax.broadcasted_iota(jnp.int32, (rows, lanes), 0) + (offset - PAST)

    def mark(d, carry):
        start, keep = carry
        return start + len_ref[0, d], jnp.where(place == start, 0.0, keep)

    _, keep = lax.fori_loop(
        0, len_ref.shape[1], mark, (jnp.int32(0), jnp.ones((rows, lanes), jnp.float32)))
    keep_t[...] = keep


def fill_maps(maps_ref, maps_t):
    count, rows = maps_ref.shape
    turned = maps_ref[...].T
    for n in range(count):
        maps_t[n * rows:(n + 1) * rows, :] = jnp.broadcast_to(turned[:, n:n + 1], (rows, LANES))


def spread(ref, row, group):
    return ref[pl.ds(row, group, stride=0), :]


def gather_positions(src_ref, dst, group, first=0):
    rows = src_ref.shape[0]

    def move(i, _):
        t = at_chunk(i, WIDE)
        wide = src_ref[pl.ds(t, WIDE), :].astype(jnp.float32)
        dst[pl.ds(first + t, WIDE)] = wide.reshape(WIDE, group, LANES)
        return 0

    lax.fori_loop(0, rows // WIDE, move, 0)


def scatter_positions(src, dst_ref, group):
    rows = dst_ref.shape[0]

    def move(i, _):
        t = at_chunk(i, WIDE)
        wide = src[pl.ds(t, WIDE)].reshape(WIDE, group * LANES)
        dst_ref[pl.ds(t, WIDE), :] = wide.astype(dst_ref.dtype)
        return 0

    lax.fori_loop(0, rows // WIDE, move, 0)


def head_kernel(group, unroll, place_ref, len_ref, maps_ref, dt_ref, gy_ref, alog_ref, head_ref,
                keep_t, maps_t, step_t, gy_t, a2_s):
    rows = dt_ref.shape[0]
    states = alog_ref.shape[0]

    @pl.when(pl.program_id(0) == 0)
    def _():
        fill_keep(place_ref[0] * rows, len_ref, keep_t)
        fill_maps(maps_ref, maps_t)

    gather_positions(gy_ref, gy_t, group)
    gather_positions(dt_ref, step_t, group)
    a2_s[...] = (-LOG2E * jnp.exp(alog_ref[...])).reshape(states, group, LANES)

    def steps(i, total):
        t = at_chunk(i, CHUNK)
        step = jnp.log1p(jnp.exp(step_t[pl.ds(t, CHUNK)]))
        for k in range(CHUNK):
            one = step[k] + (1.0 - spread(keep_t, PAST + t + k, group)) * RESET_STEP
            step_t[t + k] = one
            total = total + one
        return total

    zero = jnp.zeros((group, LANES), jnp.float32)
    total = lax.fori_loop(0, rows // CHUNK, steps, zero)

    def token(i, cars):
        t = rows - 1 - i
        gy = gy_t[t]
        step = step_t[t]
        out = []
        for n in range(states):
            decay = jnp.exp2(step * a2_s[n])
            out.append(decay * (spread(maps_t, n * rows + t, group) * gy + cars[n]))
        return tuple(out)

    cars = lax.fori_loop(0, rows, token, (zero,) * states, unroll=unroll)
    for n in range(states):
        head_ref[0, n] = cars[n]
    head_ref[0, states] = total


def head_call(group, block, blocks, place, lengths, maps, dt, gy, alog):
    rows = dt.shape[0]
    states = alog.shape[0]
    width = group * LANES
    smem = pl.BlockSpec(memory_space=pltpu.SMEM)
    col = lambda i: (0, block + i)
    f32 = jnp.float32
    return pl.pallas_call(
        functools.partial(head_kernel, group, 8),
        grid=(blocks,),
        out_shape=jax.ShapeDtypeStruct((blocks, states + 1, group, LANES), f32),
        in_specs=[smem, smem, pl.BlockSpec((states, rows), lambda i: (1, 0)),
                  pl.BlockSpec((rows, width), col),
                  pl.BlockSpec((rows, width), col), pl.BlockSpec((states, width), col)],
        out_specs=pl.BlockSpec((1, states + 1, group, LANES), lambda i: (i, 0, 0, 0)),
        scratch_shapes=[
            pltpu.VMEM((rows + 3 * PAST, LANES), f32),
            pltpu.VMEM((states * rows + 8, LANES), f32),
            pltpu.VMEM((rows, group, LANES), f32),
            pltpu.VMEM((rows, group, LANES), f32),
            pltpu.VMEM((states, group, LANES), f32),
        ],
        compiler_params=pltpu.CompilerParams(
            dimension_semantics=("arbitrary",), vmem_limit_bytes=HEAD_VMEM),
        cost_estimate=pl.CostEstimate(
            flops=blocks * rows * states * width * 1000, transcendentals=0,
            bytes_accessed=blocks * width * rows * states * 4),
        name="head",
    )(place, lengths, maps, dt, gy, alog)


def main_kernel(group, part, many, place_ref, len_ref, maps_ref, x_ref, hist_ref, dt_ref, gy_ref,
                start_ref, alog_ref, cw_ref, cb_ref, sk_ref, next_ref, next2_ref, next3_ref, *rest):
    maps_before = rest[-26] if len(rest) > 25 else None
    rest = rest[-25:]
    (gx_ref, gdt_ref, mine_ref, spill_ref, gp_ref, gm_ref,
     keep_t, maps_t, x_t, sig_t, gy_t, a2_s, small_s, start_s, gin_s,
     step_t, du_t, u_t, slope_t, w_t, v_t, gc_t, h_s, acc_s, gp_s) = rest
    rows = x_ref.shape[0]
    states = alog_ref.shape[0]
    f32 = jnp.float32
    zero = jnp.zeros((group, LANES), f32)

    first = pl.program_id(0) == 0

    @pl.when(first)
    def _():
        fill_keep(place_ref[0] * rows, len_ref, keep_t)
        fill_maps(maps_ref, maps_t)

    gather_positions(x_ref, x_t, group, 3)
    gather_positions(gy_ref, gy_t, group)
    gather_positions(dt_ref, step_t, group)
    a2_s[...] = (-LOG2E * jnp.exp(alog_ref[...])).reshape(states, group, LANES)
    start_s[...] = start_ref[...].reshape(states, group, LANES)
    x_t[0:3] = hist_ref[...].astype(f32).reshape(3, group, LANES)
    small_s[0:4] = cw_ref[...].reshape(4, group, LANES)
    small_s[4:5] = cb_ref[...].reshape(1, group, LANES)
    small_s[5:6] = sk_ref[...].reshape(1, group, LANES)
    gc_t[0:3] = jnp.zeros((3, group, LANES), f32)
    gc_t[rows + 3:rows + 6] = jnp.zeros((3, group, LANES), f32)

    def keep_at(t):
        return spread(keep_t, PAST + t, group)

    def rows_of(i, _):
        t = at_chunk(i, CHUNK)
        for k in range(CHUNK):
            keep = keep_at(t + k)
            conv = keep_at(t + k - 2) * (small_s[0] * x_t[t + k])
            conv = keep_at(t + k - 1) * (small_s[1] * x_t[t + k + 1] + conv)
            conv = keep * (small_s[2] * x_t[t + k + 2] + conv)
            conv = small_s[4] + small_s[3] * x_t[t + k + 3] + conv
            sig = 1.0 / (1.0 + jnp.exp(-conv))
            u = conv * sig
            e = jnp.exp(step_t[t + k])
            step = jnp.log1p(e)
            step_t[t + k] = step + (1.0 - keep) * RESET_STEP
            du_t[t + k] = step * u
            u_t[t + k] = u
            sig_t[t + k] = e / (1.0 + e)
            slope_t[t + k] = sig * (1.0 + conv * (1.0 - sig))
            w_t[t + k] = step
        return 0

    lax.fori_loop(0, rows // CHUNK, rows_of, 0)

    for n in range(states):
        arrived = next3_ref[0, n]
        for ref in (next2_ref, next_ref):
            arrived = ref[0, n] + jnp.exp2(ref[0, states] * a2_s[n]) * arrived
        gin_s[n] = arrived

    def fold(p):
        out = p[0:8]
        for k in range(1, group // 8):
            out = out + p[k * 8:(k + 1) * 8]
        return out

    def assign(ref, n, t, value):
        ref[n, t] = value

    def add(ref, n, t, value):
        ref[n, t] += value

    def scans(put):
        for lo in range(0, states, part):
            hi = lo + part

            for n in range(lo, hi):
                h_s[0, n - lo] = start_s[n]

            def forward(t, hs):
                step = step_t[t]
                du = du_t[t]
                out = []
                for n in range(lo, hi):
                    decay = jnp.exp2(step * a2_s[n])
                    h = decay * hs[n - lo] + spread(maps_t, n * rows + t, group) * du
                    h_s[t + 1, n - lo] = h
                    out.append(h)
                return tuple(out)

            lax.fori_loop(0, rows, forward, tuple(start_s[n] for n in range(lo, hi)), unroll=8)

            def backward(i, carry):
                cars, rates = carry
                t = rows - 1 - i
                step = step_t[t]
                du = du_t[t]
                y = gy_t[t]
                new_cars, new_rates = [], []
                w = None if lo == 0 else gc_t[t + 3]
                v = None if lo == 0 else v_t[t]
                for n in range(lo, hi):
                    m = n - lo
                    g = spread(maps_t, (states + n) * rows + t, group) * y + cars[m]
                    put(acc_s, n, t, fold(g * du))
                    put(acc_s, states + n, t, fold(h_s[t + 1, m] * y))
                    bg = spread(maps_t, n * rows + t, group) * g
                    w = bg if w is None else w + bg
                    car = jnp.exp2(step * a2_s[n]) * g
                    aq = a2_s[n] * (car * h_s[t, m])
                    v = aq if v is None else v + aq
                    new_cars.append(car)
                    new_rates.append(rates[m] + step * aq)
                gc_t[t + 3] = w
                v_t[t] = v
                return tuple(new_cars), tuple(new_rates)

            _, rates = lax.fori_loop(
                0, rows, backward,
                (tuple(gin_s[n] for n in range(lo, hi)), (zero,) * part), unroll=4)
            for n in range(lo, hi):
                gp_s[n] = rates[n - lo] * LN2

    @pl.when(first)
    def _():
        scans(assign)

    if many:
        @pl.when(jnp.logical_not(first))
        def _():
            scans(add)

    def finish(i, carry):
        taps = list(carry)
        t = at_chunk(rows // CHUNK - 1 - i, CHUNK)
        for k in range(CHUNK - 1, -1, -1):
            y = gy_t[t + k]
            u = u_t[t + k]
            w = gc_t[t + k + 3]
            grad_u = small_s[5] * y + w_t[t + k] * w
            v_t[t + k] = (u * w + LN2 * v_t[t + k]) * sig_t[t + k]
            gc = grad_u * slope_t[t + k]
            gc_t[t + k + 3] = gc
            x = small_s[0] * gc_t[t + k + 6] * keep_at(t + k + 3)
            x = (small_s[1] * gc_t[t + k + 5] + x) * keep_at(t + k + 2)
            x = (small_s[2] * gc_t[t + k + 4] + x) * keep_at(t + k + 1)
            w_t[t + k] = small_s[3] * gc + x
            e1 = keep_at(t + k) * gc
            e2 = keep_at(t + k - 1) * e1
            e3 = keep_at(t + k - 2) * e2
            taps[0] += e3 * x_t[t + k]
            taps[1] += e2 * x_t[t + k + 1]
            taps[2] += e1 * x_t[t + k + 2]
            taps[3] += gc * x_t[t + k + 3]
            taps[4] += y * u
            taps[5] += gc
        return tuple(taps)

    taps = lax.fori_loop(0, rows // CHUNK, finish, (zero,) * 6)
    for k in range(6):
        gp_s[states + k] = taps[k]
    for k in range(3):
        x = small_s[0] * gc_t[k + 3] * keep_at(k)
        x = (small_s[1] * gc_t[k + 2] + x) * keep_at(k - 1)
        x = (small_s[2] * gc_t[k + 1] + x) * keep_at(k - 2)
        small_s[6 + k] = x
    scatter_positions(w_t, gx_ref, group)
    scatter_positions(v_t, gdt_ref, group)
    mine_ref[...] = w_t[rows - 3:rows].reshape(3, group * LANES)
    spill_ref[...] = small_s[6:9].reshape(3, group * LANES)
    for k in range(states + 6, gp_s.shape[0]):
        gp_s[k] = zero
    wide = gp_s[...].reshape(gp_s.shape[0], group * LANES)
    share = gp_ref.shape[2]
    for k in range(gp_ref.shape[0]):
        gp_ref[k] = wide[:, k * share:(k + 1) * share]

    sub = lax.broadcasted_iota(jnp.int32, (8, LANES), 0)

    def pair_up(parts, shift):
        low = (sub & shift) == 0
        return [jnp.where(low, a, b) + pltpu.roll(jnp.where(low, b, a), shift, 0)
                for a, b in zip(parts[::2], parts[1::2])]

    def add_sublanes(n, _):
        for tb in range(rows // 8):
            parts = [acc_s[n, tb * 8 + k] for k in range(8)]
            for shift in (1, 2, 4):
                parts = pair_up(parts, shift)
            maps_t[pl.ds(n * rows + tb * 8, 8), :] = parts[0]
        return 0

    def add_lanes(n, _):
        flat = maps_t[pl.ds(at_chunk(n, rows), rows), :].T
        total = jnp.sum(flat, axis=0, keepdims=True)
        if maps_before is not None:
            total = total + maps_before[pl.ds(n, 1), :]
        gm_ref[pl.ds(n, 1), :] = total
        return 0

    @pl.when(pl.program_id(0) == pl.num_programs(0) - 1)
    def _():
        lax.fori_loop(0, 2 * states, add_sublanes, 0)
        lax.fori_loop(0, 2 * states, add_lanes, 0, unroll=4)


def main_call(group, part, shards, block, blocks, place, lengths, maps, x, hist, dt, gy, start,
              alog, cw, cb, sk, heads, carried):
    rows, channels = x.shape
    states = alog.shape[0]
    width = group * LANES
    share = channels // shards
    params = -(-(states + 6) // 8) * 8
    smem = pl.BlockSpec(memory_space=pltpu.SMEM)
    col = lambda i: (0, block + i)
    whole = lambda i: (0, 0)
    f32 = jnp.float32
    table = pltpu.VMEM((rows, group, LANES), f32)
    vectors = pltpu.VMEM((states, group, LANES), f32)
    operands = [place, lengths, maps, x, hist, dt, gy, start, alog, cw, cb, sk, *heads]
    in_specs = [smem, smem, pl.BlockSpec((2 * states, rows), whole),
                pl.BlockSpec((rows, width), col),
                pl.BlockSpec((3, width), col),
                pl.BlockSpec((rows, width), col),
                pl.BlockSpec((rows, width), col),
                pl.BlockSpec((states, width), col),
                pl.BlockSpec((states, width), col),
                pl.BlockSpec((4, width), col),
                pl.BlockSpec((1, width), col),
                pl.BlockSpec((1, width), col)]
    in_specs += [pl.BlockSpec((1, states + 1, group, LANES), lambda i: (i, 0, 0, 0))] * REACH
    aliases = {}
    if carried is not None:
        aliases = {len(operands) + k: k + 1 for k in range(len(carried))}
        operands += carried
        in_specs += [pl.BlockSpec(memory_space=pl.ANY)] * (len(carried) - 1)
        in_specs.append(pl.BlockSpec((2 * states, rows), whole))
    return pl.pallas_call(
        functools.partial(main_kernel, group, part, blocks > 1),
        grid=(blocks,),
        out_shape=(
            jax.ShapeDtypeStruct((rows, blocks * width), jnp.bfloat16),
            jax.ShapeDtypeStruct((rows, channels), jnp.bfloat16),
            jax.ShapeDtypeStruct((3, channels), f32),
            jax.ShapeDtypeStruct((3, channels), f32),
            jax.ShapeDtypeStruct((shards, params, share), f32),
            jax.ShapeDtypeStruct((2 * states, rows), f32),
        ),
        in_specs=in_specs,
        out_specs=(pl.BlockSpec((rows, width), lambda i: (0, i)),
                   pl.BlockSpec((rows, width), col),
                   pl.BlockSpec((3, width), col),
                   pl.BlockSpec((3, width), col),
                   pl.BlockSpec((width // share, params, share), lambda i: (block + i, 0, 0)),
                   pl.BlockSpec((2 * states, rows), whole)),
        scratch_shapes=[
            pltpu.VMEM((rows + 3 * PAST, LANES), f32),
            pltpu.VMEM((2 * states * rows + 8, LANES), f32),
            pltpu.VMEM((rows + 3, group, LANES), f32),
            table, table,
            vectors,
            pltpu.VMEM((9, group, LANES), f32),
            vectors, vectors,
            table, table, table, table, table, table,
            pltpu.VMEM((rows + 6, group, LANES), f32),
            pltpu.VMEM((rows + 1, part, group, LANES), f32),
            pltpu.VMEM((2 * states, rows, 8, LANES), f32),
            pltpu.VMEM((params, group, LANES), f32),
        ],
        input_output_aliases=aliases,
        compiler_params=pltpu.CompilerParams(
            dimension_semantics=("arbitrary",), vmem_limit_bytes=MAIN_VMEM),
        cost_estimate=pl.CostEstimate(
            flops=blocks * rows * states * width * 5000, transcendentals=0,
            bytes_accessed=blocks * width * rows * states * 18),
        name="main",
    )(*operands)


def join_kernel(count, *refs):
    out_ref = refs[-1]
    rows, width = refs[0].shape
    for b in range(count):
        out_ref[:, b * width:(b + 1) * width] = refs[b][...]
    tail = refs[count][...] + refs[count + 1][...]
    out_ref[rows - 3:rows, :] = tail.astype(out_ref.dtype)


def join_call(blocks, mine, spilled):
    count = len(blocks)
    rows, width = blocks[0].shape
    return pl.pallas_call(
        functools.partial(join_kernel, count),
        out_shape=jax.ShapeDtypeStruct((rows, count * width), blocks[0].dtype),
        compiler_params=pltpu.CompilerParams(vmem_limit_bytes=16 * MIB),
        name="join",
    )(*blocks, mine, spilled)


def on_device(inner_x, dt_raw, grad_out, state_maps, saved_states, a_log, conv_weight, conv_bias,
              skip_gain, doc_lengths):
    rows = inner_x.shape[1]
    channels = inner_x.shape[2]
    states = a_log.shape[1]
    shards = lax.axis_size("ctx")
    sections = lax.axis_size("pipe")
    group = 16
    width = group * LANES
    blocks = channels // width
    me = lax.axis_index("ctx").astype(jnp.int32)
    place = me.reshape(1)
    maps = state_maps[0].reshape(2 * states, rows)
    x, dt, gy = inner_x[0], dt_raw[0], grad_out[0]
    hist = shift_to(x[rows - 3:], "ctx", 1)

    def after(value, *earlier):
        return lax.optimization_barrier((value,) + earlier)[0]

    calls = 2
    many = blocks // calls
    here, heads = place, []
    for c in range(calls):
        own = head_call(group, c * many, many, here, doc_lengths, maps, dt, gy, a_log[0])
        heads.append([shift_to(own, "ctx", -d) for d in range(1, REACH + 1)])
        here = after(place, own)

    carried = None
    arrived = []
    for c in range(calls):
        gx, *carried = main_call(
            group, 8, shards, c * many, many, here, doc_lengths, maps, x, hist, dt, gy,
            saved_states[0, 0], a_log[0], conv_weight[0], conv_bias, skip_gain, heads[c], carried)
        arrived.append(shift_to(gx, "pipe", -1))
    gdt, mine, spill, params, grad_maps = carried
    mine, spill, params, _ = lax.optimization_barrier((mine, spill, params, arrived[-2]))

    mine = shift_to(mine, "pipe", -1)
    pairs = [(s * shards + k, (s - 1) * shards + k - 1)
             for s in range(1, sections) for k in range(1, shards)]
    spilled = lax.ppermute(spill, ("pipe", "ctx"), pairs)
    shares = lax.all_to_all(params, "ctx", 0, 0, tiled=True)
    shares = jnp.sum(shares, axis=0)[:states + 6]
    upstream = join_call(arrived, mine, spilled)
    return upstream[None], gdt[None], grad_maps.reshape(1, 2, states, rows), shares[None]


def solution(mesh):
    in_specs = (
        P("pipe", "ctx", None),
        P("pipe", "ctx", None),
        P("pipe", "ctx", None),
        P("pipe", None, None, "ctx"),
        P("pipe", "ctx", None, None),
        P("pipe", None, None),
        P("pipe", None, None),
        P("pipe", None),
        P("pipe", None),
        P("pipe", None),
    )
    out_specs = (
        P("pipe", "ctx", None),
        P("pipe", "ctx", None),
        P("pipe", None, None, "ctx"),
        P("pipe", None, "ctx"),
    )
    return jax.shard_map(
        on_device, mesh=mesh, in_specs=in_specs, out_specs=out_specs, check_vma=False
    )
```

```python
import functools

import jax
import jax.numpy as jnp
from jax import lax
from jax.experimental import pallas as pl
from jax.experimental.pallas import tpu as pltpu
from jax.sharding import PartitionSpec as P

LANES = 128
LOG2E = 1.4426950408889634
LN2 = 0.6931471805599453
RESET_STEP = 1e4
PAST = 8
CHUNK = 8
WIDE = 16
MIB = 1 << 20
HEAD_VMEM = 60 * MIB
MAIN_VMEM = 60 * MIB
REACH = 3


def shift_to(x, axis, by):
    length = lax.axis_size(axis)
    pairs = [(i, i + by) for i in range(length) if 0 <= i + by < length]
    return lax.ppermute(x, axis, pairs)


def after(value, *earlier):
    return lax.optimization_barrier((value,) + earlier)[0]


def at_chunk(i, size):
    return pl.multiple_of(i * size, size)


def fill_keep(offset, len_ref, keep_t):
    rows, lanes = keep_t.shape
    place = lax.broadcasted_iota(jnp.int32, (rows, lanes), 0) + (offset - PAST)

    def mark(d, carry):
        start, keep = carry
        return start + len_ref[0, d], jnp.where(place == start, 0.0, keep)

    _, keep = lax.fori_loop(
        0, len_ref.shape[1], mark, (jnp.int32(0), jnp.ones((rows, lanes), jnp.float32)))
    keep_t[...] = keep


def fill_maps(maps_ref, maps_t):
    count, rows = maps_ref.shape
    turned = maps_ref[...].T
    for n in range(count):
        maps_t[n * rows:(n + 1) * rows, :] = jnp.broadcast_to(turned[:, n:n + 1], (rows, LANES))


def spread(ref, row, group):
    one = ref[pl.ds(row, 8, stride=0), :]
    return jnp.concatenate([one] * (group // 8), axis=0)


def gather_positions(src_ref, dst, group, first=0):
    rows = src_ref.shape[0]

    def move(i, _):
        t = at_chunk(i, WIDE)
        wide = src_ref[pl.ds(t, WIDE), :].astype(jnp.float32)
        dst[pl.ds(first + t, WIDE)] = wide.reshape(WIDE, group, LANES)
        return 0

    lax.fori_loop(0, rows // WIDE, move, 0)


def scatter_positions(src, dst_ref, group):
    rows = dst_ref.shape[0]

    def move(i, _):
        t = at_chunk(i, WIDE)
        wide = src[pl.ds(t, WIDE)].reshape(WIDE, group * LANES)
        dst_ref[pl.ds(t, WIDE), :] = wide.astype(dst_ref.dtype)
        return 0

    lax.fori_loop(0, rows // WIDE, move, 0)


def head_kernel(group, unroll, place_ref, len_ref, maps_ref, dt_ref, gy_ref, alog_ref, head_ref,
                keep_t, maps_t, step_t, gy_t, a2_s):
    rows = dt_ref.shape[0]
    states = alog_ref.shape[0]

    @pl.when(pl.program_id(0) == 0)
    def _():
        fill_keep(place_ref[0] * rows, len_ref, keep_t)
        fill_maps(maps_ref, maps_t)

    gather_positions(gy_ref, gy_t, group)
    gather_positions(dt_ref, step_t, group)
    a2_s[...] = (-LOG2E * jnp.exp(alog_ref[...])).reshape(states, group, LANES)

    def steps(i, total):
        t = at_chunk(i, CHUNK)
        step = jnp.log1p(jnp.exp(step_t[pl.ds(t, CHUNK)]))
        for k in range(CHUNK):
            one = step[k] + (1.0 - spread(keep_t, PAST + t + k, group)) * RESET_STEP
            step_t[t + k] = one
            total = total + one
        return total

    zero = jnp.zeros((group, LANES), jnp.float32)
    total = lax.fori_loop(0, rows // CHUNK, steps, zero)

    def token(i, cars):
        t = rows - 1 - i
        gy = gy_t[t]
        step = step_t[t]
        out = []
        for n in range(states):
            decay = jnp.exp2(step * a2_s[n])
            out.append(decay * (spread(maps_t, n * rows + t, group) * gy + cars[n]))
        return tuple(out)

    cars = lax.fori_loop(0, rows, token, (zero,) * states, unroll=unroll)
    for n in range(states):
        head_ref[0, n] = cars[n]
    head_ref[0, states] = total


def head_call(group, block, blocks, place, lengths, maps, dt, gy, alog):
    rows = dt.shape[0]
    states = alog.shape[0]
    width = group * LANES
    smem = pl.BlockSpec(memory_space=pltpu.SMEM)
    col = lambda i: (0, block + i)
    f32 = jnp.float32
    return pl.pallas_call(
        functools.partial(head_kernel, group, 8),
        grid=(blocks,),
        out_shape=jax.ShapeDtypeStruct((blocks, states + 1, group, LANES), f32),
        in_specs=[smem, smem, pl.BlockSpec((states, rows), lambda i: (1, 0)),
                  pl.BlockSpec((rows, width), col),
                  pl.BlockSpec((rows, width), col), pl.BlockSpec((states, width), col)],
        out_specs=pl.BlockSpec((1, states + 1, group, LANES), lambda i: (i, 0, 0, 0)),
        scratch_shapes=[
            pltpu.VMEM((rows + 3 * PAST, LANES), f32),
            pltpu.VMEM((states * rows + 8, LANES), f32),
            pltpu.VMEM((rows, group, LANES), f32),
            pltpu.VMEM((rows, group, LANES), f32),
            pltpu.VMEM((states, group, LANES), f32),
        ],
        compiler_params=pltpu.CompilerParams(
            dimension_semantics=("arbitrary",), vmem_limit_bytes=HEAD_VMEM),
        cost_estimate=pl.CostEstimate(
            flops=blocks * rows * states * width * 1000, transcendentals=0,
            bytes_accessed=blocks * width * rows * states * 4),
        name="head",
    )(place, lengths, maps, dt, gy, alog)


def main_kernel(group, part, many, place_ref, len_ref, maps_ref, x_ref, hist_ref, dt_ref, gy_ref,
                start_ref, alog_ref, cw_ref, cb_ref, sk_ref, next_ref, next2_ref, next3_ref, *rest):
    maps_before = rest[-28] if len(rest) > 27 else None
    rest = rest[-27:]
    (gx_ref, gdt_ref, mine_ref, spill_ref, gp_ref, gm_ref,
     keep_t, maps_t, x_t, sig_t, gy_t, a2_s, small_s, start_s, gin_s,
     step_t, du_t, u_t, slope_t, w_t, v_t, gc_t, h_s, accb_s, accc_s, gp_s, dec_s) = rest
    rows = x_ref.shape[0]
    states = alog_ref.shape[0]
    f32 = jnp.float32
    zero = jnp.zeros((group, LANES), f32)

    first = pl.program_id(0) == 0

    @pl.when(first)
    def _():
        fill_keep(place_ref[0] * rows, len_ref, keep_t)
        fill_maps(maps_ref, maps_t)

    gather_positions(x_ref, x_t, group, 3)
    gather_positions(gy_ref, gy_t, group, 1)
    gy_t[0:1] = jnp.zeros((1, group, LANES), f32)
    gather_positions(dt_ref, step_t, group)
    a2_s[...] = (-LOG2E * jnp.exp(alog_ref[...])).reshape(states, group, LANES)
    start_s[...] = start_ref[...].reshape(states, group, LANES)
    x_t[0:3] = hist_ref[...].astype(f32).reshape(3, group, LANES)
    small_s[0:4] = cw_ref[...].reshape(4, group, LANES)
    small_s[4:5] = cb_ref[...].reshape(1, group, LANES)
    small_s[5:6] = sk_ref[...].reshape(1, group, LANES)
    gc_t[0:3] = jnp.zeros((3, group, LANES), f32)
    gc_t[rows + 3:rows + 6] = jnp.zeros((3, group, LANES), f32)

    def keep_at(t):
        return spread(keep_t, PAST + t, group)

    def rows_of(i, _):
        t = at_chunk(i, CHUNK)
        for k in range(CHUNK):
            keep = keep_at(t + k)
            conv = keep_at(t + k - 2) * (small_s[0] * x_t[t + k])
            conv = keep_at(t + k - 1) * (small_s[1] * x_t[t + k + 1] + conv)
            conv = keep * (small_s[2] * x_t[t + k + 2] + conv)
            conv = small_s[4] + small_s[3] * x_t[t + k + 3] + conv
            sig = 1.0 / (1.0 + jnp.exp(-conv))
            u = conv * sig
            e = jnp.exp(step_t[t + k])
            step = jnp.log1p(e)
            step_t[t + k] = step + (1.0 - keep) * RESET_STEP
            du_t[t + k] = step * u
            u_t[t + k] = u
            sig_t[t + k] = e / (1.0 + e)
            slope_t[t + k] = sig * (1.0 + conv * (1.0 - sig))
            w_t[t + k] = step
        return 0

    lax.fori_loop(0, rows // CHUNK, rows_of, 0)

    for n in range(states):
        arrived = next3_ref[0, n]
        for ref in (next2_ref, next_ref):
            arrived = ref[0, n] + jnp.exp2(ref[0, states] * a2_s[n]) * arrived
        gin_s[n] = arrived

    def fold(p):
        out = p[0:8]
        for k in range(1, group // 8):
            out = out + p[k * 8:(k + 1) * 8]
        return out

    def assign(ref, n, t, value):
        ref[n, t] = value

    def add(ref, n, t, value):
        ref[n, t] += value

    def scans(put):
        for lo in range(0, states, part):
            hi = lo + part

            def forward(t, hs):
                step = step_t[t]
                du = du_t[t]
                out = []
                for n in range(lo, hi):
                    decay = jnp.exp2(step * a2_s[n])
                    h = decay * hs[n - lo] + spread(maps_t, n * rows + t, group) * du
                    h_s[t, n - lo] = hs[n - lo]
                    dec_s[t, n - lo] = decay
                    out.append(h)
                return tuple(out)

            final = lax.fori_loop(
                0, rows, forward, tuple(start_s[n] for n in range(lo, hi)), unroll=16)
            for n in range(lo, hi):
                put(accc_s, n, rows, fold(final[n - lo] * gy_t[rows]))

            def backward(i, carry):
                cars, rates = carry
                t = rows - 1 - i
                step = step_t[t]
                du = du_t[t]
                y = gy_t[t + 1]
                y_before = gy_t[t]
                new_cars, new_rates = [], []
                w = None if lo == 0 else gc_t[t + 3]
                v = None if lo == 0 else v_t[t]
                for n in range(lo, hi):
                    m = n - lo
                    g = spread(maps_t, (states + n) * rows + t, group) * y + cars[m]
                    put(accb_s, n, t, fold(g * du))
                    h = h_s[t, m]
                    put(accc_s, n, t, fold(h * y_before))
                    bg = spread(maps_t, n * rows + t, group) * g
                    w = bg if w is None else w + bg
                    car = dec_s[t, m] * g
                    aq = a2_s[n] * (car * h)
                    v = aq if v is None else v + aq
                    new_cars.append(car)
                    new_rates.append(rates[m] + step * aq)
                gc_t[t + 3] = w
                v_t[t] = v
                return tuple(new_cars), tuple(new_rates)

            _, rates = lax.fori_loop(
                0, rows, backward,
                (tuple(gin_s[n] for n in range(lo, hi)), (zero,) * part), unroll=8)
            for n in range(lo, hi):
                gp_s[n] = rates[n - lo] * LN2

    @pl.when(first)
    def _():
        scans(assign)

    if many:
        @pl.when(jnp.logical_not(first))
        def _():
            scans(add)

    def finish(i, carry):
        taps = list(carry)
        t = at_chunk(rows // CHUNK - 1 - i, CHUNK)
        for k in range(CHUNK - 1, -1, -1):
            y = gy_t[t + k + 1]
            u = u_t[t + k]
            w = gc_t[t + k + 3]
            grad_u = small_s[5] * y + w_t[t + k] * w
            v_t[t + k] = (u * w + LN2 * v_t[t + k]) * sig_t[t + k]
            gc = grad_u * slope_t[t + k]
            gc_t[t + k + 3] = gc
            x = small_s[0] * gc_t[t + k + 6] * keep_at(t + k + 3)
            x = (small_s[1] * gc_t[t + k + 5] + x) * keep_at(t + k + 2)
            x = (small_s[2] * gc_t[t + k + 4] + x) * keep_at(t + k + 1)
            w_t[t + k] = small_s[3] * gc + x
            e1 = keep_at(t + k) * gc
            e2 = keep_at(t + k - 1) * e1
            e3 = keep_at(t + k - 2) * e2
            taps[0] += e3 * x_t[t + k]
            taps[1] += e2 * x_t[t + k + 1]
            taps[2] += e1 * x_t[t + k + 2]
            taps[3] += gc * x_t[t + k + 3]
            taps[4] += y * u
            taps[5] += gc
        return tuple(taps)

    taps = lax.fori_loop(0, rows // CHUNK, finish, (zero,) * 6)
    for k in range(6):
        gp_s[states + k] = taps[k]
    for k in range(3):
        x = small_s[0] * gc_t[k + 3] * keep_at(k)
        x = (small_s[1] * gc_t[k + 2] + x) * keep_at(k - 1)
        x = (small_s[2] * gc_t[k + 1] + x) * keep_at(k - 2)
        small_s[6 + k] = x
    scatter_positions(w_t, gx_ref, group)
    scatter_positions(v_t, gdt_ref, group)
    mine_ref[...] = w_t[rows - 3:rows].reshape(3, group * LANES)
    spill_ref[...] = small_s[6:9].reshape(3, group * LANES)
    for k in range(states + 6, gp_s.shape[0]):
        gp_s[k] = zero
    wide = gp_s[...].reshape(gp_s.shape[0], group * LANES)
    share = gp_ref.shape[2]
    for k in range(gp_ref.shape[0]):
        gp_ref[k] = wide[:, k * share:(k + 1) * share]

    sub = lax.broadcasted_iota(jnp.int32, (8, LANES), 0)

    def pair_up(parts, shift):
        low = (sub & shift) == 0
        return [jnp.where(low, a, b) + pltpu.roll(jnp.where(low, b, a), shift, 0)
                for a, b in zip(parts[::2], parts[1::2])]

    def add_sublanes(ref, ahead, base):
        def add_state(n, _):
            for tb in range(rows // 8):
                parts = [ref[n, tb * 8 + k + ahead] for k in range(8)]
                for shift in (1, 2, 4):
                    parts = pair_up(parts, shift)
                maps_t[pl.ds((base + n) * rows + tb * 8, 8), :] = parts[0]
            return 0

        lax.fori_loop(0, states, add_state, 0)

    def add_lanes(n, _):
        flat = maps_t[pl.ds(at_chunk(n, rows), rows), :].T
        total = jnp.sum(flat, axis=0, keepdims=True)
        if maps_before is not None:
            total = total + maps_before[pl.ds(n, 1), :]
        gm_ref[pl.ds(n, 1), :] = total
        return 0

    @pl.when(pl.program_id(0) == pl.num_programs(0) - 1)
    def _():
        add_sublanes(accb_s, 0, 0)
        add_sublanes(accc_s, 1, states)
        lax.fori_loop(0, 2 * states, add_lanes, 0, unroll=4)


def main_call(group, part, shards, block, blocks, place, lengths, maps, x, hist, dt, gy, start,
              alog, cw, cb, sk, heads, carried):
    rows, channels = x.shape
    states = alog.shape[0]
    width = group * LANES
    share = channels // shards
    params = -(-(states + 6) // 8) * 8
    smem = pl.BlockSpec(memory_space=pltpu.SMEM)
    col = lambda i: (0, block + i)
    whole = lambda i: (0, 0)
    f32 = jnp.float32
    table = pltpu.VMEM((rows, group, LANES), f32)
    vectors = pltpu.VMEM((states, group, LANES), f32)
    operands = [place, lengths, maps, x, hist, dt, gy, start, alog, cw, cb, sk, *heads]
    in_specs = [smem, smem, pl.BlockSpec((2 * states, rows), whole),
                pl.BlockSpec((rows, width), col),
                pl.BlockSpec((3, width), col),
                pl.BlockSpec((rows, width), col),
                pl.BlockSpec((rows, width), col),
                pl.BlockSpec((states, width), col),
                pl.BlockSpec((states, width), col),
                pl.BlockSpec((4, width), col),
                pl.BlockSpec((1, width), col),
                pl.BlockSpec((1, width), col)]
    in_specs += [pl.BlockSpec((1, states + 1, group, LANES), lambda i: (i, 0, 0, 0))] * REACH
    aliases = {}
    if carried is not None:
        aliases = {len(operands) + k: k + 1 for k in range(len(carried))}
        operands += carried
        in_specs += [pl.BlockSpec(memory_space=pl.ANY)] * (len(carried) - 1)
        in_specs.append(pl.BlockSpec((2 * states, rows), whole))
    return pl.pallas_call(
        functools.partial(main_kernel, group, part, blocks > 1),
        grid=(blocks,),
        out_shape=(
            jax.ShapeDtypeStruct((rows, blocks * width), jnp.bfloat16),
            jax.ShapeDtypeStruct((rows, channels), jnp.bfloat16),
            jax.ShapeDtypeStruct((3, channels), f32),
            jax.ShapeDtypeStruct((3, channels), f32),
            jax.ShapeDtypeStruct((shards, params, share), f32),
            jax.ShapeDtypeStruct((2 * states, rows), f32),
        ),
        in_specs=in_specs,
        out_specs=(pl.BlockSpec((rows, width), lambda i: (0, i)),
                   pl.BlockSpec((rows, width), col),
                   pl.BlockSpec((3, width), col),
                   pl.BlockSpec((3, width), col),
                   pl.BlockSpec((width // share, params, share), lambda i: (block + i, 0, 0)),
                   pl.BlockSpec((2 * states, rows), whole)),
        scratch_shapes=[
            pltpu.VMEM((rows + 3 * PAST, LANES), f32),
            pltpu.VMEM((2 * states * rows + 8, LANES), f32),
            pltpu.VMEM((rows + 3, group, LANES), f32),
            table,
            pltpu.VMEM((rows + 1, group, LANES), f32),
            vectors,
            pltpu.VMEM((9, group, LANES), f32),
            vectors, vectors,
            table, table, table, table, table, table,
            pltpu.VMEM((rows + 6, group, LANES), f32),
            pltpu.VMEM((rows, part, group, LANES), f32),
            pltpu.VMEM((states, rows, 8, LANES), f32),
            pltpu.VMEM((states, rows + 1, 8, LANES), f32),
            pltpu.VMEM((params, group, LANES), f32),
            pltpu.VMEM((rows, part, group, LANES), f32),
        ],
        input_output_aliases=aliases,
        compiler_params=pltpu.CompilerParams(
            dimension_semantics=("arbitrary",), vmem_limit_bytes=MAIN_VMEM),
        cost_estimate=pl.CostEstimate(
            flops=blocks * rows * states * width * 5000, transcendentals=0,
            bytes_accessed=blocks * width * rows * states * 18),
        name="main",
    )(*operands)


def join_kernel(count, *refs):
    out_ref = refs[-1]
    rows, width = refs[0].shape
    for b in range(count):
        out_ref[:, b * width:(b + 1) * width] = refs[b][...]
    tail = refs[count][...] + refs[count + 1][...]
    out_ref[rows - 3:rows, :] = tail.astype(out_ref.dtype)


def join_call(blocks, mine, spilled):
    count = len(blocks)
    rows, width = blocks[0].shape
    return pl.pallas_call(
        functools.partial(join_kernel, count),
        out_shape=jax.ShapeDtypeStruct((rows, count * width), blocks[0].dtype),
        compiler_params=pltpu.CompilerParams(vmem_limit_bytes=16 * MIB),
        name="join",
    )(*blocks, mine, spilled)


def on_device(inner_x, dt_raw, grad_out, state_maps, saved_states, a_log, conv_weight, conv_bias,
              skip_gain, doc_lengths):
    rows = inner_x.shape[1]
    channels = inner_x.shape[2]
    states = a_log.shape[1]
    shards = lax.axis_size("ctx")
    sections = lax.axis_size("pipe")
    group = 16
    width = group * LANES
    blocks = channels // width
    me = lax.axis_index("ctx").astype(jnp.int32)
    place = me.reshape(1)
    maps = state_maps[0].reshape(2 * states, rows)
    x, dt, gy = inner_x[0], dt_raw[0], grad_out[0]
    hist = shift_to(x[rows - 3:], "ctx", 1)

    def after(value, *earlier):
        return lax.optimization_barrier((value,) + earlier)[0]

    calls = 2
    many = blocks // calls
    here, heads = place, []
    for c in range(calls):
        own = head_call(group, c * many, many, here, doc_lengths, maps, dt, gy, a_log[0])
        heads.append([shift_to(own, "ctx", -d) for d in range(1, REACH + 1)])
        here = after(place, own)

    carried = None
    arrived = []
    for c in range(calls):
        gx, *carried = main_call(
            group, 4, shards, c * many, many, here, doc_lengths, maps, x, hist, dt, gy,
            saved_states[0, 0], a_log[0], conv_weight[0], conv_bias, skip_gain, heads[c], carried)
        arrived.append(shift_to(gx, "pipe", -1))
    gdt, mine, spill, params, grad_maps = carried
    mine, spill, params, _ = lax.optimization_barrier((mine, spill, params, arrived[-2]))

    mine = shift_to(mine, "pipe", -1)
    pairs = [(s * shards + k, (s - 1) * shards + k - 1)
             for s in range(1, sections) for k in range(1, shards)]
    spilled = lax.ppermute(spill, ("pipe", "ctx"), pairs)
    sides = params.reshape((shards // 2, 2) + params.shape[1:])
    side = me % 2
    given = lax.dynamic_index_in_dim(sides, 1 - side, 1, keepdims=False)
    got = lax.ppermute(given, "ctx", [(k, k ^ 1) for k in range(shards)])
    half = lax.dynamic_index_in_dim(sides, side, 1, keepdims=False) + got
    groups = [list(range(k, shards, 2)) for k in range(2)]
    shares = lax.all_to_all(half, "ctx", 0, 0, tiled=True, axis_index_groups=groups)
    shares = jnp.sum(shares, axis=0)[:states + 6]
    upstream = join_call(arrived, mine, spilled)
    return upstream[None], gdt[None], grad_maps.reshape(1, 2, states, rows), shares[None]


def solution(mesh):
    in_specs = (
        P("pipe", "ctx", None),
        P("pipe", "ctx", None),
        P("pipe", "ctx", None),
        P("pipe", None, None, "ctx"),
        P("pipe", "ctx", None, None),
        P("pipe", None, None),
        P("pipe", None, None),
        P("pipe", None),
        P("pipe", None),
        P("pipe", None),
    )
    out_specs = (
        P("pipe", "ctx", None),
        P("pipe", "ctx", None),
        P("pipe", None, None, "ctx"),
        P("pipe", None, "ctx"),
    )
    return jax.shard_map(
        on_device, mesh=mesh, in_specs=in_specs, out_specs=out_specs, check_vma=False
    )
```

```python
import functools

import jax
import jax.numpy as jnp
from jax import lax
from jax.experimental import pallas as pl
from jax.experimental.pallas import tpu as pltpu
from jax.sharding import PartitionSpec as P

LANES = 128
LOG2E = 1.4426950408889634
LN2 = 0.6931471805599453
RESET_STEP = 1e4
PAST = 8
CHUNK = 8
WIDE = 16
MIB = 1 << 20
HEAD_VMEM = 60 * MIB
MAIN_VMEM = 60 * MIB
REACH = 3


def shift_to(x, axis, by):
    length = lax.axis_size(axis)
    pairs = [(i, i + by) for i in range(length) if 0 <= i + by < length]
    return lax.ppermute(x, axis, pairs)


def after(value, *earlier):
    return lax.optimization_barrier((value,) + earlier)[0]


def at_chunk(i, size):
    return pl.multiple_of(i * size, size)


def fill_keep(offset, len_ref, keep_t):
    rows, lanes = keep_t.shape
    place = lax.broadcasted_iota(jnp.int32, (rows, lanes), 0) + (offset - PAST)

    def mark(d, carry):
        start, keep = carry
        return start + len_ref[0, d], jnp.where(place == start, 0.0, keep)

    _, keep = lax.fori_loop(
        0, len_ref.shape[1], mark, (jnp.int32(0), jnp.ones((rows, lanes), jnp.float32)))
    keep_t[...] = keep


def fill_maps(maps_ref, maps_t):
    count, rows = maps_ref.shape
    turned = maps_ref[...].T
    for n in range(count):
        maps_t[n * rows:(n + 1) * rows, :] = jnp.broadcast_to(turned[:, n:n + 1], (rows, LANES))


def spread(ref, row, group):
    one = ref[pl.ds(row, 8, stride=0), :]
    return jnp.concatenate([one] * (group // 8), axis=0)


def gather_positions(src_ref, dst, group, first=0):
    rows = src_ref.shape[0]

    def move(i, _):
        t = at_chunk(i, WIDE)
        wide = src_ref[pl.ds(t, WIDE), :].astype(jnp.float32)
        dst[pl.ds(first + t, WIDE)] = wide.reshape(WIDE, group, LANES)
        return 0

    lax.fori_loop(0, rows // WIDE, move, 0)


def scatter_positions(src, dst_ref, group):
    rows = dst_ref.shape[0]

    def move(i, _):
        t = at_chunk(i, WIDE)
        wide = src[pl.ds(t, WIDE)].reshape(WIDE, group * LANES)
        dst_ref[pl.ds(t, WIDE), :] = wide.astype(dst_ref.dtype)
        return 0

    lax.fori_loop(0, rows // WIDE, move, 0)


def head_kernel(group, unroll, place_ref, len_ref, maps_ref, dt_ref, gy_ref, alog_ref, head_ref,
                keep_t, maps_t, step_t, gy_t, a2_s):
    rows = dt_ref.shape[0]
    states = alog_ref.shape[0]

    @pl.when(pl.program_id(0) == 0)
    def _():
        fill_keep(place_ref[0] * rows, len_ref, keep_t)
        fill_maps(maps_ref, maps_t)

    gather_positions(gy_ref, gy_t, group)
    gather_positions(dt_ref, step_t, group)
    a2_s[...] = (-LOG2E * jnp.exp(alog_ref[...])).reshape(states, group, LANES)

    def steps(i, total):
        t = at_chunk(i, CHUNK)
        step = jnp.log1p(jnp.exp(step_t[pl.ds(t, CHUNK)]))
        for k in range(CHUNK):
            one = step[k] + (1.0 - spread(keep_t, PAST + t + k, group)) * RESET_STEP
            step_t[t + k] = one
            total = total + one
        return total

    zero = jnp.zeros((group, LANES), jnp.float32)
    total = lax.fori_loop(0, rows // CHUNK, steps, zero)

    def token(i, cars):
        t = rows - 1 - i
        gy = gy_t[t]
        step = step_t[t]
        out = []
        for n in range(states):
            decay = jnp.exp2(step * a2_s[n])
            out.append(decay * (spread(maps_t, n * rows + t, group) * gy + cars[n]))
        return tuple(out)

    cars = lax.fori_loop(0, rows, token, (zero,) * states, unroll=unroll)
    for n in range(states):
        head_ref[0, n] = cars[n]
    head_ref[0, states] = total


def head_call(group, block, blocks, place, lengths, maps, dt, gy, alog):
    rows = dt.shape[0]
    states = alog.shape[0]
    width = group * LANES
    smem = pl.BlockSpec(memory_space=pltpu.SMEM)
    col = lambda i: (0, block + i)
    f32 = jnp.float32
    return pl.pallas_call(
        functools.partial(head_kernel, group, 8),
        grid=(blocks,),
        out_shape=jax.ShapeDtypeStruct((blocks, states + 1, group, LANES), f32),
        in_specs=[smem, smem, pl.BlockSpec((states, rows), lambda i: (1, 0)),
                  pl.BlockSpec((rows, width), col),
                  pl.BlockSpec((rows, width), col), pl.BlockSpec((states, width), col)],
        out_specs=pl.BlockSpec((1, states + 1, group, LANES), lambda i: (i, 0, 0, 0)),
        scratch_shapes=[
            pltpu.VMEM((rows + 3 * PAST, LANES), f32),
            pltpu.VMEM((states * rows + 8, LANES), f32),
            pltpu.VMEM((rows, group, LANES), f32),
            pltpu.VMEM((rows, group, LANES), f32),
            pltpu.VMEM((states, group, LANES), f32),
        ],
        compiler_params=pltpu.CompilerParams(
            dimension_semantics=("arbitrary",), vmem_limit_bytes=HEAD_VMEM),
        cost_estimate=pl.CostEstimate(
            flops=blocks * rows * states * width * 1000, transcendentals=0,
            bytes_accessed=blocks * width * rows * states * 4),
        name="head",
    )(place, lengths, maps, dt, gy, alog)


def main_kernel(group, part, many, place_ref, len_ref, maps_ref, x_ref, hist_ref, dt_ref, gy_ref,
                start_ref, alog_ref, cw_ref, cb_ref, sk_ref, next_ref, next2_ref, next3_ref, *rest):
    maps_before = rest[-28] if len(rest) > 27 else None
    rest = rest[-27:]
    (gx_ref, gdt_ref, mine_ref, spill_ref, gp_ref, gm_ref,
     keep_t, maps_t, x_t, sig_t, gy_t, a2_s, small_s, start_s, gin_s,
     step_t, du_t, u_t, slope_t, w_t, v_t, gc_t, h_s, accb_s, accc_s, gp_s, dec_s) = rest
    rows = x_ref.shape[0]
    states = alog_ref.shape[0]
    f32 = jnp.float32
    zero = jnp.zeros((group, LANES), f32)

    first = pl.program_id(0) == 0

    @pl.when(first)
    def _():
        fill_keep(place_ref[0] * rows, len_ref, keep_t)
        fill_maps(maps_ref, maps_t)

    gather_positions(x_ref, x_t, group, 3)
    gather_positions(gy_ref, gy_t, group, 1)
    gy_t[0:1] = jnp.zeros((1, group, LANES), f32)
    gather_positions(dt_ref, step_t, group)
    a2_s[...] = (-LOG2E * jnp.exp(alog_ref[...])).reshape(states, group, LANES)
    start_s[...] = start_ref[...].reshape(states, group, LANES)
    x_t[0:3] = hist_ref[...].astype(f32).reshape(3, group, LANES)
    small_s[0:4] = cw_ref[...].reshape(4, group, LANES)
    small_s[4:5] = cb_ref[...].reshape(1, group, LANES)
    small_s[5:6] = sk_ref[...].reshape(1, group, LANES)
    gc_t[0:3] = jnp.zeros((3, group, LANES), f32)
    gc_t[rows + 3:rows + 6] = jnp.zeros((3, group, LANES), f32)

    def keep_at(t):
        return spread(keep_t, PAST + t, group)

    def rows_of(i, _):
        t = at_chunk(i, CHUNK)
        for k in range(CHUNK):
            keep = keep_at(t + k)
            conv = keep_at(t + k - 2) * (small_s[0] * x_t[t + k])
            conv = keep_at(t + k - 1) * (small_s[1] * x_t[t + k + 1] + conv)
            conv = keep * (small_s[2] * x_t[t + k + 2] + conv)
            conv = small_s[4] + small_s[3] * x_t[t + k + 3] + conv
            sig = 1.0 / (1.0 + jnp.exp(-conv))
            u = conv * sig
            e = jnp.exp(step_t[t + k])
            step = jnp.log1p(e)
            step_t[t + k] = step + (1.0 - keep) * RESET_STEP
            du_t[t + k] = step * u
            u_t[t + k] = u
            sig_t[t + k] = e / (1.0 + e)
            slope_t[t + k] = sig * (1.0 + conv * (1.0 - sig))
            w_t[t + k] = step
        return 0

    lax.fori_loop(0, rows // CHUNK, rows_of, 0)

    for n in range(states):
        arrived = next3_ref[0, n]
        for ref in (next2_ref, next_ref):
            arrived = ref[0, n] + jnp.exp2(ref[0, states] * a2_s[n]) * arrived
        gin_s[n] = arrived

    def fold(p):
        out = p[0:8]
        for k in range(1, group // 8):
            out = out + p[k * 8:(k + 1) * 8]
        return out

    def assign(ref, n, t, value):
        ref[n, t] = value

    def add(ref, n, t, value):
        ref[n, t] += value

    def scans(put):
        for lo in range(0, states, part):
            hi = lo + part

            def forward(t, hs):
                step = step_t[t]
                du = du_t[t]
                out = []
                for n in range(lo, hi):
                    decay = jnp.exp2(step * a2_s[n])
                    h = decay * hs[n - lo] + spread(maps_t, n * rows + t, group) * du
                    h_s[t, n - lo] = hs[n - lo]
                    dec_s[t, n - lo] = decay
                    out.append(h)
                return tuple(out)

            final = lax.fori_loop(
                0, rows, forward, tuple(start_s[n] for n in range(lo, hi)), unroll=16)
            for n in range(lo, hi):
                put(accc_s, n, rows, fold(final[n - lo] * gy_t[rows]))

            def backward(i, carry):
                cars, rates = carry
                t = rows - 1 - i
                step = step_t[t]
                du = du_t[t]
                y = gy_t[t + 1]
                y_before = gy_t[t]
                new_cars, new_rates = [], []
                w = None if lo == 0 else gc_t[t + 3]
                v = None if lo == 0 else v_t[t]
                for n in range(lo, hi):
                    m = n - lo
                    g = spread(maps_t, (states + n) * rows + t, group) * y + cars[m]
                    put(accb_s, n, t, fold(g * du))
                    h = h_s[t, m]
                    put(accc_s, n, t, fold(h * y_before))
                    bg = spread(maps_t, n * rows + t, group) * g
                    w = bg if w is None else w + bg
                    car = dec_s[t, m] * g
                    aq = a2_s[n] * (car * h)
                    v = aq if v is None else v + aq
                    new_cars.append(car)
                    new_rates.append(rates[m] + step * aq)
                gc_t[t + 3] = w
                v_t[t] = v
                return tuple(new_cars), tuple(new_rates)

            _, rates = lax.fori_loop(
                0, rows, backward,
                (tuple(gin_s[n] for n in range(lo, hi)), (zero,) * part), unroll=8)
            for n in range(lo, hi):
                gp_s[n] = rates[n - lo] * LN2

    @pl.when(first)
    def _():
        scans(assign)

    if many:
        @pl.when(jnp.logical_not(first))
        def _():
            scans(add)

    def finish(i, carry):
        taps = list(carry)
        t = at_chunk(rows // CHUNK - 1 - i, CHUNK)
        for k in range(CHUNK - 1, -1, -1):
            y = gy_t[t + k + 1]
            u = u_t[t + k]
            w = gc_t[t + k + 3]
            grad_u = small_s[5] * y + w_t[t + k] * w
            v_t[t + k] = (u * w + LN2 * v_t[t + k]) * sig_t[t + k]
            gc = grad_u * slope_t[t + k]
            gc_t[t + k + 3] = gc
            x = small_s[0] * gc_t[t + k + 6] * keep_at(t + k + 3)
            x = (small_s[1] * gc_t[t + k + 5] + x) * keep_at(t + k + 2)
            x = (small_s[2] * gc_t[t + k + 4] + x) * keep_at(t + k + 1)
            w_t[t + k] = small_s[3] * gc + x
            e1 = keep_at(t + k) * gc
            e2 = keep_at(t + k - 1) * e1
            e3 = keep_at(t + k - 2) * e2
            taps[0] += e3 * x_t[t + k]
            taps[1] += e2 * x_t[t + k + 1]
            taps[2] += e1 * x_t[t + k + 2]
            taps[3] += gc * x_t[t + k + 3]
            taps[4] += y * u
            taps[5] += gc
        return tuple(taps)

    taps = lax.fori_loop(0, rows // CHUNK, finish, (zero,) * 6)
    for k in range(6):
        gp_s[states + k] = taps[k]
    for k in range(3):
        x = small_s[0] * gc_t[k + 3] * keep_at(k)
        x = (small_s[1] * gc_t[k + 2] + x) * keep_at(k - 1)
        x = (small_s[2] * gc_t[k + 1] + x) * keep_at(k - 2)
        small_s[6 + k] = x
    scatter_positions(w_t, gx_ref, group)
    scatter_positions(v_t, gdt_ref, group)
    mine_ref[...] = w_t[rows - 3:rows].reshape(3, group * LANES)
    spill_ref[...] = small_s[6:9].reshape(3, group * LANES)
    for k in range(states + 6, gp_s.shape[0]):
        gp_s[k] = zero
    wide = gp_s[...].reshape(gp_s.shape[0], group * LANES)
    share = gp_ref.shape[2]
    for k in range(gp_ref.shape[0]):
        gp_ref[k] = wide[:, k * share:(k + 1) * share]

    sub = lax.broadcasted_iota(jnp.int32, (8, LANES), 0)

    def pair_up(parts, shift):
        low = (sub & shift) == 0
        return [jnp.where(low, a, b) + pltpu.roll(jnp.where(low, b, a), shift, 0)
                for a, b in zip(parts[::2], parts[1::2])]

    def add_sublanes(ref, ahead, base):
        def add_state(n, _):
            for tb in range(rows // 8):
                parts = [ref[n, tb * 8 + k + ahead] for k in range(8)]
                for shift in (1, 2, 4):
                    parts = pair_up(parts, shift)
                maps_t[pl.ds((base + n) * rows + tb * 8, 8), :] = parts[0]
            return 0

        lax.fori_loop(0, states, add_state, 0)

    def add_lanes(n, _):
        flat = maps_t[pl.ds(at_chunk(n, rows), rows), :].T
        total = jnp.sum(flat, axis=0, keepdims=True)
        if maps_before is not None:
            total = total + maps_before[pl.ds(n, 1), :]
        gm_ref[pl.ds(n, 1), :] = total
        return 0

    @pl.when(pl.program_id(0) == pl.num_programs(0) - 1)
    def _():
        add_sublanes(accb_s, 0, 0)
        add_sublanes(accc_s, 1, states)
        lax.fori_loop(0, 2 * states, add_lanes, 0, unroll=4)


def main_call(group, part, shards, block, blocks, skip, place, lengths, maps, x, hist, dt, gy, start,
              alog, cw, cb, sk, heads, carried):
    rows, channels = x.shape
    states = alog.shape[0]
    width = group * LANES
    share = channels // shards
    params = -(-(states + 6) // 8) * 8
    smem = pl.BlockSpec(memory_space=pltpu.SMEM)
    col = lambda i: (0, block + i)
    whole = lambda i: (0, 0)
    f32 = jnp.float32
    table = pltpu.VMEM((rows, group, LANES), f32)
    vectors = pltpu.VMEM((states, group, LANES), f32)
    operands = [place, lengths, maps, x, hist, dt, gy, start, alog, cw, cb, sk, *heads]
    in_specs = [smem, smem, pl.BlockSpec((2 * states, rows), whole),
                pl.BlockSpec((rows, width), col),
                pl.BlockSpec((3, width), col),
                pl.BlockSpec((rows, width), col),
                pl.BlockSpec((rows, width), col),
                pl.BlockSpec((states, width), col),
                pl.BlockSpec((states, width), col),
                pl.BlockSpec((4, width), col),
                pl.BlockSpec((1, width), col),
                pl.BlockSpec((1, width), col)]
    in_specs += [pl.BlockSpec((1, states + 1, group, LANES), lambda i: (skip + i, 0, 0, 0))] * REACH
    aliases = {}
    if carried is not None:
        aliases = {len(operands) + k: k + 1 for k in range(len(carried))}
        operands += carried
        in_specs += [pl.BlockSpec(memory_space=pl.ANY)] * (len(carried) - 1)
        in_specs.append(pl.BlockSpec((2 * states, rows), whole))
    return pl.pallas_call(
        functools.partial(main_kernel, group, part, blocks > 1),
        grid=(blocks,),
        out_shape=(
            jax.ShapeDtypeStruct((rows, blocks * width), jnp.bfloat16),
            jax.ShapeDtypeStruct((rows, channels), jnp.bfloat16),
            jax.ShapeDtypeStruct((3, channels), f32),
            jax.ShapeDtypeStruct((3, channels), f32),
            jax.ShapeDtypeStruct((shards, params, share), f32),
            jax.ShapeDtypeStruct((2 * states, rows), f32),
        ),
        in_specs=in_specs,
        out_specs=(pl.BlockSpec((rows, width), lambda i: (0, i)),
                   pl.BlockSpec((rows, width), col),
                   pl.BlockSpec((3, width), col),
                   pl.BlockSpec((3, width), col),
                   pl.BlockSpec((width // share, params, share), lambda i: (block + i, 0, 0)),
                   pl.BlockSpec((2 * states, rows), whole)),
        scratch_shapes=[
            pltpu.VMEM((rows + 3 * PAST, LANES), f32),
            pltpu.VMEM((2 * states * rows + 8, LANES), f32),
            pltpu.VMEM((rows + 3, group, LANES), f32),
            table,
            pltpu.VMEM((rows + 1, group, LANES), f32),
            vectors,
            pltpu.VMEM((9, group, LANES), f32),
            vectors, vectors,
            table, table, table, table, table, table,
            pltpu.VMEM((rows + 6, group, LANES), f32),
            pltpu.VMEM((rows, part, group, LANES), f32),
            pltpu.VMEM((states, rows, 8, LANES), f32),
            pltpu.VMEM((states, rows + 1, 8, LANES), f32),
            pltpu.VMEM((params, group, LANES), f32),
            pltpu.VMEM((rows, part, group, LANES), f32),
        ],
        input_output_aliases=aliases,
        compiler_params=pltpu.CompilerParams(
            dimension_semantics=("arbitrary",), vmem_limit_bytes=MAIN_VMEM),
        cost_estimate=pl.CostEstimate(
            flops=blocks * rows * states * width * 5000, transcendentals=0,
            bytes_accessed=blocks * width * rows * states * 18),
        name="main",
    )(*operands)


def join_kernel(count, *refs):
    out_ref = refs[-1]
    rows = out_ref.shape[0]
    at = 0
    for ref in refs[:count]:
        out_ref[:, at:at + ref.shape[1]] = ref[...]
        at += ref.shape[1]
    tail = refs[count][...] + refs[count + 1][...]
    out_ref[rows - 3:rows, :] = tail.astype(out_ref.dtype)


def join_call(blocks, mine, spilled):
    count = len(blocks)
    rows = blocks[0].shape[0]
    return pl.pallas_call(
        functools.partial(join_kernel, count),
        out_shape=jax.ShapeDtypeStruct((rows, mine.shape[1]), blocks[0].dtype),
        compiler_params=pltpu.CompilerParams(vmem_limit_bytes=16 * MIB),
        name="join",
    )(*blocks, mine, spilled)


def on_device(inner_x, dt_raw, grad_out, state_maps, saved_states, a_log, conv_weight, conv_bias,
              skip_gain, doc_lengths):
    rows = inner_x.shape[1]
    channels = inner_x.shape[2]
    states = a_log.shape[1]
    shards = lax.axis_size("ctx")
    sections = lax.axis_size("pipe")
    group = 16
    width = group * LANES
    blocks = channels // width
    me = lax.axis_index("ctx").astype(jnp.int32)
    place = me.reshape(1)
    maps = state_maps[0].reshape(2 * states, rows)
    x, dt, gy = inner_x[0], dt_raw[0], grad_out[0]
    hist = shift_to(x[rows - 3:], "ctx", 1)

    def after(value, *earlier):
        return lax.optimization_barrier((value,) + earlier)[0]

    many = blocks // 2
    here, heads = place, []
    for first in (0, many):
        own = head_call(group, first, many, here, doc_lengths, maps, dt, gy, a_log[0])
        heads.append([shift_to(own, "ctx", -d) for d in range(1, REACH + 1)])
        here = after(place, own)

    calls = [(0, many, 0, heads[0])] + [(many + b, 1, b, heads[1]) for b in range(many)]
    carried = None
    arrived = []
    for block, count, skip, arriving in calls:
        gx, *carried = main_call(
            group, 4, shards, block, count, skip, here, doc_lengths, maps, x, hist, dt, gy,
            saved_states[0, 0], a_log[0], conv_weight[0], conv_bias, skip_gain, arriving, carried)
        arrived.append(shift_to(gx, "pipe", -1))
    gdt, mine, spill, params, grad_maps = carried
    mine, spill, params, *_ = lax.optimization_barrier((mine, spill, params, *arrived[:-1]))

    mine, spill, _ = lax.optimization_barrier((mine, spill, arrived[-1]))
    mine = shift_to(mine, "pipe", -1)
    pairs = [(s * shards + k, (s - 1) * shards + k - 1)
             for s in range(1, sections) for k in range(1, shards)]
    spilled = lax.ppermute(spill, ("pipe", "ctx"), pairs)
    sides = params.reshape((shards // 2, 2) + params.shape[1:])
    side = me % 2
    given = lax.dynamic_index_in_dim(sides, 1 - side, 1, keepdims=False)
    got = lax.ppermute(given, "ctx", [(k, k ^ 1) for k in range(shards)])
    half = lax.dynamic_index_in_dim(sides, side, 1, keepdims=False) + got
    groups = [list(range(k, shards, 2)) for k in range(2)]
    shares = lax.all_to_all(half, "ctx", 0, 0, tiled=True, axis_index_groups=groups)
    shares = jnp.sum(shares, axis=0)[:states + 6]
    upstream = join_call(arrived, mine, spilled)
    return upstream[None], gdt[None], grad_maps.reshape(1, 2, states, rows), shares[None]


def solution(mesh):
    in_specs = (
        P("pipe", "ctx", None),
        P("pipe", "ctx", None),
        P("pipe", "ctx", None),
        P("pipe", None, None, "ctx"),
        P("pipe", "ctx", None, None),
        P("pipe", None, None),
        P("pipe", None, None),
        P("pipe", None),
        P("pipe", None),
        P("pipe", None),
    )
    out_specs = (
        P("pipe", "ctx", None),
        P("pipe", "ctx", None),
        P("pipe", None, None, "ctx"),
        P("pipe", None, "ctx"),
    )
    return jax.shard_map(
        on_device, mesh=mesh, in_specs=in_specs, out_specs=out_specs, check_vma=False
    )
```

```python
import functools

import jax
import jax.numpy as jnp
from jax import lax
from jax.experimental import pallas as pl
from jax.experimental.pallas import tpu as pltpu
from jax.sharding import PartitionSpec as P

LANES = 128
LOG2E = 1.4426950408889634
LN2 = 0.6931471805599453
RESET_STEP = 1e4
PAST = 8
CHUNK = 8
WIDE = 16
MIB = 1 << 20
HEAD_VMEM = 60 * MIB
MAIN_VMEM = 60 * MIB
REACH = 3


def shift_to(x, axis, by):
    length = lax.axis_size(axis)
    pairs = [(i, i + by) for i in range(length) if 0 <= i + by < length]
    return lax.ppermute(x, axis, pairs)


def after(value, *earlier):
    return lax.optimization_barrier((value,) + earlier)[0]


def at_chunk(i, size):
    return pl.multiple_of(i * size, size)


def fill_keep(offset, len_ref, keep_t):
    rows, lanes = keep_t.shape
    place = lax.broadcasted_iota(jnp.int32, (rows, lanes), 0) + (offset - PAST)

    def mark(d, carry):
        start, keep = carry
        return start + len_ref[0, d], jnp.where(place == start, 0.0, keep)

    _, keep = lax.fori_loop(
        0, len_ref.shape[1], mark, (jnp.int32(0), jnp.ones((rows, lanes), jnp.float32)))
    keep_t[...] = keep


def fill_maps(maps_ref, maps_t):
    count, rows = maps_ref.shape
    turned = maps_ref[...].T
    for n in range(count):
        maps_t[n * rows:(n + 1) * rows, :] = jnp.broadcast_to(turned[:, n:n + 1], (rows, LANES))


def spread(ref, row, group):
    one = ref[pl.ds(row, 8, stride=0), :]
    return jnp.concatenate([one] * (group // 8), axis=0)


def gather_positions(src_ref, dst, group, first=0):
    rows = src_ref.shape[0]

    def move(i, _):
        t = at_chunk(i, WIDE)
        wide = src_ref[pl.ds(t, WIDE), :].astype(jnp.float32)
        dst[pl.ds(first + t, WIDE)] = wide.reshape(WIDE, group, LANES)
        return 0

    lax.fori_loop(0, rows // WIDE, move, 0)


def scatter_positions(src, dst_ref, group):
    rows = dst_ref.shape[0]

    def move(i, _):
        t = at_chunk(i, WIDE)
        wide = src[pl.ds(t, WIDE)].reshape(WIDE, group * LANES)
        dst_ref[pl.ds(t, WIDE), :] = wide.astype(dst_ref.dtype)
        return 0

    lax.fori_loop(0, rows // WIDE, move, 0)


def head_kernel(group, unroll, place_ref, len_ref, maps_ref, dt_ref, gy_ref, alog_ref, head_ref,
                keep_t, maps_t, step_t, gy_t, a2_s):
    rows = dt_ref.shape[0]
    states = alog_ref.shape[0]

    @pl.when(pl.program_id(0) == 0)
    def _():
        fill_keep(place_ref[0] * rows, len_ref, keep_t)
        fill_maps(maps_ref, maps_t)

    gather_positions(gy_ref, gy_t, group)
    gather_positions(dt_ref, step_t, group)
    a2_s[...] = (-LOG2E * jnp.exp(alog_ref[...])).reshape(states, group, LANES)

    def steps(i, total):
        t = at_chunk(i, CHUNK)
        step = jnp.log1p(jnp.exp(step_t[pl.ds(t, CHUNK)]))
        for k in range(CHUNK):
            one = step[k] + (1.0 - spread(keep_t, PAST + t + k, group)) * RESET_STEP
            step_t[t + k] = one
            total = total + one
        return total

    zero = jnp.zeros((group, LANES), jnp.float32)
    total = lax.fori_loop(0, rows // CHUNK, steps, zero)

    def token(i, cars):
        t = rows - 1 - i
        gy = gy_t[t]
        step = step_t[t]
        out = []
        for n in range(states):
            decay = jnp.exp2(step * a2_s[n])
            out.append(decay * (spread(maps_t, n * rows + t, group) * gy + cars[n]))
        return tuple(out)

    cars = lax.fori_loop(0, rows, token, (zero,) * states, unroll=unroll)
    for n in range(states):
        head_ref[0, n] = cars[n]
    head_ref[0, states] = total


def head_call(group, block, blocks, place, lengths, maps, dt, gy, alog):
    rows = dt.shape[0]
    states = alog.shape[0]
    width = group * LANES
    smem = pl.BlockSpec(memory_space=pltpu.SMEM)
    col = lambda i: (0, block + i)
    f32 = jnp.float32
    return pl.pallas_call(
        functools.partial(head_kernel, group, 8),
        grid=(blocks,),
        out_shape=jax.ShapeDtypeStruct((blocks, states + 1, group, LANES), f32),
        in_specs=[smem, smem, pl.BlockSpec((states, rows), lambda i: (1, 0)),
                  pl.BlockSpec((rows, width), col),
                  pl.BlockSpec((rows, width), col), pl.BlockSpec((states, width), col)],
        out_specs=pl.BlockSpec((1, states + 1, group, LANES), lambda i: (i, 0, 0, 0)),
        scratch_shapes=[
            pltpu.VMEM((rows + 3 * PAST, LANES), f32),
            pltpu.VMEM((states * rows + 8, LANES), f32),
            pltpu.VMEM((rows, group, LANES), f32),
            pltpu.VMEM((rows, group, LANES), f32),
            pltpu.VMEM((states, group, LANES), f32),
        ],
        compiler_params=pltpu.CompilerParams(
            dimension_semantics=("arbitrary",), vmem_limit_bytes=HEAD_VMEM),
        cost_estimate=pl.CostEstimate(
            flops=blocks * rows * states * width * 1000, transcendentals=0,
            bytes_accessed=blocks * width * rows * states * 4),
        name="head",
    )(place, lengths, maps, dt, gy, alog)


def main_kernel(group, part, many, place_ref, len_ref, maps_ref, x_ref, hist_ref, dt_ref, gy_ref,
                start_ref, alog_ref, cw_ref, cb_ref, sk_ref, next_ref, next2_ref, next3_ref, *rest):
    maps_before = rest[-28] if len(rest) > 27 else None
    rest = rest[-27:]
    (gx_ref, gdt_ref, mine_ref, spill_ref, gp_ref, gm_ref,
     keep_t, maps_t, x_t, sig_t, gy_t, a2_s, small_s, start_s, gin_s,
     step_t, du_t, u_t, slope_t, w_t, v_t, gc_t, h_s, accb_s, accc_s, gp_s, dec_s) = rest
    rows = x_ref.shape[0]
    states = alog_ref.shape[0]
    f32 = jnp.float32
    zero = jnp.zeros((group, LANES), f32)

    first = pl.program_id(0) == 0

    @pl.when(first)
    def _():
        fill_keep(place_ref[0] * rows, len_ref, keep_t)
        fill_maps(maps_ref, maps_t)

    gather_positions(x_ref, x_t, group, 3)
    gather_positions(gy_ref, gy_t, group, 1)
    gy_t[0:1] = jnp.zeros((1, group, LANES), f32)
    gather_positions(dt_ref, step_t, group)
    a2_s[...] = (-LOG2E * jnp.exp(alog_ref[...])).reshape(states, group, LANES)
    start_s[...] = start_ref[...].reshape(states, group, LANES)
    x_t[0:3] = hist_ref[...].astype(f32).reshape(3, group, LANES)
    small_s[0:4] = cw_ref[...].reshape(4, group, LANES)
    small_s[4:5] = cb_ref[...].reshape(1, group, LANES)
    small_s[5:6] = sk_ref[...].reshape(1, group, LANES)
    gc_t[0:3] = jnp.zeros((3, group, LANES), f32)
    gc_t[rows + 3:rows + 6] = jnp.zeros((3, group, LANES), f32)

    def keep_at(t):
        return spread(keep_t, PAST + t, group)

    def rows_of(i, _):
        t = at_chunk(i, CHUNK)
        for k in range(CHUNK):
            keep = keep_at(t + k)
            conv = keep_at(t + k - 2) * (small_s[0] * x_t[t + k])
            conv = keep_at(t + k - 1) * (small_s[1] * x_t[t + k + 1] + conv)
            conv = keep * (small_s[2] * x_t[t + k + 2] + conv)
            conv = small_s[4] + small_s[3] * x_t[t + k + 3] + conv
            sig = 1.0 / (1.0 + jnp.exp(-conv))
            u = conv * sig
            e = jnp.exp(step_t[t + k])
            step = jnp.log1p(e)
            step_t[t + k] = step + (1.0 - keep) * RESET_STEP
            du_t[t + k] = step * u
            u_t[t + k] = u
            sig_t[t + k] = e / (1.0 + e)
            slope_t[t + k] = sig * (1.0 + conv * (1.0 - sig))
            w_t[t + k] = step
        return 0

    lax.fori_loop(0, rows // CHUNK, rows_of, 0)

    for n in range(states):
        arrived = next3_ref[0, n]
        for ref in (next2_ref, next_ref):
            arrived = ref[0, n] + jnp.exp2(ref[0, states] * a2_s[n]) * arrived
        gin_s[n] = arrived

    def fold(p):
        out = p[0:8]
        for k in range(1, group // 8):
            out = out + p[k * 8:(k + 1) * 8]
        return out

    def assign(ref, n, t, value):
        ref[n, t] = value

    def add(ref, n, t, value):
        ref[n, t] += value

    def scans(put):
        for lo in range(0, states, part):
            hi = lo + part

            def forward(t, hs):
                step = step_t[t]
                du = du_t[t]
                out = []
                for n in range(lo, hi):
                    decay = jnp.exp2(step * a2_s[n])
                    h = decay * hs[n - lo] + spread(maps_t, n * rows + t, group) * du
                    h_s[t, n - lo] = hs[n - lo]
                    dec_s[t, n - lo] = decay
                    out.append(h)
                return tuple(out)

            final = lax.fori_loop(
                0, rows, forward, tuple(start_s[n] for n in range(lo, hi)), unroll=16)
            for n in range(lo, hi):
                put(accc_s, n, rows, fold(final[n - lo] * gy_t[rows]))

            def backward(i, carry):
                cars, rates = carry
                t = rows - 1 - i
                step = step_t[t]
                du = du_t[t]
                y = gy_t[t + 1]
                y_before = gy_t[t]
                new_cars, new_rates = [], []
                w = None if lo == 0 else gc_t[t + 3]
                v = None if lo == 0 else v_t[t]
                for n in range(lo, hi):
                    m = n - lo
                    g = spread(maps_t, (states + n) * rows + t, group) * y + cars[m]
                    put(accb_s, n, t, fold(g * du))
                    h = h_s[t, m]
                    put(accc_s, n, t, fold(h * y_before))
                    bg = spread(maps_t, n * rows + t, group) * g
                    w = bg if w is None else w + bg
                    car = dec_s[t, m] * g
                    aq = a2_s[n] * (car * h)
                    v = aq if v is None else v + aq
                    new_cars.append(car)
                    new_rates.append(rates[m] + step * aq)
                gc_t[t + 3] = w
                v_t[t] = v
                return tuple(new_cars), tuple(new_rates)

            _, rates = lax.fori_loop(
                0, rows, backward,
                (tuple(gin_s[n] for n in range(lo, hi)), (zero,) * part), unroll=8)
            for n in range(lo, hi):
                gp_s[n] = rates[n - lo] * LN2

    @pl.when(first)
    def _():
        scans(assign)

    if many:
        @pl.when(jnp.logical_not(first))
        def _():
            scans(add)

    def finish(i, carry):
        taps = list(carry)
        t = at_chunk(rows // CHUNK - 1 - i, CHUNK)
        for k in range(CHUNK - 1, -1, -1):
            y = gy_t[t + k + 1]
            u = u_t[t + k]
            w = gc_t[t + k + 3]
            grad_u = small_s[5] * y + w_t[t + k] * w
            v_t[t + k] = (u * w + LN2 * v_t[t + k]) * sig_t[t + k]
            gc = grad_u * slope_t[t + k]
            gc_t[t + k + 3] = gc
            x = small_s[0] * gc_t[t + k + 6] * keep_at(t + k + 3)
            x = (small_s[1] * gc_t[t + k + 5] + x) * keep_at(t + k + 2)
            x = (small_s[2] * gc_t[t + k + 4] + x) * keep_at(t + k + 1)
            w_t[t + k] = small_s[3] * gc + x
            e1 = keep_at(t + k) * gc
            e2 = keep_at(t + k - 1) * e1
            e3 = keep_at(t + k - 2) * e2
            taps[0] += e3 * x_t[t + k]
            taps[1] += e2 * x_t[t + k + 1]
            taps[2] += e1 * x_t[t + k + 2]
            taps[3] += gc * x_t[t + k + 3]
            taps[4] += y * u
            taps[5] += gc
        return tuple(taps)

    taps = lax.fori_loop(0, rows // CHUNK, finish, (zero,) * 6)
    for k in range(6):
        gp_s[states + k] = taps[k]
    for k in range(3):
        x = small_s[0] * gc_t[k + 3] * keep_at(k)
        x = (small_s[1] * gc_t[k + 2] + x) * keep_at(k - 1)
        x = (small_s[2] * gc_t[k + 1] + x) * keep_at(k - 2)
        small_s[6 + k] = x
    scatter_positions(w_t, gx_ref, group)
    scatter_positions(v_t, gdt_ref, group)
    mine_ref[...] = w_t[rows - 3:rows].reshape(3, group * LANES)
    spill_ref[...] = small_s[6:9].reshape(3, group * LANES)
    for k in range(states + 6, gp_s.shape[0]):
        gp_s[k] = zero
    wide = gp_s[...].reshape(gp_s.shape[0], group * LANES)
    share = gp_ref.shape[2]
    for k in range(gp_ref.shape[0]):
        gp_ref[k] = wide[:, k * share:(k + 1) * share]

    sub = lax.broadcasted_iota(jnp.int32, (8, LANES), 0)

    def pair_up(parts, shift):
        low = (sub & shift) == 0
        return [jnp.where(low, a, b) + pltpu.roll(jnp.where(low, b, a), shift, 0)
                for a, b in zip(parts[::2], parts[1::2])]

    def add_sublanes(ref, ahead, base):
        def add_state(n, _):
            for tb in range(rows // 8):
                parts = [ref[n, tb * 8 + k + ahead] for k in range(8)]
                for shift in (1, 2, 4):
                    parts = pair_up(parts, shift)
                maps_t[pl.ds((base + n) * rows + tb * 8, 8), :] = parts[0]
            return 0

        lax.fori_loop(0, states, add_state, 0)

    def add_lanes(n, _):
        flat = maps_t[pl.ds(at_chunk(n, rows), rows), :].T
        total = jnp.sum(flat, axis=0, keepdims=True)
        if maps_before is not None:
            total = total + maps_before[pl.ds(n, 1), :]
        gm_ref[pl.ds(n, 1), :] = total
        return 0

    @pl.when(pl.program_id(0) == pl.num_programs(0) - 1)
    def _():
        add_sublanes(accb_s, 0, 0)
        add_sublanes(accc_s, 1, states)
        lax.fori_loop(0, 2 * states, add_lanes, 0, unroll=4)


def main_call(group, part, shards, block, blocks, skip, place, lengths, maps, x, hist, dt, gy, start,
              alog, cw, cb, sk, heads, carried):
    rows, channels = x.shape
    states = alog.shape[0]
    width = group * LANES
    share = channels // shards
    params = -(-(states + 6) // 8) * 8
    smem = pl.BlockSpec(memory_space=pltpu.SMEM)
    col = lambda i: (0, block + i)
    whole = lambda i: (0, 0)
    f32 = jnp.float32
    table = pltpu.VMEM((rows, group, LANES), f32)
    vectors = pltpu.VMEM((states, group, LANES), f32)
    operands = [place, lengths, maps, x, hist, dt, gy, start, alog, cw, cb, sk, *heads]
    in_specs = [smem, smem, pl.BlockSpec((2 * states, rows), whole),
                pl.BlockSpec((rows, width), col),
                pl.BlockSpec((3, width), col),
                pl.BlockSpec((rows, width), col),
                pl.BlockSpec((rows, width), col),
                pl.BlockSpec((states, width), col),
                pl.BlockSpec((states, width), col),
                pl.BlockSpec((4, width), col),
                pl.BlockSpec((1, width), col),
                pl.BlockSpec((1, width), col)]
    in_specs += [pl.BlockSpec((1, states + 1, group, LANES), lambda i: (skip + i, 0, 0, 0))] * REACH
    aliases = {}
    if carried is not None:
        aliases = {len(operands) + k: k + 1 for k in range(len(carried))}
        operands += carried
        in_specs += [pl.BlockSpec(memory_space=pl.ANY)] * (len(carried) - 1)
        in_specs.append(pl.BlockSpec((2 * states, rows), whole))
    return pl.pallas_call(
        functools.partial(main_kernel, group, part, blocks > 1),
        grid=(blocks,),
        out_shape=(
            jax.ShapeDtypeStruct((rows, blocks * width), jnp.bfloat16),
            jax.ShapeDtypeStruct((rows, channels), jnp.bfloat16),
            jax.ShapeDtypeStruct((3, channels), f32),
            jax.ShapeDtypeStruct((3, channels), f32),
            jax.ShapeDtypeStruct((shards, params, share), f32),
            jax.ShapeDtypeStruct((2 * states, rows), f32),
        ),
        in_specs=in_specs,
        out_specs=(pl.BlockSpec((rows, width), lambda i: (0, i)),
                   pl.BlockSpec((rows, width), col),
                   pl.BlockSpec((3, width), col),
                   pl.BlockSpec((3, width), col),
                   pl.BlockSpec((width // share, params, share), lambda i: (block + i, 0, 0)),
                   pl.BlockSpec((2 * states, rows), whole)),
        scratch_shapes=[
            pltpu.VMEM((rows + 3 * PAST, LANES), f32),
            pltpu.VMEM((2 * states * rows + 8, LANES), f32),
            pltpu.VMEM((rows + 3, group, LANES), f32),
            table,
            pltpu.VMEM((rows + 1, group, LANES), f32),
            vectors,
            pltpu.VMEM((9, group, LANES), f32),
            vectors, vectors,
            table, table, table, table, table, table,
            pltpu.VMEM((rows + 6, group, LANES), f32),
            pltpu.VMEM((rows, part, group, LANES), f32),
            pltpu.VMEM((states, rows, 8, LANES), f32),
            pltpu.VMEM((states, rows + 1, 8, LANES), f32),
            pltpu.VMEM((params, group, LANES), f32),
            pltpu.VMEM((rows, part, group, LANES), f32),
        ],
        input_output_aliases=aliases,
        compiler_params=pltpu.CompilerParams(
            dimension_semantics=("arbitrary",), vmem_limit_bytes=MAIN_VMEM),
        cost_estimate=pl.CostEstimate(
            flops=blocks * rows * states * width * 5000, transcendentals=0,
            bytes_accessed=blocks * width * rows * states * 18),
        name="main",
    )(*operands)


def join_kernel(count, *refs):
    out_ref = refs[-1]
    rows = out_ref.shape[0]
    at = 0
    for ref in refs[:count]:
        out_ref[:, at:at + ref.shape[1]] = ref[...]
        at += ref.shape[1]
    tail = refs[count][...] + refs[count + 1][...]
    out_ref[rows - 3:rows, :] = tail.astype(out_ref.dtype)


def join_call(blocks, mine, spilled):
    count = len(blocks)
    rows = blocks[0].shape[0]
    return pl.pallas_call(
        functools.partial(join_kernel, count),
        out_shape=jax.ShapeDtypeStruct((rows, mine.shape[1]), blocks[0].dtype),
        compiler_params=pltpu.CompilerParams(vmem_limit_bytes=16 * MIB),
        name="join",
    )(*blocks, mine, spilled)


def on_device(inner_x, dt_raw, grad_out, state_maps, saved_states, a_log, conv_weight, conv_bias,
              skip_gain, doc_lengths):
    rows = inner_x.shape[1]
    channels = inner_x.shape[2]
    states = a_log.shape[1]
    shards = lax.axis_size("ctx")
    sections = lax.axis_size("pipe")
    group = 16
    width = group * LANES
    blocks = channels // width
    me = lax.axis_index("ctx").astype(jnp.int32)
    place = me.reshape(1)
    maps = state_maps[0].reshape(2 * states, rows)
    x, dt, gy = inner_x[0], dt_raw[0], grad_out[0]
    hist = shift_to(x[rows - 3:], "ctx", 1)

    def after(value, *earlier):
        return lax.optimization_barrier((value,) + earlier)[0]

    many = blocks // 2
    here, heads = place, []
    for first in (0, many):
        own = head_call(group, first, many, here, doc_lengths, maps, dt, gy, a_log[0])
        heads.append([shift_to(own, "ctx", -d) for d in range(1, REACH + 1)])
        here = after(place, own)

    calls = [(0, many, 0, heads[0])] + [(many + b, 1, b, heads[1]) for b in range(many)]
    carried = None
    arrived = []
    for block, count, skip, arriving in calls:
        gx, *carried = main_call(
            group, 4, shards, block, count, skip, here, doc_lengths, maps, x, hist, dt, gy,
            saved_states[0, 0], a_log[0], conv_weight[0], conv_bias, skip_gain, arriving, carried)
        arrived.append(shift_to(gx, "pipe", -1))
    gdt, mine, spill, params, grad_maps = carried
    mine, spill, params, *_ = lax.optimization_barrier((mine, spill, params, *arrived[:-1]))

    spill = after(spill, arrived[-1])
    mine = shift_to(mine, "pipe", -1)
    pairs = [(s * shards + k, (s - 1) * shards + k - 1)
             for s in range(1, sections) for k in range(1, shards)]
    spilled = lax.ppermute(spill, ("pipe", "ctx"), pairs)
    sides = params.reshape((shards // 2, 2) + params.shape[1:])
    side = me % 2
    given = lax.dynamic_index_in_dim(sides, 1 - side, 1, keepdims=False)
    got = lax.ppermute(given, "ctx", [(k, k ^ 1) for k in range(shards)])
    half = lax.dynamic_index_in_dim(sides, side, 1, keepdims=False) + got
    groups = [list(range(k, shards, 2)) for k in range(2)]
    shares = lax.all_to_all(half, "ctx", 0, 0, tiled=True, axis_index_groups=groups)
    shares = jnp.sum(shares, axis=0)[:states + 6]
    upstream = join_call(arrived, mine, spilled)
    return upstream[None], gdt[None], grad_maps.reshape(1, 2, states, rows), shares[None]


def solution(mesh):
    in_specs = (
        P("pipe", "ctx", None),
        P("pipe", "ctx", None),
        P("pipe", "ctx", None),
        P("pipe", None, None, "ctx"),
        P("pipe", "ctx", None, None),
        P("pipe", None, None),
        P("pipe", None, None),
        P("pipe", None),
        P("pipe", None),
        P("pipe", None),
    )
    out_specs = (
        P("pipe", "ctx", None),
        P("pipe", "ctx", None),
        P("pipe", None, None, "ctx"),
        P("pipe", None, "ctx"),
    )
    return jax.shard_map(
        on_device, mesh=mesh, in_specs=in_specs, out_specs=out_specs, check_vma=False
    )
```

```python
import functools

import jax
import jax.numpy as jnp
from jax import lax
from jax.experimental import pallas as pl
from jax.experimental.pallas import tpu as pltpu
from jax.sharding import PartitionSpec as P

LANES = 128
LOG2E = 1.4426950408889634
LN2 = 0.6931471805599453
RESET_STEP = 1e4
PAST = 8
CHUNK = 8
WIDE = 16
MIB = 1 << 20
HEAD_VMEM = 60 * MIB
JOIN_COST = 1 << 32
MAIN_VMEM = 60 * MIB
REACH = 3


def shift_to(x, axis, by):
    length = lax.axis_size(axis)
    pairs = [(i, i + by) for i in range(length) if 0 <= i + by < length]
    return lax.ppermute(x, axis, pairs)


def after(value, *earlier):
    return lax.optimization_barrier((value,) + earlier)[0]


def at_chunk(i, size):
    return pl.multiple_of(i * size, size)


def fill_keep(offset, len_ref, keep_t):
    rows, lanes = keep_t.shape
    place = lax.broadcasted_iota(jnp.int32, (rows, lanes), 0) + (offset - PAST)

    def mark(d, carry):
        start, keep = carry
        return start + len_ref[0, d], jnp.where(place == start, 0.0, keep)

    _, keep = lax.fori_loop(
        0, len_ref.shape[1], mark, (jnp.int32(0), jnp.ones((rows, lanes), jnp.float32)))
    keep_t[...] = keep


def fill_maps(maps_ref, maps_t):
    count, rows = maps_ref.shape
    turned = maps_ref[...].T
    for n in range(count):
        maps_t[n * rows:(n + 1) * rows, :] = jnp.broadcast_to(turned[:, n:n + 1], (rows, LANES))


def spread(ref, row, group):
    one = ref[pl.ds(row, 8, stride=0), :]
    return jnp.concatenate([one] * (group // 8), axis=0)


def gather_positions(src_ref, dst, group, first=0):
    rows = src_ref.shape[0]

    def move(i, _):
        t = at_chunk(i, WIDE)
        wide = src_ref[pl.ds(t, WIDE), :].astype(jnp.float32)
        dst[pl.ds(first + t, WIDE)] = wide.reshape(WIDE, group, LANES)
        return 0

    lax.fori_loop(0, rows // WIDE, move, 0)


def scatter_positions(src, dst_ref, group):
    rows = dst_ref.shape[0]

    def move(i, _):
        t = at_chunk(i, WIDE)
        wide = src[pl.ds(t, WIDE)].reshape(WIDE, group * LANES)
        dst_ref[pl.ds(t, WIDE), :] = wide.astype(dst_ref.dtype)
        return 0

    lax.fori_loop(0, rows // WIDE, move, 0)


def head_kernel(group, unroll, place_ref, len_ref, maps_ref, dt_ref, gy_ref, alog_ref, head_ref,
                keep_t, maps_t, step_t, gy_t, a2_s):
    rows = dt_ref.shape[0]
    states = alog_ref.shape[0]

    @pl.when(pl.program_id(0) == 0)
    def _():
        fill_keep(place_ref[0] * rows, len_ref, keep_t)
        fill_maps(maps_ref, maps_t)

    gather_positions(gy_ref, gy_t, group)
    gather_positions(dt_ref, step_t, group)
    a2_s[...] = (-LOG2E * jnp.exp(alog_ref[...])).reshape(states, group, LANES)

    def steps(i, total):
        t = at_chunk(i, CHUNK)
        step = jnp.log1p(jnp.exp(step_t[pl.ds(t, CHUNK)]))
        for k in range(CHUNK):
            one = step[k] + (1.0 - spread(keep_t, PAST + t + k, group)) * RESET_STEP
            step_t[t + k] = one
            total = total + one
        return total

    zero = jnp.zeros((group, LANES), jnp.float32)
    total = lax.fori_loop(0, rows // CHUNK, steps, zero)

    def token(i, cars):
        t = rows - 1 - i
        gy = gy_t[t]
        step = step_t[t]
        out = []
        for n in range(states):
            decay = jnp.exp2(step * a2_s[n])
            out.append(decay * (spread(maps_t, n * rows + t, group) * gy + cars[n]))
        return tuple(out)

    cars = lax.fori_loop(0, rows, token, (zero,) * states, unroll=unroll)
    for n in range(states):
        head_ref[0, n] = cars[n]
    head_ref[0, states] = total


def head_call(group, block, blocks, place, lengths, maps, dt, gy, alog):
    rows = dt.shape[0]
    states = alog.shape[0]
    width = group * LANES
    smem = pl.BlockSpec(memory_space=pltpu.SMEM)
    col = lambda i: (0, block + i)
    f32 = jnp.float32
    return pl.pallas_call(
        functools.partial(head_kernel, group, 8),
        grid=(blocks,),
        out_shape=jax.ShapeDtypeStruct((blocks, states + 1, group, LANES), f32),
        in_specs=[smem, smem, pl.BlockSpec((states, rows), lambda i: (1, 0)),
                  pl.BlockSpec((rows, width), col),
                  pl.BlockSpec((rows, width), col), pl.BlockSpec((states, width), col)],
        out_specs=pl.BlockSpec((1, states + 1, group, LANES), lambda i: (i, 0, 0, 0)),
        scratch_shapes=[
            pltpu.VMEM((rows + 3 * PAST, LANES), f32),
            pltpu.VMEM((states * rows + 8, LANES), f32),
            pltpu.VMEM((rows, group, LANES), f32),
            pltpu.VMEM((rows, group, LANES), f32),
            pltpu.VMEM((states, group, LANES), f32),
        ],
        compiler_params=pltpu.CompilerParams(
            dimension_semantics=("arbitrary",), vmem_limit_bytes=HEAD_VMEM),
        cost_estimate=pl.CostEstimate(
            flops=blocks * rows * states * width * 1000, transcendentals=0,
            bytes_accessed=blocks * width * rows * states * 4),
        name="head",
    )(place, lengths, maps, dt, gy, alog)


def main_kernel(group, part, many, place_ref, len_ref, maps_ref, x_ref, hist_ref, dt_ref, gy_ref,
                start_ref, alog_ref, cw_ref, cb_ref, sk_ref, next_ref, next2_ref, next3_ref, *rest):
    maps_before = rest[-28] if len(rest) > 27 else None
    rest = rest[-27:]
    (gx_ref, gdt_ref, mine_ref, spill_ref, gp_ref, gm_ref,
     keep_t, maps_t, x_t, sig_t, gy_t, a2_s, small_s, start_s, gin_s,
     step_t, du_t, u_t, slope_t, w_t, v_t, gc_t, h_s, accb_s, accc_s, gp_s, dec_s) = rest
    rows = x_ref.shape[0]
    states = alog_ref.shape[0]
    f32 = jnp.float32
    zero = jnp.zeros((group, LANES), f32)

    first = pl.program_id(0) == 0

    @pl.when(first)
    def _():
        fill_keep(place_ref[0] * rows, len_ref, keep_t)
        fill_maps(maps_ref, maps_t)

    gather_positions(x_ref, x_t, group, 3)
    gather_positions(gy_ref, gy_t, group, 1)
    gy_t[0:1] = jnp.zeros((1, group, LANES), f32)
    gather_positions(dt_ref, step_t, group)
    a2_s[...] = (-LOG2E * jnp.exp(alog_ref[...])).reshape(states, group, LANES)
    start_s[...] = start_ref[...].reshape(states, group, LANES)
    x_t[0:3] = hist_ref[...].astype(f32).reshape(3, group, LANES)
    small_s[0:4] = cw_ref[...].reshape(4, group, LANES)
    small_s[4:5] = cb_ref[...].reshape(1, group, LANES)
    small_s[5:6] = sk_ref[...].reshape(1, group, LANES)
    gc_t[0:3] = jnp.zeros((3, group, LANES), f32)
    gc_t[rows + 3:rows + 6] = jnp.zeros((3, group, LANES), f32)

    def keep_at(t):
        return spread(keep_t, PAST + t, group)

    def rows_of(i, _):
        t = at_chunk(i, CHUNK)
        for k in range(CHUNK):
            keep = keep_at(t + k)
            conv = keep_at(t + k - 2) * (small_s[0] * x_t[t + k])
            conv = keep_at(t + k - 1) * (small_s[1] * x_t[t + k + 1] + conv)
            conv = keep * (small_s[2] * x_t[t + k + 2] + conv)
            conv = small_s[4] + small_s[3] * x_t[t + k + 3] + conv
            sig = 1.0 / (1.0 + jnp.exp(-conv))
            u = conv * sig
            e = jnp.exp(step_t[t + k])
            step = jnp.log1p(e)
            step_t[t + k] = step + (1.0 - keep) * RESET_STEP
            du_t[t + k] = step * u
            u_t[t + k] = u
            sig_t[t + k] = e / (1.0 + e)
            slope_t[t + k] = sig * (1.0 + conv * (1.0 - sig))
            w_t[t + k] = step
        return 0

    lax.fori_loop(0, rows // CHUNK, rows_of, 0)

    for n in range(states):
        arrived = next3_ref[0, n]
        for ref in (next2_ref, next_ref):
            arrived = ref[0, n] + jnp.exp2(ref[0, states] * a2_s[n]) * arrived
        gin_s[n] = arrived

    def fold(p):
        out = p[0:8]
        for k in range(1, group // 8):
            out = out + p[k * 8:(k + 1) * 8]
        return out

    def assign(ref, n, t, value):
        ref[n, t] = value

    def add(ref, n, t, value):
        ref[n, t] += value

    def scans(put):
        for lo in range(0, states, part):
            hi = lo + part

            def forward(t, hs):
                step = step_t[t]
                du = du_t[t]
                out = []
                for n in range(lo, hi):
                    decay = jnp.exp2(step * a2_s[n])
                    h = decay * hs[n - lo] + spread(maps_t, n * rows + t, group) * du
                    h_s[t, n - lo] = hs[n - lo]
                    dec_s[t, n - lo] = decay
                    out.append(h)
                return tuple(out)

            final = lax.fori_loop(
                0, rows, forward, tuple(start_s[n] for n in range(lo, hi)), unroll=16)
            for n in range(lo, hi):
                put(accc_s, n, rows, fold(final[n - lo] * gy_t[rows]))

            def backward(i, carry):
                cars, rates = carry
                t = rows - 1 - i
                step = step_t[t]
                du = du_t[t]
                y = gy_t[t + 1]
                y_before = gy_t[t]
                new_cars, new_rates = [], []
                w = None if lo == 0 else gc_t[t + 3]
                v = None if lo == 0 else v_t[t]
                for n in range(lo, hi):
                    m = n - lo
                    g = spread(maps_t, (states + n) * rows + t, group) * y + cars[m]
                    put(accb_s, n, t, fold(g * du))
                    h = h_s[t, m]
                    put(accc_s, n, t, fold(h * y_before))
                    bg = spread(maps_t, n * rows + t, group) * g
                    w = bg if w is None else w + bg
                    car = dec_s[t, m] * g
                    aq = a2_s[n] * (car * h)
                    v = aq if v is None else v + aq
                    new_cars.append(car)
                    new_rates.append(rates[m] + step * aq)
                gc_t[t + 3] = w
                v_t[t] = v
                return tuple(new_cars), tuple(new_rates)

            _, rates = lax.fori_loop(
                0, rows, backward,
                (tuple(gin_s[n] for n in range(lo, hi)), (zero,) * part), unroll=8)
            for n in range(lo, hi):
                gp_s[n] = rates[n - lo] * LN2

    @pl.when(first)
    def _():
        scans(assign)

    if many:
        @pl.when(jnp.logical_not(first))
        def _():
            scans(add)

    def finish(i, carry):
        taps = list(carry)
        t = at_chunk(rows // CHUNK - 1 - i, CHUNK)
        for k in range(CHUNK - 1, -1, -1):
            y = gy_t[t + k + 1]
            u = u_t[t + k]
            w = gc_t[t + k + 3]
            grad_u = small_s[5] * y + w_t[t + k] * w
            v_t[t + k] = (u * w + LN2 * v_t[t + k]) * sig_t[t + k]
            gc = grad_u * slope_t[t + k]
            gc_t[t + k + 3] = gc
            x = small_s[0] * gc_t[t + k + 6] * keep_at(t + k + 3)
            x = (small_s[1] * gc_t[t + k + 5] + x) * keep_at(t + k + 2)
            x = (small_s[2] * gc_t[t + k + 4] + x) * keep_at(t + k + 1)
            w_t[t + k] = small_s[3] * gc + x
            e1 = keep_at(t + k) * gc
            e2 = keep_at(t + k - 1) * e1
            e3 = keep_at(t + k - 2) * e2
            taps[0] += e3 * x_t[t + k]
            taps[1] += e2 * x_t[t + k + 1]
            taps[2] += e1 * x_t[t + k + 2]
            taps[3] += gc * x_t[t + k + 3]
            taps[4] += y * u
            taps[5] += gc
        return tuple(taps)

    taps = lax.fori_loop(0, rows // CHUNK, finish, (zero,) * 6)
    for k in range(6):
        gp_s[states + k] = taps[k]
    for k in range(3):
        x = small_s[0] * gc_t[k + 3] * keep_at(k)
        x = (small_s[1] * gc_t[k + 2] + x) * keep_at(k - 1)
        x = (small_s[2] * gc_t[k + 1] + x) * keep_at(k - 2)
        small_s[6 + k] = x
    scatter_positions(w_t, gx_ref, group)
    scatter_positions(v_t, gdt_ref, group)
    mine_ref[...] = w_t[rows - 3:rows].reshape(3, group * LANES)
    spill_ref[...] = small_s[6:9].reshape(3, group * LANES)
    for k in range(states + 6, gp_s.shape[0]):
        gp_s[k] = zero
    wide = gp_s[...].reshape(gp_s.shape[0], group * LANES)
    share = gp_ref.shape[2]
    for k in range(gp_ref.shape[0]):
        gp_ref[k] = wide[:, k * share:(k + 1) * share]

    sub = lax.broadcasted_iota(jnp.int32, (8, LANES), 0)

    def pair_up(parts, shift):
        low = (sub & shift) == 0
        return [jnp.where(low, a, b) + pltpu.roll(jnp.where(low, b, a), shift, 0)
                for a, b in zip(parts[::2], parts[1::2])]

    def add_sublanes(ref, ahead, base):
        def add_state(n, _):
            for tb in range(rows // 8):
                parts = [ref[n, tb * 8 + k + ahead] for k in range(8)]
                for shift in (1, 2, 4):
                    parts = pair_up(parts, shift)
                maps_t[pl.ds((base + n) * rows + tb * 8, 8), :] = parts[0]
            return 0

        lax.fori_loop(0, states, add_state, 0)

    def add_lanes(n, _):
        flat = maps_t[pl.ds(at_chunk(n, rows), rows), :].T
        total = jnp.sum(flat, axis=0, keepdims=True)
        if maps_before is not None:
            total = total + maps_before[pl.ds(n, 1), :]
        gm_ref[pl.ds(n, 1), :] = total
        return 0

    @pl.when(pl.program_id(0) == pl.num_programs(0) - 1)
    def _():
        add_sublanes(accb_s, 0, 0)
        add_sublanes(accc_s, 1, states)
        lax.fori_loop(0, 2 * states, add_lanes, 0, unroll=4)


def main_call(group, part, shards, block, blocks, skip, place, lengths, maps, x, hist, dt, gy, start,
              alog, cw, cb, sk, heads, carried):
    rows, channels = x.shape
    states = alog.shape[0]
    width = group * LANES
    share = channels // shards
    params = -(-(states + 6) // 8) * 8
    smem = pl.BlockSpec(memory_space=pltpu.SMEM)
    col = lambda i: (0, block + i)
    whole = lambda i: (0, 0)
    f32 = jnp.float32
    table = pltpu.VMEM((rows, group, LANES), f32)
    vectors = pltpu.VMEM((states, group, LANES), f32)
    operands = [place, lengths, maps, x, hist, dt, gy, start, alog, cw, cb, sk, *heads]
    in_specs = [smem, smem, pl.BlockSpec((2 * states, rows), whole),
                pl.BlockSpec((rows, width), col),
                pl.BlockSpec((3, width), col),
                pl.BlockSpec((rows, width), col),
                pl.BlockSpec((rows, width), col),
                pl.BlockSpec((states, width), col),
                pl.BlockSpec((states, width), col),
                pl.BlockSpec((4, width), col),
                pl.BlockSpec((1, width), col),
                pl.BlockSpec((1, width), col)]
    in_specs += [pl.BlockSpec((1, states + 1, group, LANES), lambda i: (skip + i, 0, 0, 0))] * REACH
    aliases = {}
    if carried is not None:
        aliases = {len(operands) + k: k + 1 for k in range(len(carried))}
        operands += carried
        in_specs += [pl.BlockSpec(memory_space=pl.ANY)] * (len(carried) - 1)
        in_specs.append(pl.BlockSpec((2 * states, rows), whole))
    return pl.pallas_call(
        functools.partial(main_kernel, group, part, blocks > 1),
        grid=(blocks,),
        out_shape=(
            jax.ShapeDtypeStruct((rows, blocks * width), jnp.bfloat16),
            jax.ShapeDtypeStruct((rows, channels), jnp.bfloat16),
            jax.ShapeDtypeStruct((3, channels), f32),
            jax.ShapeDtypeStruct((3, channels), f32),
            jax.ShapeDtypeStruct((shards, params, share), f32),
            jax.ShapeDtypeStruct((2 * states, rows), f32),
        ),
        in_specs=in_specs,
        out_specs=(pl.BlockSpec((rows, width), lambda i: (0, i)),
                   pl.BlockSpec((rows, width), col),
                   pl.BlockSpec((3, width), col),
                   pl.BlockSpec((3, width), col),
                   pl.BlockSpec((width // share, params, share), lambda i: (block + i, 0, 0)),
                   pl.BlockSpec((2 * states, rows), whole)),
        scratch_shapes=[
            pltpu.VMEM((rows + 3 * PAST, LANES), f32),
            pltpu.VMEM((2 * states * rows + 8, LANES), f32),
            pltpu.VMEM((rows + 3, group, LANES), f32),
            table,
            pltpu.VMEM((rows + 1, group, LANES), f32),
            vectors,
            pltpu.VMEM((9, group, LANES), f32),
            vectors, vectors,
            table, table, table, table, table, table,
            pltpu.VMEM((rows + 6, group, LANES), f32),
            pltpu.VMEM((rows, part, group, LANES), f32),
            pltpu.VMEM((states, rows, 8, LANES), f32),
            pltpu.VMEM((states, rows + 1, 8, LANES), f32),
            pltpu.VMEM((params, group, LANES), f32),
            pltpu.VMEM((rows, part, group, LANES), f32),
        ],
        input_output_aliases=aliases,
        compiler_params=pltpu.CompilerParams(
            dimension_semantics=("arbitrary",), vmem_limit_bytes=MAIN_VMEM),
        cost_estimate=pl.CostEstimate(
            flops=blocks * rows * states * width * 5000, transcendentals=0,
            bytes_accessed=blocks * width * rows * states * 18),
        name="main",
    )(*operands)


def join_kernel(count, *refs):
    out_ref = refs[-1]
    rows = out_ref.shape[0]
    at = 0
    for ref in refs[:count]:
        out_ref[:, at:at + ref.shape[1]] = ref[...]
        at += ref.shape[1]
    tail = refs[count][...] + refs[count + 1][...]
    out_ref[rows - 3:rows, :] = tail.astype(out_ref.dtype)


def join_call(blocks, mine, spilled):
    count = len(blocks)
    rows = blocks[0].shape[0]
    return pl.pallas_call(
        functools.partial(join_kernel, count),
        out_shape=jax.ShapeDtypeStruct((rows, mine.shape[1]), blocks[0].dtype),
        compiler_params=pltpu.CompilerParams(vmem_limit_bytes=16 * MIB),
        cost_estimate=pl.CostEstimate(
            flops=JOIN_COST, transcendentals=0, bytes_accessed=JOIN_COST // 250),
        name="join",
    )(*blocks, mine, spilled)


def on_device(inner_x, dt_raw, grad_out, state_maps, saved_states, a_log, conv_weight, conv_bias,
              skip_gain, doc_lengths):
    rows = inner_x.shape[1]
    channels = inner_x.shape[2]
    states = a_log.shape[1]
    shards = lax.axis_size("ctx")
    sections = lax.axis_size("pipe")
    group = 16
    width = group * LANES
    blocks = channels // width
    me = lax.axis_index("ctx").astype(jnp.int32)
    place = me.reshape(1)
    maps = state_maps[0].reshape(2 * states, rows)
    x, dt, gy = inner_x[0], dt_raw[0], grad_out[0]
    hist = shift_to(x[rows - 3:], "ctx", 1)

    def after(value, *earlier):
        return lax.optimization_barrier((value,) + earlier)[0]

    many = blocks // 2
    here, heads = place, []
    for first in (0, many):
        own = head_call(group, first, many, here, doc_lengths, maps, dt, gy, a_log[0])
        heads.append([shift_to(own, "ctx", -d) for d in range(1, REACH + 1)])
        here = after(place, own)

    calls = [(0, many, 0, heads[0])] + [(many + b, 1, b, heads[1]) for b in range(many)]
    carried = None
    arrived = []
    for block, count, skip, arriving in calls:
        gx, *carried = main_call(
            group, 4, shards, block, count, skip, here, doc_lengths, maps, x, hist, dt, gy,
            saved_states[0, 0], a_log[0], conv_weight[0], conv_bias, skip_gain, arriving, carried)
        arrived.append(shift_to(gx, "pipe", -1))
    gdt, mine, spill, params, grad_maps = carried
    mine, spill, params, *_ = lax.optimization_barrier((mine, spill, params, *arrived[:-1]))

    mine = shift_to(mine, "pipe", -1)
    pairs = [(s * shards + k, (s - 1) * shards + k - 1)
             for s in range(1, sections) for k in range(1, shards)]
    spilled = lax.ppermute(spill, ("pipe", "ctx"), pairs)
    sides = params.reshape((shards // 2, 2) + params.shape[1:])
    side = me % 2
    given = lax.dynamic_index_in_dim(sides, 1 - side, 1, keepdims=False)
    got = lax.ppermute(given, "ctx", [(k, k ^ 1) for k in range(shards)])
    half = lax.dynamic_index_in_dim(sides, side, 1, keepdims=False) + got
    groups = [list(range(k, shards, 2)) for k in range(2)]
    shares = lax.all_to_all(half, "ctx", 0, 0, tiled=True, axis_index_groups=groups)
    shares = jnp.sum(shares, axis=0)[:states + 6]
    upstream = join_call(arrived, mine, spilled)
    return upstream[None], gdt[None], grad_maps.reshape(1, 2, states, rows), shares[None]


def solution(mesh):
    in_specs = (
        P("pipe", "ctx", None),
        P("pipe", "ctx", None),
        P("pipe", "ctx", None),
        P("pipe", None, None, "ctx"),
        P("pipe", "ctx", None, None),
        P("pipe", None, None),
        P("pipe", None, None),
        P("pipe", None),
        P("pipe", None),
        P("pipe", None),
    )
    out_specs = (
        P("pipe", "ctx", None),
        P("pipe", "ctx", None),
        P("pipe", None, None, "ctx"),
        P("pipe", None, "ctx"),
    )
    return jax.shard_map(
        on_device, mesh=mesh, in_specs=in_specs, out_specs=out_specs, check_vma=False
    )
```

```python
import functools

import jax
import jax.numpy as jnp
from jax import lax
from jax.experimental import pallas as pl
from jax.experimental.pallas import tpu as pltpu
from jax.sharding import PartitionSpec as P

LANES = 128
LOG2E = 1.4426950408889634
LN2 = 0.6931471805599453
RESET_STEP = 1e4
PAST = 8
CHUNK = 16
WIDE = 16
MIB = 1 << 20
HEAD_VMEM = 60 * MIB
JOIN_COST = 1 << 32
MAIN_VMEM = 60 * MIB
REACH = 3


def shift_to(x, axis, by):
    length = lax.axis_size(axis)
    pairs = [(i, i + by) for i in range(length) if 0 <= i + by < length]
    return lax.ppermute(x, axis, pairs)


def after(value, *earlier):
    return lax.optimization_barrier((value,) + earlier)[0]


def at_chunk(i, size):
    return pl.multiple_of(i * size, size)


def fill_keep(offset, len_ref, keep_t):
    rows, lanes = keep_t.shape
    place = lax.broadcasted_iota(jnp.int32, (rows, lanes), 0) + (offset - PAST)

    def mark(d, carry):
        start, keep = carry
        return start + len_ref[0, d], jnp.where(place == start, 0.0, keep)

    _, keep = lax.fori_loop(
        0, len_ref.shape[1], mark, (jnp.int32(0), jnp.ones((rows, lanes), jnp.float32)))
    keep_t[...] = keep


def fill_maps(maps_ref, maps_t):
    count, rows = maps_ref.shape
    turned = maps_ref[...].T
    for n in range(count):
        maps_t[n * rows:(n + 1) * rows, :] = jnp.broadcast_to(turned[:, n:n + 1], (rows, LANES))


def spread(ref, row, group):
    one = ref[pl.ds(row, 8, stride=0), :]
    return jnp.concatenate([one] * (group // 8), axis=0)


def gather_positions(src_ref, dst, group, first=0):
    rows = src_ref.shape[0]

    def move(i, _):
        t = at_chunk(i, WIDE)
        wide = src_ref[pl.ds(t, WIDE), :].astype(jnp.float32)
        dst[pl.ds(first + t, WIDE)] = wide.reshape(WIDE, group, LANES)
        return 0

    lax.fori_loop(0, rows // WIDE, move, 0)


def scatter_positions(src, dst_ref, group):
    rows = dst_ref.shape[0]

    def move(i, _):
        t = at_chunk(i, WIDE)
        wide = src[pl.ds(t, WIDE)].reshape(WIDE, group * LANES)
        dst_ref[pl.ds(t, WIDE), :] = wide.astype(dst_ref.dtype)
        return 0

    lax.fori_loop(0, rows // WIDE, move, 0)


def head_kernel(group, unroll, place_ref, len_ref, maps_ref, dt_ref, gy_ref, alog_ref, head_ref,
                keep_t, maps_t, step_t, gy_t, a2_s):
    rows = dt_ref.shape[0]
    states = alog_ref.shape[0]

    @pl.when(pl.program_id(0) == 0)
    def _():
        fill_keep(place_ref[0] * rows, len_ref, keep_t)
        fill_maps(maps_ref, maps_t)

    gather_positions(gy_ref, gy_t, group)
    gather_positions(dt_ref, step_t, group)
    a2_s[...] = (-LOG2E * jnp.exp(alog_ref[...])).reshape(states, group, LANES)

    def steps(i, total):
        t = at_chunk(i, CHUNK)
        step = jnp.log1p(jnp.exp(step_t[pl.ds(t, CHUNK)]))
        for k in range(CHUNK):
            one = step[k] + (1.0 - spread(keep_t, PAST + t + k, group)) * RESET_STEP
            step_t[t + k] = one
            total = total + one
        return total

    zero = jnp.zeros((group, LANES), jnp.float32)
    total = lax.fori_loop(0, rows // CHUNK, steps, zero)

    def token(i, cars):
        t = rows - 1 - i
        gy = gy_t[t]
        step = step_t[t]
        out = []
        for n in range(states):
            decay = jnp.exp2(step * a2_s[n])
            out.append(decay * (spread(maps_t, n * rows + t, group) * gy + cars[n]))
        return tuple(out)

    cars = lax.fori_loop(0, rows, token, (zero,) * states, unroll=unroll)
    for n in range(states):
        head_ref[0, n] = cars[n]
    head_ref[0, states] = total


def head_call(group, block, blocks, place, lengths, maps, dt, gy, alog):
    rows = dt.shape[0]
    states = alog.shape[0]
    width = group * LANES
    smem = pl.BlockSpec(memory_space=pltpu.SMEM)
    col = lambda i: (0, block + i)
    f32 = jnp.float32
    return pl.pallas_call(
        functools.partial(head_kernel, group, 8),
        grid=(blocks,),
        out_shape=jax.ShapeDtypeStruct((blocks, states + 1, group, LANES), f32),
        in_specs=[smem, smem, pl.BlockSpec((states, rows), lambda i: (1, 0)),
                  pl.BlockSpec((rows, width), col),
                  pl.BlockSpec((rows, width), col), pl.BlockSpec((states, width), col)],
        out_specs=pl.BlockSpec((1, states + 1, group, LANES), lambda i: (i, 0, 0, 0)),
        scratch_shapes=[
            pltpu.VMEM((rows + 3 * PAST, LANES), f32),
            pltpu.VMEM((states * rows + 8, LANES), f32),
            pltpu.VMEM((rows, group, LANES), f32),
            pltpu.VMEM((rows, group, LANES), f32),
            pltpu.VMEM((states, group, LANES), f32),
        ],
        compiler_params=pltpu.CompilerParams(
            dimension_semantics=("arbitrary",), vmem_limit_bytes=HEAD_VMEM),
        cost_estimate=pl.CostEstimate(
            flops=blocks * rows * states * width * 1000, transcendentals=0,
            bytes_accessed=blocks * width * rows * states * 4),
        name="head",
    )(place, lengths, maps, dt, gy, alog)


def main_kernel(group, part, many, place_ref, len_ref, maps_ref, x_ref, hist_ref, dt_ref, gy_ref,
                start_ref, alog_ref, cw_ref, cb_ref, sk_ref, next_ref, next2_ref, next3_ref, *rest):
    maps_before = rest[-28] if len(rest) > 27 else None
    rest = rest[-27:]
    (gx_ref, gdt_ref, mine_ref, spill_ref, gp_ref, gm_ref,
     keep_t, maps_t, x_t, sig_t, gy_t, a2_s, small_s, start_s, gin_s,
     step_t, du_t, u_t, slope_t, w_t, v_t, gc_t, h_s, accb_s, accc_s, gp_s, dec_s) = rest
    rows = x_ref.shape[0]
    states = alog_ref.shape[0]
    f32 = jnp.float32
    zero = jnp.zeros((group, LANES), f32)

    first = pl.program_id(0) == 0

    @pl.when(first)
    def _():
        fill_keep(place_ref[0] * rows, len_ref, keep_t)
        fill_maps(maps_ref, maps_t)

    gather_positions(x_ref, x_t, group, 3)
    gather_positions(gy_ref, gy_t, group, 1)
    gy_t[0:1] = jnp.zeros((1, group, LANES), f32)
    gather_positions(dt_ref, step_t, group)
    a2_s[...] = (-LOG2E * jnp.exp(alog_ref[...])).reshape(states, group, LANES)
    start_s[...] = start_ref[...].reshape(states, group, LANES)
    x_t[0:3] = hist_ref[...].astype(f32).reshape(3, group, LANES)
    small_s[0:4] = cw_ref[...].reshape(4, group, LANES)
    small_s[4:5] = cb_ref[...].reshape(1, group, LANES)
    small_s[5:6] = sk_ref[...].reshape(1, group, LANES)
    gc_t[0:3] = jnp.zeros((3, group, LANES), f32)
    gc_t[rows + 3:rows + 6] = jnp.zeros((3, group, LANES), f32)

    def keep_at(t):
        return spread(keep_t, PAST + t, group)

    def rows_of(i, _):
        t = at_chunk(i, CHUNK)
        for k in range(CHUNK):
            keep = keep_at(t + k)
            conv = keep_at(t + k - 2) * (small_s[0] * x_t[t + k])
            conv = keep_at(t + k - 1) * (small_s[1] * x_t[t + k + 1] + conv)
            conv = keep * (small_s[2] * x_t[t + k + 2] + conv)
            conv = small_s[4] + small_s[3] * x_t[t + k + 3] + conv
            sig = 1.0 / (1.0 + jnp.exp(-conv))
            u = conv * sig
            e = jnp.exp(step_t[t + k])
            step = jnp.log1p(e)
            step_t[t + k] = step + (1.0 - keep) * RESET_STEP
            du_t[t + k] = step * u
            u_t[t + k] = u
            sig_t[t + k] = e / (1.0 + e)
            slope_t[t + k] = sig * (1.0 + conv * (1.0 - sig))
            w_t[t + k] = step
        return 0

    lax.fori_loop(0, rows // CHUNK, rows_of, 0)

    for n in range(states):
        arrived = next3_ref[0, n]
        for ref in (next2_ref, next_ref):
            arrived = ref[0, n] + jnp.exp2(ref[0, states] * a2_s[n]) * arrived
        gin_s[n] = arrived

    def fold(p):
        out = p[0:8]
        for k in range(1, group // 8):
            out = out + p[k * 8:(k + 1) * 8]
        return out

    def assign(ref, n, t, value):
        ref[n, t] = value

    def add(ref, n, t, value):
        ref[n, t] += value

    def scans(put):
        for lo in range(0, states, part):
            hi = lo + part

            def forward(t, hs):
                step = step_t[t]
                du = du_t[t]
                out = []
                for n in range(lo, hi):
                    decay = jnp.exp2(step * a2_s[n])
                    h = decay * hs[n - lo] + spread(maps_t, n * rows + t, group) * du
                    h_s[t, n - lo] = hs[n - lo]
                    dec_s[t, n - lo] = decay
                    out.append(h)
                return tuple(out)

            final = lax.fori_loop(
                0, rows, forward, tuple(start_s[n] for n in range(lo, hi)), unroll=32)
            for n in range(lo, hi):
                put(accc_s, n, rows, fold(final[n - lo] * gy_t[rows]))

            def backward(i, carry):
                cars, rates = carry
                t = rows - 1 - i
                step = step_t[t]
                du = du_t[t]
                y = gy_t[t + 1]
                y_before = gy_t[t]
                new_cars, new_rates = [], []
                w = None if lo == 0 else gc_t[t + 3]
                v = None if lo == 0 else v_t[t]
                for n in range(lo, hi):
                    m = n - lo
                    g = spread(maps_t, (states + n) * rows + t, group) * y + cars[m]
                    put(accb_s, n, t, fold(g * du))
                    h = h_s[t, m]
                    put(accc_s, n, t, fold(h * y_before))
                    bg = spread(maps_t, n * rows + t, group) * g
                    w = bg if w is None else w + bg
                    car = dec_s[t, m] * g
                    aq = a2_s[n] * (car * h)
                    v = aq if v is None else v + aq
                    new_cars.append(car)
                    new_rates.append(rates[m] + step * aq)
                gc_t[t + 3] = w
                v_t[t] = v
                return tuple(new_cars), tuple(new_rates)

            _, rates = lax.fori_loop(
                0, rows, backward,
                (tuple(gin_s[n] for n in range(lo, hi)), (zero,) * part), unroll=8)
            for n in range(lo, hi):
                gp_s[n] = rates[n - lo] * LN2

    @pl.when(first)
    def _():
        scans(assign)

    if many:
        @pl.when(jnp.logical_not(first))
        def _():
            scans(add)

    def finish(i, carry):
        taps = list(carry)
        t = at_chunk(rows // CHUNK - 1 - i, CHUNK)
        for k in range(CHUNK - 1, -1, -1):
            y = gy_t[t + k + 1]
            u = u_t[t + k]
            w = gc_t[t + k + 3]
            grad_u = small_s[5] * y + w_t[t + k] * w
            v_t[t + k] = (u * w + LN2 * v_t[t + k]) * sig_t[t + k]
            gc = grad_u * slope_t[t + k]
            gc_t[t + k + 3] = gc
            x = small_s[0] * gc_t[t + k + 6] * keep_at(t + k + 3)
            x = (small_s[1] * gc_t[t + k + 5] + x) * keep_at(t + k + 2)
            x = (small_s[2] * gc_t[t + k + 4] + x) * keep_at(t + k + 1)
            w_t[t + k] = small_s[3] * gc + x
            e1 = keep_at(t + k) * gc
            e2 = keep_at(t + k - 1) * e1
            e3 = keep_at(t + k - 2) * e2
            taps[0] += e3 * x_t[t + k]
            taps[1] += e2 * x_t[t + k + 1]
            taps[2] += e1 * x_t[t + k + 2]
            taps[3] += gc * x_t[t + k + 3]
            taps[4] += y * u
            taps[5] += gc
        return tuple(taps)

    taps = lax.fori_loop(0, rows // CHUNK, finish, (zero,) * 6)
    for k in range(6):
        gp_s[states + k] = taps[k]
    for k in range(3):
        x = small_s[0] * gc_t[k + 3] * keep_at(k)
        x = (small_s[1] * gc_t[k + 2] + x) * keep_at(k - 1)
        x = (small_s[2] * gc_t[k + 1] + x) * keep_at(k - 2)
        small_s[6 + k] = x
    scatter_positions(w_t, gx_ref, group)
    scatter_positions(v_t, gdt_ref, group)
    mine_ref[...] = w_t[rows - 3:rows].reshape(3, group * LANES)
    spill_ref[...] = small_s[6:9].reshape(3, group * LANES)
    for k in range(states + 6, gp_s.shape[0]):
        gp_s[k] = zero
    wide = gp_s[...].reshape(gp_s.shape[0], group * LANES)
    share = gp_ref.shape[2]
    for k in range(gp_ref.shape[0]):
        gp_ref[k] = wide[:, k * share:(k + 1) * share]

    sub = lax.broadcasted_iota(jnp.int32, (8, LANES), 0)

    def pair_up(parts, shift):
        low = (sub & shift) == 0
        return [jnp.where(low, a, b) + pltpu.roll(jnp.where(low, b, a), shift, 0)
                for a, b in zip(parts[::2], parts[1::2])]

    def add_sublanes(ref, ahead, base):
        def add_state(n, _):
            for tb in range(rows // 8):
                parts = [ref[n, tb * 8 + k + ahead] for k in range(8)]
                for shift in (1, 2, 4):
                    parts = pair_up(parts, shift)
                maps_t[pl.ds((base + n) * rows + tb * 8, 8), :] = parts[0]
            return 0

        lax.fori_loop(0, states, add_state, 0, unroll=2)

    def add_lanes(n, _):
        flat = maps_t[pl.ds(at_chunk(n, rows), rows), :].T
        total = jnp.sum(flat, axis=0, keepdims=True)
        if maps_before is not None:
            total = total + maps_before[pl.ds(n, 1), :]
        gm_ref[pl.ds(n, 1), :] = total
        return 0

    @pl.when(pl.program_id(0) == pl.num_programs(0) - 1)
    def _():
        add_sublanes(accb_s, 0, 0)
        add_sublanes(accc_s, 1, states)
        lax.fori_loop(0, 2 * states, add_lanes, 0, unroll=8)


def main_call(group, part, shards, block, blocks, skip, place, lengths, maps, x, hist, dt, gy, start,
              alog, cw, cb, sk, heads, carried):
    rows, channels = x.shape
    states = alog.shape[0]
    width = group * LANES
    share = channels // shards
    params = -(-(states + 6) // 8) * 8
    smem = pl.BlockSpec(memory_space=pltpu.SMEM)
    col = lambda i: (0, block + i)
    whole = lambda i: (0, 0)
    f32 = jnp.float32
    table = pltpu.VMEM((rows, group, LANES), f32)
    vectors = pltpu.VMEM((states, group, LANES), f32)
    operands = [place, lengths, maps, x, hist, dt, gy, start, alog, cw, cb, sk, *heads]
    in_specs = [smem, smem, pl.BlockSpec((2 * states, rows), whole),
                pl.BlockSpec((rows, width), col),
                pl.BlockSpec((3, width), col),
                pl.BlockSpec((rows, width), col),
                pl.BlockSpec((rows, width), col),
                pl.BlockSpec((states, width), col),
                pl.BlockSpec((states, width), col),
                pl.BlockSpec((4, width), col),
                pl.BlockSpec((1, width), col),
                pl.BlockSpec((1, width), col)]
    in_specs += [pl.BlockSpec((1, states + 1, group, LANES), lambda i: (skip + i, 0, 0, 0))] * REACH
    aliases = {}
    if carried is not None:
        aliases = {len(operands) + k: k + 1 for k in range(len(carried))}
        operands += carried
        in_specs += [pl.BlockSpec(memory_space=pl.ANY)] * (len(carried) - 1)
        in_specs.append(pl.BlockSpec((2 * states, rows), whole))
    return pl.pallas_call(
        functools.partial(main_kernel, group, part, blocks > 1),
        grid=(blocks,),
        out_shape=(
            jax.ShapeDtypeStruct((rows, blocks * width), jnp.bfloat16),
            jax.ShapeDtypeStruct((rows, channels), jnp.bfloat16),
            jax.ShapeDtypeStruct((3, channels), f32),
            jax.ShapeDtypeStruct((3, channels), f32),
            jax.ShapeDtypeStruct((shards, params, share), f32),
            jax.ShapeDtypeStruct((2 * states, rows), f32),
        ),
        in_specs=in_specs,
        out_specs=(pl.BlockSpec((rows, width), lambda i: (0, i)),
                   pl.BlockSpec((rows, width), col),
                   pl.BlockSpec((3, width), col),
                   pl.BlockSpec((3, width), col),
                   pl.BlockSpec((width // share, params, share), lambda i: (block + i, 0, 0)),
                   pl.BlockSpec((2 * states, rows), whole)),
        scratch_shapes=[
            pltpu.VMEM((rows + 3 * PAST, LANES), f32),
            pltpu.VMEM((2 * states * rows + 8, LANES), f32),
            pltpu.VMEM((rows + 3, group, LANES), f32),
            table,
            pltpu.VMEM((rows + 1, group, LANES), f32),
            vectors,
            pltpu.VMEM((9, group, LANES), f32),
            vectors, vectors,
            table, table, table, table, table, table,
            pltpu.VMEM((rows + 6, group, LANES), f32),
            pltpu.VMEM((rows, part, group, LANES), f32),
            pltpu.VMEM((states, rows, 8, LANES), f32),
            pltpu.VMEM((states, rows + 1, 8, LANES), f32),
            pltpu.VMEM((params, group, LANES), f32),
            pltpu.VMEM((rows, part, group, LANES), f32),
        ],
        input_output_aliases=aliases,
        compiler_params=pltpu.CompilerParams(
            dimension_semantics=("arbitrary",), vmem_limit_bytes=MAIN_VMEM),
        cost_estimate=pl.CostEstimate(
            flops=blocks * rows * states * width * 5000, transcendentals=0,
            bytes_accessed=blocks * width * rows * states * 18),
        name="main",
    )(*operands)


def join_kernel(count, *refs):
    out_ref = refs[-1]
    rows = out_ref.shape[0]
    at = 0
    for ref in refs[:count]:
        out_ref[:, at:at + ref.shape[1]] = ref[...]
        at += ref.shape[1]
    tail = refs[count][...] + refs[count + 1][...]
    out_ref[rows - 3:rows, :] = tail.astype(out_ref.dtype)


def join_call(blocks, mine, spilled):
    count = len(blocks)
    rows = blocks[0].shape[0]
    return pl.pallas_call(
        functools.partial(join_kernel, count),
        out_shape=jax.ShapeDtypeStruct((rows, mine.shape[1]), blocks[0].dtype),
        compiler_params=pltpu.CompilerParams(vmem_limit_bytes=16 * MIB),
        cost_estimate=pl.CostEstimate(
            flops=JOIN_COST, transcendentals=0, bytes_accessed=JOIN_COST // 250),
        name="join",
    )(*blocks, mine, spilled)


def on_device(inner_x, dt_raw, grad_out, state_maps, saved_states, a_log, conv_weight, conv_bias,
              skip_gain, doc_lengths):
    rows = inner_x.shape[1]
    channels = inner_x.shape[2]
    states = a_log.shape[1]
    shards = lax.axis_size("ctx")
    sections = lax.axis_size("pipe")
    group = 16
    width = group * LANES
    blocks = channels // width
    me = lax.axis_index("ctx").astype(jnp.int32)
    place = me.reshape(1)
    maps = state_maps[0].reshape(2 * states, rows)
    x, dt, gy = inner_x[0], dt_raw[0], grad_out[0]
    hist = shift_to(x[rows - 3:], "ctx", 1)

    def after(value, *earlier):
        return lax.optimization_barrier((value,) + earlier)[0]

    many = blocks // 2
    here, heads = place, []
    for first in (0, many):
        own = head_call(group, first, many, here, doc_lengths, maps, dt, gy, a_log[0])
        heads.append([shift_to(own, "ctx", -d) for d in range(1, REACH + 1)])
        here = after(place, own)

    calls = [(0, many, 0, heads[0])] + [(many + b, 1, b, heads[1]) for b in range(many)]
    carried = None
    arrived = []
    for block, count, skip, arriving in calls:
        gx, *carried = main_call(
            group, 4, shards, block, count, skip, here, doc_lengths, maps, x, hist, dt, gy,
            saved_states[0, 0], a_log[0], conv_weight[0], conv_bias, skip_gain, arriving, carried)
        arrived.append(shift_to(gx, "pipe", -1))
    gdt, mine, spill, params, grad_maps = carried
    mine, spill, params, *_ = lax.optimization_barrier((mine, spill, params, *arrived[:-1]))

    mine = shift_to(mine, "pipe", -1)
    pairs = [(s * shards + k, (s - 1) * shards + k - 1)
             for s in range(1, sections) for k in range(1, shards)]
    spilled = lax.ppermute(spill, ("pipe", "ctx"), pairs)
    sides = params.reshape((shards // 2, 2) + params.shape[1:])
    side = me % 2
    given = lax.dynamic_index_in_dim(sides, 1 - side, 1, keepdims=False)
    got = lax.ppermute(given, "ctx", [(k, k ^ 1) for k in range(shards)])
    half = lax.dynamic_index_in_dim(sides, side, 1, keepdims=False) + got
    groups = [list(range(k, shards, 2)) for k in range(2)]
    shares = lax.all_to_all(half, "ctx", 0, 0, tiled=True, axis_index_groups=groups)
    shares = jnp.sum(shares, axis=0)[:states + 6]
    upstream = join_call(arrived, mine, spilled)
    return upstream[None], gdt[None], grad_maps.reshape(1, 2, states, rows), shares[None]


def solution(mesh):
    in_specs = (
        P("pipe", "ctx", None),
        P("pipe", "ctx", None),
        P("pipe", "ctx", None),
        P("pipe", None, None, "ctx"),
        P("pipe", "ctx", None, None),
        P("pipe", None, None),
        P("pipe", None, None),
        P("pipe", None),
        P("pipe", None),
        P("pipe", None),
    )
    out_specs = (
        P("pipe", "ctx", None),
        P("pipe", "ctx", None),
        P("pipe", None, None, "ctx"),
        P("pipe", None, "ctx"),
    )
    return jax.shard_map(
        on_device, mesh=mesh, in_specs=in_specs, out_specs=out_specs, check_vma=False
    )
```

```python
import functools

import jax
import jax.numpy as jnp
from jax import lax
from jax.experimental import pallas as pl
from jax.experimental.pallas import tpu as pltpu
from jax.sharding import PartitionSpec as P

LANES = 128
LOG2E = 1.4426950408889634
LN2 = 0.6931471805599453
RESET_STEP = 1e4
PAST = 8
CHUNK = 16
WIDE = 16
MIB = 1 << 20
HEAD_VMEM = 60 * MIB
JOIN_COST = 1 << 32
MAIN_VMEM = 60 * MIB
REACH = 3


def shift_to(x, axis, by):
    length = lax.axis_size(axis)
    pairs = [(i, i + by) for i in range(length) if 0 <= i + by < length]
    return lax.ppermute(x, axis, pairs)


def after(value, *earlier):
    return lax.optimization_barrier((value,) + earlier)[0]


def at_chunk(i, size):
    return pl.multiple_of(i * size, size)


def fill_keep(offset, len_ref, keep_t):
    rows, lanes = keep_t.shape
    place = lax.broadcasted_iota(jnp.int32, (rows, lanes), 0) + (offset - PAST)

    def mark(d, carry):
        start, keep = carry
        return start + len_ref[0, d], jnp.where(place == start, 0.0, keep)

    _, keep = lax.fori_loop(
        0, len_ref.shape[1], mark, (jnp.int32(0), jnp.ones((rows, lanes), jnp.float32)))
    keep_t[...] = keep


def fill_maps(maps_ref, maps_t):
    count, rows = maps_ref.shape
    turned = maps_ref[...].T
    for n in range(count):
        maps_t[n * rows:(n + 1) * rows, :] = jnp.broadcast_to(turned[:, n:n + 1], (rows, LANES))


def spread(ref, row, group):
    one = ref[pl.ds(row, 8, stride=0), :]
    return jnp.concatenate([one] * (group // 8), axis=0)


def gather_positions(src_ref, dst, group, first=0):
    rows = src_ref.shape[0]

    def move(i, _):
        t = at_chunk(i, WIDE)
        wide = src_ref[pl.ds(t, WIDE), :].astype(jnp.float32)
        dst[pl.ds(first + t, WIDE)] = wide.reshape(WIDE, group, LANES)
        return 0

    lax.fori_loop(0, rows // WIDE, move, 0, unroll=2)


def scatter_positions(src, dst_ref, group):
    rows = dst_ref.shape[0]

    def move(i, _):
        t = at_chunk(i, WIDE)
        wide = src[pl.ds(t, WIDE)].reshape(WIDE, group * LANES)
        dst_ref[pl.ds(t, WIDE), :] = wide.astype(dst_ref.dtype)
        return 0

    lax.fori_loop(0, rows // WIDE, move, 0, unroll=2)


def head_kernel(group, unroll, place_ref, len_ref, maps_ref, dt_ref, gy_ref, alog_ref, head_ref,
                keep_t, maps_t, step_t, gy_t, a2_s):
    rows = dt_ref.shape[0]
    states = alog_ref.shape[0]

    @pl.when(pl.program_id(0) == 0)
    def _():
        fill_keep(place_ref[0] * rows, len_ref, keep_t)
        fill_maps(maps_ref, maps_t)

    gather_positions(gy_ref, gy_t, group)
    gather_positions(dt_ref, step_t, group)
    a2_s[...] = (-LOG2E * jnp.exp(alog_ref[...])).reshape(states, group, LANES)

    def steps(i, total):
        t = at_chunk(i, CHUNK)
        step = jnp.log1p(jnp.exp(step_t[pl.ds(t, CHUNK)]))
        for k in range(CHUNK):
            one = step[k] + (1.0 - spread(keep_t, PAST + t + k, group)) * RESET_STEP
            step_t[t + k] = one
            total = total + one
        return total

    zero = jnp.zeros((group, LANES), jnp.float32)
    total = lax.fori_loop(0, rows // CHUNK, steps, zero)

    def token(i, cars):
        t = rows - 1 - i
        gy = gy_t[t]
        step = step_t[t]
        out = []
        for n in range(states):
            decay = jnp.exp2(step * a2_s[n])
            out.append(decay * (spread(maps_t, n * rows + t, group) * gy + cars[n]))
        return tuple(out)

    cars = lax.fori_loop(0, rows, token, (zero,) * states, unroll=unroll)
    for n in range(states):
        head_ref[0, n] = cars[n]
    head_ref[0, states] = total


def head_call(group, block, blocks, place, lengths, maps, dt, gy, alog):
    rows = dt.shape[0]
    states = alog.shape[0]
    width = group * LANES
    smem = pl.BlockSpec(memory_space=pltpu.SMEM)
    col = lambda i: (0, block + i)
    f32 = jnp.float32
    return pl.pallas_call(
        functools.partial(head_kernel, group, 8),
        grid=(blocks,),
        out_shape=jax.ShapeDtypeStruct((blocks, states + 1, group, LANES), f32),
        in_specs=[smem, smem, pl.BlockSpec((states, rows), lambda i: (1, 0)),
                  pl.BlockSpec((rows, width), col),
                  pl.BlockSpec((rows, width), col), pl.BlockSpec((states, width), col)],
        out_specs=pl.BlockSpec((1, states + 1, group, LANES), lambda i: (i, 0, 0, 0)),
        scratch_shapes=[
            pltpu.VMEM((rows + 3 * PAST, LANES), f32),
            pltpu.VMEM((states * rows + 8, LANES), f32),
            pltpu.VMEM((rows, group, LANES), f32),
            pltpu.VMEM((rows, group, LANES), f32),
            pltpu.VMEM((states, group, LANES), f32),
        ],
        compiler_params=pltpu.CompilerParams(
            dimension_semantics=("arbitrary",), vmem_limit_bytes=HEAD_VMEM),
        cost_estimate=pl.CostEstimate(
            flops=blocks * rows * states * width * 1000, transcendentals=0,
            bytes_accessed=blocks * width * rows * states * 4),
        name="head",
    )(place, lengths, maps, dt, gy, alog)


def main_kernel(group, part, many, place_ref, len_ref, maps_ref, x_ref, hist_ref, dt_ref, gy_ref,
                start_ref, alog_ref, cw_ref, cb_ref, sk_ref, next_ref, next2_ref, next3_ref, *rest):
    maps_before = rest[-28] if len(rest) > 27 else None
    rest = rest[-27:]
    (gx_ref, gdt_ref, mine_ref, spill_ref, gp_ref, gm_ref,
     keep_t, maps_t, x_t, sig_t, gy_t, a2_s, small_s, start_s, gin_s,
     step_t, du_t, u_t, slope_t, w_t, v_t, gc_t, h_s, accb_s, accc_s, gp_s, dec_s) = rest
    rows = x_ref.shape[0]
    states = alog_ref.shape[0]
    f32 = jnp.float32
    zero = jnp.zeros((group, LANES), f32)

    first = pl.program_id(0) == 0

    @pl.when(first)
    def _():
        fill_keep(place_ref[0] * rows, len_ref, keep_t)
        fill_maps(maps_ref, maps_t)

    gather_positions(x_ref, x_t, group, 3)
    gather_positions(gy_ref, gy_t, group, 1)
    gy_t[0:1] = jnp.zeros((1, group, LANES), f32)
    gather_positions(dt_ref, step_t, group)
    a2_s[...] = (-LOG2E * jnp.exp(alog_ref[...])).reshape(states, group, LANES)
    start_s[...] = start_ref[...].reshape(states, group, LANES)
    x_t[0:3] = hist_ref[...].astype(f32).reshape(3, group, LANES)
    small_s[0:4] = cw_ref[...].reshape(4, group, LANES)
    small_s[4:5] = cb_ref[...].reshape(1, group, LANES)
    small_s[5:6] = sk_ref[...].reshape(1, group, LANES)
    gc_t[0:3] = jnp.zeros((3, group, LANES), f32)
    gc_t[rows + 3:rows + 6] = jnp.zeros((3, group, LANES), f32)

    def keep_at(t):
        return spread(keep_t, PAST + t, group)

    def rows_of(i, _):
        t = at_chunk(i, CHUNK)
        for k in range(CHUNK):
            keep = keep_at(t + k)
            conv = keep_at(t + k - 2) * (small_s[0] * x_t[t + k])
            conv = keep_at(t + k - 1) * (small_s[1] * x_t[t + k + 1] + conv)
            conv = keep * (small_s[2] * x_t[t + k + 2] + conv)
            conv = small_s[4] + small_s[3] * x_t[t + k + 3] + conv
            sig = 1.0 / (1.0 + jnp.exp(-conv))
            u = conv * sig
            e = jnp.exp(step_t[t + k])
            step = jnp.log1p(e)
            step_t[t + k] = step + (1.0 - keep) * RESET_STEP
            du_t[t + k] = step * u
            u_t[t + k] = u
            sig_t[t + k] = e / (1.0 + e)
            slope_t[t + k] = sig * (1.0 + conv * (1.0 - sig))
            w_t[t + k] = step
        return 0

    lax.fori_loop(0, rows // CHUNK, rows_of, 0)

    for n in range(states):
        arrived = next3_ref[0, n]
        for ref in (next2_ref, next_ref):
            arrived = ref[0, n] + jnp.exp2(ref[0, states] * a2_s[n]) * arrived
        gin_s[n] = arrived

    def fold(p):
        out = p[0:8]
        for k in range(1, group // 8):
            out = out + p[k * 8:(k + 1) * 8]
        return out

    def assign(ref, n, t, value):
        ref[n, t] = value

    def add(ref, n, t, value):
        ref[n, t] += value

    def scans(put):
        for lo in range(0, states, part):
            hi = lo + part

            def forward(t, hs):
                step = step_t[t]
                du = du_t[t]
                out = []
                for n in range(lo, hi):
                    decay = jnp.exp2(step * a2_s[n])
                    h = decay * hs[n - lo] + spread(maps_t, n * rows + t, group) * du
                    h_s[t, n - lo] = hs[n - lo]
                    dec_s[t, n - lo] = decay
                    out.append(h)
                return tuple(out)

            final = lax.fori_loop(
                0, rows, forward, tuple(start_s[n] for n in range(lo, hi)), unroll=32)
            for n in range(lo, hi):
                put(accc_s, n, rows, fold(final[n - lo] * gy_t[rows]))

            def backward(i, carry):
                cars, rates = carry
                t = rows - 1 - i
                step = step_t[t]
                du = du_t[t]
                y = gy_t[t + 1]
                y_before = gy_t[t]
                new_cars, new_rates = [], []
                w = None if lo == 0 else gc_t[t + 3]
                v = None if lo == 0 else v_t[t]
                for n in range(lo, hi):
                    m = n - lo
                    g = spread(maps_t, (states + n) * rows + t, group) * y + cars[m]
                    put(accb_s, n, t, fold(g * du))
                    h = h_s[t, m]
                    put(accc_s, n, t, fold(h * y_before))
                    bg = spread(maps_t, n * rows + t, group) * g
                    w = bg if w is None else w + bg
                    car = dec_s[t, m] * g
                    aq = a2_s[n] * (car * h)
                    v = aq if v is None else v + aq
                    new_cars.append(car)
                    new_rates.append(rates[m] + step * aq)
                gc_t[t + 3] = w
                v_t[t] = v
                return tuple(new_cars), tuple(new_rates)

            _, rates = lax.fori_loop(
                0, rows, backward,
                (tuple(gin_s[n] for n in range(lo, hi)), (zero,) * part), unroll=8)
            for n in range(lo, hi):
                gp_s[n] = rates[n - lo] * LN2

    @pl.when(first)
    def _():
        scans(assign)

    if many:
        @pl.when(jnp.logical_not(first))
        def _():
            scans(add)

    def finish(i, carry):
        taps = list(carry)
        t = at_chunk(rows // CHUNK - 1 - i, CHUNK)
        for k in range(CHUNK - 1, -1, -1):
            y = gy_t[t + k + 1]
            u = u_t[t + k]
            w = gc_t[t + k + 3]
            grad_u = small_s[5] * y + w_t[t + k] * w
            v_t[t + k] = (u * w + LN2 * v_t[t + k]) * sig_t[t + k]
            gc = grad_u * slope_t[t + k]
            gc_t[t + k + 3] = gc
            x = small_s[0] * gc_t[t + k + 6] * keep_at(t + k + 3)
            x = (small_s[1] * gc_t[t + k + 5] + x) * keep_at(t + k + 2)
            x = (small_s[2] * gc_t[t + k + 4] + x) * keep_at(t + k + 1)
            w_t[t + k] = small_s[3] * gc + x
            e1 = keep_at(t + k) * gc
            e2 = keep_at(t + k - 1) * e1
            e3 = keep_at(t + k - 2) * e2
            taps[0] += e3 * x_t[t + k]
            taps[1] += e2 * x_t[t + k + 1]
            taps[2] += e1 * x_t[t + k + 2]
            taps[3] += gc * x_t[t + k + 3]
            taps[4] += y * u
            taps[5] += gc
        return tuple(taps)

    taps = lax.fori_loop(0, rows // CHUNK, finish, (zero,) * 6)
    for k in range(6):
        gp_s[states + k] = taps[k]
    for k in range(3):
        x = small_s[0] * gc_t[k + 3] * keep_at(k)
        x = (small_s[1] * gc_t[k + 2] + x) * keep_at(k - 1)
        x = (small_s[2] * gc_t[k + 1] + x) * keep_at(k - 2)
        small_s[6 + k] = x
    scatter_positions(w_t, gx_ref, group)
    scatter_positions(v_t, gdt_ref, group)
    mine_ref[...] = w_t[rows - 3:rows].reshape(3, group * LANES)
    spill_ref[...] = small_s[6:9].reshape(3, group * LANES)
    for k in range(states + 6, gp_s.shape[0]):
        gp_s[k] = zero
    wide = gp_s[...].reshape(gp_s.shape[0], group * LANES)
    share = gp_ref.shape[2]
    for k in range(gp_ref.shape[0]):
        gp_ref[k] = wide[:, k * share:(k + 1) * share]

    sub = lax.broadcasted_iota(jnp.int32, (8, LANES), 0)

    def pair_up(parts, shift):
        low = (sub & shift) == 0
        return [jnp.where(low, a, b) + pltpu.roll(jnp.where(low, b, a), shift, 0)
                for a, b in zip(parts[::2], parts[1::2])]

    def add_sublanes(ref, ahead, base):
        def add_state(n, _):
            for tb in range(rows // 8):
                parts = [ref[n, tb * 8 + k + ahead] for k in range(8)]
                for shift in (1, 2, 4):
                    parts = pair_up(parts, shift)
                maps_t[pl.ds((base + n) * rows + tb * 8, 8), :] = parts[0]
            return 0

        lax.fori_loop(0, states, add_state, 0, unroll=4)

    def add_lanes(n, _):
        flat = maps_t[pl.ds(at_chunk(n, rows), rows), :].T
        total = jnp.sum(flat, axis=0, keepdims=True)
        if maps_before is not None:
            total = total + maps_before[pl.ds(n, 1), :]
        gm_ref[pl.ds(n, 1), :] = total
        return 0

    @pl.when(pl.program_id(0) == pl.num_programs(0) - 1)
    def _():
        add_sublanes(accb_s, 0, 0)
        add_sublanes(accc_s, 1, states)
        lax.fori_loop(0, 2 * states, add_lanes, 0, unroll=8)


def main_call(group, part, shards, block, blocks, skip, place, lengths, maps, x, hist, dt, gy, start,
              alog, cw, cb, sk, heads, carried):
    rows, channels = x.shape
    states = alog.shape[0]
    width = group * LANES
    share = channels // shards
    params = -(-(states + 6) // 8) * 8
    smem = pl.BlockSpec(memory_space=pltpu.SMEM)
    col = lambda i: (0, block + i)
    whole = lambda i: (0, 0)
    f32 = jnp.float32
    table = pltpu.VMEM((rows, group, LANES), f32)
    vectors = pltpu.VMEM((states, group, LANES), f32)
    operands = [place, lengths, maps, x, hist, dt, gy, start, alog, cw, cb, sk, *heads]
    in_specs = [smem, smem, pl.BlockSpec((2 * states, rows), whole),
                pl.BlockSpec((rows, width), col),
                pl.BlockSpec((3, width), col),
                pl.BlockSpec((rows, width), col),
                pl.BlockSpec((rows, width), col),
                pl.BlockSpec((states, width), col),
                pl.BlockSpec((states, width), col),
                pl.BlockSpec((4, width), col),
                pl.BlockSpec((1, width), col),
                pl.BlockSpec((1, width), col)]
    in_specs += [pl.BlockSpec((1, states + 1, group, LANES), lambda i: (skip + i, 0, 0, 0))] * REACH
    aliases = {}
    if carried is not None:
        aliases = {len(operands) + k: k + 1 for k in range(len(carried))}
        operands += carried
        in_specs += [pl.BlockSpec(memory_space=pl.ANY)] * (len(carried) - 1)
        in_specs.append(pl.BlockSpec((2 * states, rows), whole))
    return pl.pallas_call(
        functools.partial(main_kernel, group, part, blocks > 1),
        grid=(blocks,),
        out_shape=(
            jax.ShapeDtypeStruct((rows, blocks * width), jnp.bfloat16),
            jax.ShapeDtypeStruct((rows, channels), jnp.bfloat16),
            jax.ShapeDtypeStruct((3, channels), f32),
            jax.ShapeDtypeStruct((3, channels), f32),
            jax.ShapeDtypeStruct((shards, params, share), f32),
            jax.ShapeDtypeStruct((2 * states, rows), f32),
        ),
        in_specs=in_specs,
        out_specs=(pl.BlockSpec((rows, width), lambda i: (0, i)),
                   pl.BlockSpec((rows, width), col),
                   pl.BlockSpec((3, width), col),
                   pl.BlockSpec((3, width), col),
                   pl.BlockSpec((width // share, params, share), lambda i: (block + i, 0, 0)),
                   pl.BlockSpec((2 * states, rows), whole)),
        scratch_shapes=[
            pltpu.VMEM((rows + 3 * PAST, LANES), f32),
            pltpu.VMEM((2 * states * rows + 8, LANES), f32),
            pltpu.VMEM((rows + 3, group, LANES), f32),
            table,
            pltpu.VMEM((rows + 1, group, LANES), f32),
            vectors,
            pltpu.VMEM((9, group, LANES), f32),
            vectors, vectors,
            table, table, table, table, table, table,
            pltpu.VMEM((rows + 6, group, LANES), f32),
            pltpu.VMEM((rows, part, group, LANES), f32),
            pltpu.VMEM((states, rows, 8, LANES), f32),
            pltpu.VMEM((states, rows + 1, 8, LANES), f32),
            pltpu.VMEM((params, group, LANES), f32),
            pltpu.VMEM((rows, part, group, LANES), f32),
        ],
        input_output_aliases=aliases,
        compiler_params=pltpu.CompilerParams(
            dimension_semantics=("arbitrary",), vmem_limit_bytes=MAIN_VMEM),
        cost_estimate=pl.CostEstimate(
            flops=blocks * rows * states * width * 5000, transcendentals=0,
            bytes_accessed=blocks * width * rows * states * 18),
        name="main",
    )(*operands)


def join_kernel(count, *refs):
    out_ref = refs[-1]
    rows = out_ref.shape[0]
    at = 0
    for ref in refs[:count]:
        out_ref[:, at:at + ref.shape[1]] = ref[...]
        at += ref.shape[1]
    tail = refs[count][...] + refs[count + 1][...]
    out_ref[rows - 3:rows, :] = tail.astype(out_ref.dtype)


def join_call(blocks, mine, spilled):
    count = len(blocks)
    rows = blocks[0].shape[0]
    return pl.pallas_call(
        functools.partial(join_kernel, count),
        out_shape=jax.ShapeDtypeStruct((rows, mine.shape[1]), blocks[0].dtype),
        compiler_params=pltpu.CompilerParams(vmem_limit_bytes=16 * MIB),
        cost_estimate=pl.CostEstimate(
            flops=JOIN_COST, transcendentals=0, bytes_accessed=JOIN_COST // 250),
        name="join",
    )(*blocks, mine, spilled)


def on_device(inner_x, dt_raw, grad_out, state_maps, saved_states, a_log, conv_weight, conv_bias,
              skip_gain, doc_lengths):
    rows = inner_x.shape[1]
    channels = inner_x.shape[2]
    states = a_log.shape[1]
    shards = lax.axis_size("ctx")
    sections = lax.axis_size("pipe")
    group = 16
    width = group * LANES
    blocks = channels // width
    me = lax.axis_index("ctx").astype(jnp.int32)
    place = me.reshape(1)
    maps = state_maps[0].reshape(2 * states, rows)
    x, dt, gy = inner_x[0], dt_raw[0], grad_out[0]
    hist = shift_to(x[rows - 3:], "ctx", 1)

    def after(value, *earlier):
        return lax.optimization_barrier((value,) + earlier)[0]

    many = blocks // 2
    here, heads = place, []
    for first in (0, many):
        own = head_call(group, first, many, here, doc_lengths, maps, dt, gy, a_log[0])
        heads.append([shift_to(own, "ctx", -d) for d in range(1, REACH + 1)])
        here = after(place, own)

    calls = [(0, many, 0, heads[0])] + [(many + b, 1, b, heads[1]) for b in range(many)]
    carried = None
    arrived = []
    for block, count, skip, arriving in calls:
        gx, *carried = main_call(
            group, 4, shards, block, count, skip, here, doc_lengths, maps, x, hist, dt, gy,
            saved_states[0, 0], a_log[0], conv_weight[0], conv_bias, skip_gain, arriving, carried)
        arrived.append(shift_to(gx, "pipe", -1))
    gdt, mine, spill, params, grad_maps = carried
    mine, spill, params, *_ = lax.optimization_barrier((mine, spill, params, *arrived[:-1]))

    mine = shift_to(mine, "pipe", -1)
    pairs = [(s * shards + k, (s - 1) * shards + k - 1)
             for s in range(1, sections) for k in range(1, shards)]
    spilled = lax.ppermute(spill, ("pipe", "ctx"), pairs)
    sides = params.reshape((shards // 2, 2) + params.shape[1:])
    side = me % 2
    given = lax.dynamic_index_in_dim(sides, 1 - side, 1, keepdims=False)
    got = lax.ppermute(given, "ctx", [(k, k ^ 1) for k in range(shards)])
    half = lax.dynamic_index_in_dim(sides, side, 1, keepdims=False) + got
    groups = [list(range(k, shards, 2)) for k in range(2)]
    shares = lax.all_to_all(half, "ctx", 0, 0, tiled=True, axis_index_groups=groups)
    shares = jnp.sum(shares, axis=0)[:states + 6]
    upstream = join_call(arrived, mine, spilled)
    return upstream[None], gdt[None], grad_maps.reshape(1, 2, states, rows), shares[None]


def solution(mesh):
    in_specs = (
        P("pipe", "ctx", None),
        P("pipe", "ctx", None),
        P("pipe", "ctx", None),
        P("pipe", None, None, "ctx"),
        P("pipe", "ctx", None, None),
        P("pipe", None, None),
        P("pipe", None, None),
        P("pipe", None),
        P("pipe", None),
        P("pipe", None),
    )
    out_specs = (
        P("pipe", "ctx", None),
        P("pipe", "ctx", None),
        P("pipe", None, None, "ctx"),
        P("pipe", None, "ctx"),
    )
    return jax.shard_map(
        on_device, mesh=mesh, in_specs=in_specs, out_specs=out_specs, check_vma=False
    )
```
